32 devices in a mesh: sec: 8 (over z, x), row: 4 (over y, core).
Axes of the slice: x: 2, y: 2, z: 4, core: 2. Of those that a mesh axis runs over, the one named last changes fastest.
Arguments:
- left_block: bfloat16 [16, 2048, 128], P('sec', 'row'), may hold values from -6 to 6
- right_block: bfloat16 [16, 128, 2048], P('sec'), may hold values from -6 to 6
- left_ops: float32 [4, 16, 16], replicated, may hold values from -1.5 to 1.5
- right_ops: float32 [4, 16, 16], replicated, may hold values from -1.5 to 1.5
- charges: int32 [16], replicated, may hold values from 0 to 6
- live_states: int32 [16], replicated, may hold values from 64 to 128
- kept: int32 [16], replicated, may hold values from 64 to 128
- start: int32 [16, 128], replicated, may hold values from 0 to 511, all different within a row
Outputs:
- basis: float32 [16, 2048, 128], P('sec', 'row')
- right_new: float32 [16, 128, 2048], P('sec', None, 'row')
The draws below stay inside these ranges and needn't reach their ends.
Inputs may be any that keep to these rules, and one draw needn't show every extreme that they name: The 128 start columns of a sector are distinct.
All inputs are finite; a program needn't handle non-finite values.
Results may differ from the reference program's by a relative error of at most 0.0065.
Values may be sent and summed in bfloat16 or wider, within the bound.
A program may use at most 64 MiB of HBM per device.

```python
import jax
import jax.numpy as jnp
from jax import lax

SITE = 16
STATES = 128
KEEP = 128
TERMS = 4
ITERS = 2
SECTORS = 16
ROWS = 2048
COLS = 2048


def set_ends(result, stream_key, least, top_value):
    place = [jax.random.randint(jax.random.fold_in(stream_key, axis), (), 0, length) for axis, length in enumerate(result.shape)]
    widest = result.shape.index(max(result.shape))
    neighbour = place[:widest] + [(place[widest] + 1) % result.shape[widest]] + place[widest + 1:]
    return result.at[tuple(place)].set(least).at[tuple(neighbour)].set(top_value)


def levels(stream_key, shape, shards, smallest, largest):
    factor_of, own = 1.0, jax.random.fold_in(stream_key, 6)
    for dim, shards_of in shards:
        draws = jnp.exp(jax.random.uniform(jax.random.fold_in(own, dim), (shards_of,), jnp.float32, smallest / len(shards), largest / len(shards)))
        factor_of = factor_of * jnp.repeat(draws, shape[dim] // shards_of).reshape([-1 if axis == dim else 1 for axis in range(len(shape))])
    return factor_of


def different_ones(stream_key, rows, count, top, lift):
    ranking = jax.random.permutation(jax.random.fold_in(stream_key, 1), count)
    favour = ranking
    for power in range(3):
        favour = favour * favour // count
    favour = favour * lift // count
    tickets = jax.random.randint(jax.random.fold_in(stream_key, 2), (rows, count), 0, 4096) + favour
    holders = jax.random.permutation(jax.random.fold_in(stream_key, 3), rows)[jnp.arange(count) % rows]
    tickets = jnp.where(jnp.arange(rows)[:, None] == holders[None, :], 1 << 14, tickets)
    score = tickets * count + jnp.arange(count)
    return lax.top_k(score.astype(jnp.int32), top)[1].astype(jnp.int32)


def noise(own_key, shape, spread, reach, shards=(), kind=jnp.bfloat16):
    factor_of = levels(own_key, shape, shards, -0.22, 0.18) if shards else 1.0
    values = jax.random.normal(own_key, shape, jnp.float32) * spread * factor_of
    return jnp.minimum(jnp.maximum(values, -reach), reach).astype(kind)


def setup_inputs(seed: int = 0) -> dict:
    keys = jax.random.split(jax.random.key(seed), 9)
    return {
        "left_block": noise(keys[0], (SECTORS, ROWS, STATES), 1.0, 6.0, ((0, 8), (1, 4))),
        "right_block": noise(keys[1], (SECTORS, STATES, COLS), 1.0, 6.0, ((0, 8),)),
        "left_ops": noise(keys[2], (TERMS, SITE, SITE), SITE ** -0.5, 1.5, (), jnp.float32),
        "right_ops": noise(keys[3], (TERMS, SITE, SITE), SITE ** -0.5, 1.5, (), jnp.float32),
        "charges": set_ends(jax.random.randint(keys[4], (SECTORS,), 0, 7), jax.random.fold_in(keys[4], 1), 0, 6).astype(jnp.int32),
        "live_states": set_ends(jax.random.randint(keys[5], (SECTORS,), STATES // 2, STATES + 1), jax.random.fold_in(keys[5], 1), STATES // 2, STATES).astype(jnp.int32),
        "kept": set_ends(jax.random.randint(keys[6], (SECTORS,), KEEP // 2, KEEP + 1), jax.random.fold_in(keys[6], 1), KEEP // 2, KEEP).astype(jnp.int32),
        "start": different_ones(keys[7], SECTORS, TERMS * STATES, KEEP, 0),
    }


chemical = 0.4
highest = lax.Precision.HIGHEST

def gate_rows(tensor_block, operators):
    site_dim = operators.shape[1]
    grouped = tensor_block.astype(jnp.float32).reshape(tensor_block.shape[0] // site_dim, site_dim, tensor_block.shape[1])
    mixed_rows = jnp.einsum('tij,ajk->aitk', operators.astype(jnp.float32), grouped, precision=highest)
    return mixed_rows.reshape(tensor_block.shape[0], operators.shape[0] * tensor_block.shape[1]).astype(jnp.bfloat16)

def gate_columns(tensor_block, operators):
    site_dim = operators.shape[1]
    grouped = tensor_block.astype(jnp.float32).reshape(tensor_block.shape[0], site_dim, tensor_block.shape[1] // site_dim)
    mixed_columns = jnp.einsum('tij,kjb->tkib', operators.astype(jnp.float32), grouped, precision=highest)
    return mixed_columns.reshape(operators.shape[0] * tensor_block.shape[0], tensor_block.shape[1]).astype(jnp.bfloat16)

def orthonormal(krylov):
    gram_matrix = jnp.dot(krylov.T, krylov, precision=highest)
    factor = jnp.linalg.cholesky(gram_matrix)
    return jax.scipy.linalg.solve_triangular(factor, krylov.T, lower=True).T

def reference(left_block, right_block, left_ops, right_ops, charges, live_states, kept, start):
    half_count = SECTORS // 2

    def one_sector(packed):
        left_tensor, right_tensor, live_count, charge_value, kept_count, columns = packed
        row_states = jnp.arange(left_tensor.shape[0], dtype=jnp.int32) // SITE
        left_masked = jnp.where((row_states < live_count)[:, None], left_tensor, jnp.zeros((), jnp.bfloat16))
        left_gated = gate_rows(left_masked, left_ops)
        right_gated = gate_columns(right_tensor, right_ops)
        weight = jnp.exp(-chemical * charge_value.astype(jnp.float32))
        theta_block = weight * jnp.dot(left_gated.astype(jnp.float32), right_gated.astype(jnp.float32), preferred_element_type=jnp.float32)
        krylov = jnp.take(left_gated, columns, axis=1).astype(jnp.float32)
        for round_index in range(ITERS):
            ortho_block = orthonormal(krylov)
            projected = jnp.dot(theta_block.T, ortho_block, precision=highest)
            krylov = jnp.dot(theta_block, projected, precision=highest)
        ortho_block = orthonormal(krylov)
        right_part = jnp.dot(ortho_block.T, theta_block, precision=highest)
        keep_mask = (jnp.arange(KEEP, dtype=jnp.int32) < kept_count).astype(jnp.float32)
        return (ortho_block * keep_mask[None, :], right_part * keep_mask[:, None])
    paired = (left_block, jnp.roll(right_block, -half_count, axis=0), live_states, jnp.roll(charges, -half_count), jnp.roll(kept, -half_count), start)
    basis_all, right_all = lax.map(one_sector, paired)
    total_weight = jnp.sum(right_all * right_all)
    right_all = right_all / jnp.sqrt(total_weight)
    return (basis_all, jnp.roll(right_all, half_count, axis=0))
```

```python
import functools

import jax
import jax.numpy as jnp
from jax import lax
from jax.experimental import pallas as pl
from jax.experimental.pallas import tpu as pltpu
from jax.sharding import PartitionSpec as P

MESH = pl.DeviceIdType.MESH
HIGHEST = lax.Precision.HIGHEST
F32, BF16 = jnp.float32, jnp.bfloat16
chemical = 0.4
ITERS = 2
PANEL = 16
CHUNKS = 2
PIECES = 2
VM = pl.BlockSpec(memory_space=pltpu.VMEM)
SM = pl.BlockSpec(memory_space=pltpu.SMEM)
ANY = pl.BlockSpec(memory_space=pl.ANY)


def nn(a, b, precision=None):
    return lax.dot_general(
        a, b, (((1,), (0,)), ((), ())), precision=precision, preferred_element_type=F32
    )


def nt(a, b, precision=None):
    return lax.dot_general(
        a, b, (((1,), (1,)), ((), ())), precision=precision, preferred_element_type=F32
    )


def tn(a, b, precision=None):
    return lax.dot_general(
        a, b, (((0,), (0,)), ((), ())), precision=precision, preferred_element_type=F32
    )


def split2(x):
    high = x.astype(BF16)
    return high, (x - high.astype(F32)).astype(BF16)


def split3(x):
    high, rest = x.astype(BF16), None
    rest = x - high.astype(F32)
    mid = rest.astype(BF16)
    return high, mid, (rest - mid.astype(F32)).astype(BF16)


def presplit_nn(parts, x):
    high, low = split2(x)
    both = nn(parts[0], jnp.concatenate([high, low], axis=1))
    width = x.shape[1]
    return both[:, :width] + both[:, width:] + nn(parts[1], high)


def nt3(a, b):
    ah, al = split2(a)
    bh, bl = split2(b)
    return nt(jnp.concatenate([ah, al, ah], axis=1), jnp.concatenate([bh, bh, bl], axis=1))


def iota(shape, dim):
    return lax.broadcasted_iota(jnp.int32, shape, dim)


def spread(ops, row_of, col_of, same):
    site = ops.shape[0]
    pick_rows = (iota((row_of.shape[0], site), 1) == row_of).astype(BF16)
    pick_cols = (iota((site, col_of.shape[1]), 0) == col_of).astype(BF16)
    out = []
    for part in split2(ops):
        wide = nn(nn(pick_rows, part).astype(BF16), pick_cols)
        out.append(jnp.where(same, wide, 0.0).astype(BF16))
    return out


def inverse_factor(gram, s_ref, t_ref):
    size = gram.shape[0]
    s_ref[...] = gram
    t_ref[...] = (iota((size, size), 0) == iota((size, size), 1)).astype(F32)
    sub = iota((PANEL, size), 0)
    lane = iota((PANEL, size), 1)

    def panel(p, carry):
        base = pl.multiple_of(p * PANEL, PANEL)
        upper = s_ref[pl.ds(base, PANEL), :]
        lower = t_ref[pl.ds(base, PANEL), :]
        turned = pltpu.roll(upper, lax.rem(size - base, size), 1)
        cols = [jnp.broadcast_to(turned[:, c : c + 1], (PANEL, size)) for c in range(PANEL)]
        for j in range(PANEL):
            scale = lax.rsqrt(cols[j][j : j + 1, :])
            below = jnp.where(sub > j, cols[j] * scale, 0.0)
            at_j = sub == j

            def eliminate(x):
                pivot = x[j : j + 1, :] * scale
                return jnp.where(at_j, pivot, x - below * pivot)

            upper, lower = eliminate(upper), eliminate(lower)
            cols = [eliminate(c) if i > j else c for i, c in enumerate(cols)]
        t_ref[pl.ds(base, PANEL), :] = lower
        u3, l3 = split3(upper), split3(lower)
        later = lane >= base + PANEL
        m3 = [jnp.where(later, x.astype(F32), 0.0).astype(BF16) for x in u3]
        pairs = ((0, 0), (0, 1), (1, 0), (1, 1), (0, 2), (2, 0))
        lhs = jnp.concatenate([m3[i] for i, _ in pairs], axis=0)
        rhs = jnp.concatenate([jnp.concatenate([u3[k], l3[k]], axis=1) for _, k in pairs], axis=0)
        change = tn(lhs, rhs)
        s_ref[...] = s_ref[...] - change[:, :size]
        t_ref[...] = t_ref[...] - change[:, size:]
        return carry

    lax.fori_loop(0, size // PANEL, panel, 0)


def halvings(count):
    out, step = [], count // 2
    while step:
        out.append(step)
        step //= 2
    return out


def gate_kernel(
    row_count, sec_count, left_hbm, right_hbm, lops_ref, rops_ref, charges_ref, live_ref, kept_ref,
    start_ref, u_out, w_out, lown, lrecv, rown, rpart, kl_ref, kr_ref, at_ref, own_ref, b_ref, bw_ref,
    ga_ref, gah_ref, gal_ref, gbh_ref, gbl_ref, s_ref, t_ref, csend, crecv, msend, mrecv, total_ref,
    local, lsend, lget, fsend, fget, csems, cgets, msems, mgets, tsems, tgets,
):
    slots, rows, states = left_hbm.shape
    terms, site = lops_ref.shape[0], lops_ref.shape[1]
    cols = right_hbm.shape[2]
    width = cols // site
    group = 256 // site
    block = group * site
    bond = terms * states
    keep = start_ref.shape[1]
    sector_count = slots * sec_count
    mates = row_count // slots
    here = site // row_count
    piece = rows // PIECES
    half = sec_count // 2

    sec, row = lax.axis_index("sec"), lax.axis_index("row")
    slot, mate = row // mates, row % mates
    partner = jnp.bitwise_xor(sec, half)
    home = sec * slots + slot
    mirror = lax.rem(home + sector_count // 2, sector_count)

    def slot_row(t):
        return t * mates + mate

    def other_slot(d):
        return lax.rem(slot + d, slots)

    def other_mate(d):
        return lax.rem(mate + d, mates)

    neighbours = [d for d in halvings(sec_count) if d != half]
    greeted = [(partner, slot_row(t)) for t in range(slots)]
    greeted += [(sec, slot_row(other_slot(d))) for d in range(1, slots)]
    greeted += [(sec, slot * mates + other_mate(d)) for d in range(1, mates)]
    greeted += [(jnp.bitwise_xor(sec, d), row) for d in neighbours]
    barrier = pltpu.get_barrier_semaphore()
    for device in greeted:
        pl.semaphore_signal(barrier, inc=1, device_id=device, device_id_type=MESH)

    near = [pltpu.make_async_copy(right_hbm.at[slot], rown, local.at[0])]
    near.append(pltpu.make_async_copy(left_hbm, lown, local.at[1]))
    for copy in near:
        copy.start()

    r0, c0 = iota((block, 1), 0), iota((1, block), 1)
    for t in range(terms):
        parts = spread(rops_ref[t], r0 // group, c0 // group, (r0 % group) == (c0 % group))
        for h in range(2):
            kr_ref[h, t * block : (t + 1) * block, :] = parts[h]

    pl.semaphore_wait(barrier, len(greeted))

    def remote(source, target, send, recv, device):
        return pltpu.make_async_remote_copy(
            src_ref=source, dst_ref=target, send_sem=send, recv_sem=recv,
            device_id=device, device_id_type=MESH,
        )

    def rows_at(owner, k):
        return pl.ds(pl.multiple_of(owner * rows + k * piece, piece), piece)

    sent = []
    for k in range(PIECES):
        for t in range(slots):
            copy = remote(
                left_hbm.at[t, pl.ds(k * piece, piece), :], lrecv.at[rows_at(row, k), :],
                lsend.at[t, k], lget.at[slot, k], (partner, slot_row(t)),
            )
            copy.start()
            sent.append(copy)

    for t in range(terms):
        parts = spread(lops_ref[t].T, r0 % site, c0 % site, (r0 // site) == (c0 // site))
        for h in range(2):
            kl_ref[h, :, t * block : (t + 1) * block] = parts[h]
    for copy in near:
        copy.wait()

    def right_chunk(c, carry):
        base = pl.multiple_of(c * group, group)
        part = rown[pl.ds(base, group), :]
        stack = jnp.concatenate([part[:, j * width : (j + 1) * width] for j in range(site)], axis=0)
        out = (nn(kr_ref[0], stack) + nn(kr_ref[1], stack)).astype(BF16)
        for t in range(terms):
            for i in range(site):
                b_ref[pl.ds(t * states + base, group), i * width : (i + 1) * width] = out[
                    t * block + i * group : t * block + (i + 1) * group, :
                ]
        return carry

    lax.fori_loop(0, states // group, right_chunk, 0)
    gbh_ref[...], gbl_ref[...] = split2(nt(b_ref[...], b_ref[...]))

    def gate_left(part, first, limit, store):
        part = jnp.where(iota((block, states), 0) + first < limit, part.astype(F32), 0.0)
        turned = part.T.astype(BF16)
        out = nn(turned, kl_ref[0]) + nn(turned, kl_ref[1])
        for t in range(terms):
            store(t, out[:, t * block : (t + 1) * block].astype(BF16))

    limit = live_ref[mirror] * site
    forwarded = []
    for k in range(PIECES):
        arrived = []
        for t in range(slots):
            owner = slot_row(t)
            place = lrecv.at[rows_at(owner, k), :]
            remote(place, place, lsend.at[t, k], lget.at[t, k], (partner, owner)).wait_recv()
            for d in range(1, mates):
                copy = remote(
                    place, place, fsend.at[d - 1, t, k], fget.at[d - 1, t, k],
                    (sec, slot * mates + other_mate(d)),
                )
                copy.start()
                forwarded.append(copy)
            arrived.append((owner, None))
        for d in range(1, mates):
            for t in range(slots):
                owner = t * mates + other_mate(mates - d)
                place = lrecv.at[rows_at(owner, k), :]
                arrived.append((owner, remote(
                    place, place, fsend.at[d - 1, t, k], fget.at[d - 1, t, k],
                    (sec, slot * mates + other_mate(mates - d)),
                )))
        for index, (owner, copy) in enumerate(arrived):
            if copy is not None:
                copy.wait_recv()
            for q in range(piece // block):
                column = ((k * row_count + index) * (piece // block) + q) * block

                def store(t, value):
                    at_ref[t * states : (t + 1) * states, column : column + block] = value

                first = owner * rows + k * piece + q * block
                gate_left(lrecv[pl.ds(pl.multiple_of(first, block), block), :], first, limit, store)
        span = row_count * piece
        gram = nt(at_ref[:, k * span : (k + 1) * span], at_ref[:, k * span : (k + 1) * span])
        ga_ref[...] = gram if k == 0 else ga_ref[...] + gram
    gah_ref[...], gal_ref[...] = split2(ga_ref[...])
    for copy in sent + forwarded:
        copy.wait_send()

    weight = jnp.exp(jnp.full((1, states), charges_ref[home], jnp.int32).astype(F32) * (-chemical))
    coef = (iota((bond, keep), 0) == start_ref[pl.ds(mirror, 1), :]).astype(F32)
    for round_index in range(ITERS + 1):
        if round_index < ITERS:
            image = presplit_nn((gah_ref[...], gal_ref[...]), coef)
        else:
            image = nn(ga_ref[...], coef, HIGHEST)
        inverse_factor(tn(coef, image, HIGHEST), s_ref, t_ref)
        image = nt3(image, t_ref[...])
        if round_index < ITERS:
            coef = presplit_nn((gbh_ref[...], gbl_ref[...]), image) * (weight * weight)
        else:
            coef = nt3(coef, t_ref[...])
    kept_here = iota((bond, keep), 1) < kept_ref[home]
    csend[...] = jnp.where(kept_here, coef, 0.0).astype(BF16)
    out = jnp.where(kept_here, image * weight, 0.0)
    msend[...] = out.astype(BF16)
    per = out * presplit_nn((gbh_ref[...], gbl_ref[...]), out)
    total_ref[0] = jnp.sum(per.reshape(bond // 8, 8, keep), axis=0)

    part = bond // mates

    def coef_at(t, m):
        return crecv.at[t, pl.ds(pl.multiple_of(m * part, part), part), :]

    flying = []

    def go(*args):
        copy = remote(*args)
        copy.start()
        flying.append(copy)

    go(
        csend.at[pl.ds(pl.multiple_of(mate * part, part), part), :], coef_at(slot, mate),
        csems.at[0], cgets.at[0], (partner, row),
    )
    for d in range(1, slots):
        go(msend, mrecv.at[slot], msems.at[d - 1], mgets.at[d - 1], (sec, slot_row(other_slot(d))))
    for d in range(1, slots):
        go(total_ref.at[0], total_ref.at[d], tsems.at[d - 1], tgets.at[d - 1], (sec, slot_row(other_slot(d))))

    def own_chunk(c, carry):
        t = c // (rows // block)
        q = lax.rem(c, rows // block)
        first = pl.multiple_of(q * block, block)

        def store(term, value):
            own_ref[t, term * states : (term + 1) * states, pl.ds(first, block)] = value

        owner = lax.rem(sec * slots + t, sector_count)
        gate_left(
            lown[t, pl.ds(first, block), :], row * rows + first, live_ref[owner] * site, store
        )
        return carry

    lax.fori_loop(0, slots * (rows // block), own_chunk, 0)

    part_rows = here * group
    part_cols = cols // row_count
    for d in range(slots):
        t = other_slot(d)
        if d == 0:
            bw_ref[t] = b_ref[:, pl.ds(pl.multiple_of(row * part_cols, part_cols), part_cols)]
            continue
        again = pltpu.make_async_copy(right_hbm.at[t], rown, local.at[0])
        again.start()
        again.wait()

        def part_chunk(c, carry):
            base = pl.multiple_of(c * group, group)
            piece_rows = rown[pl.ds(base, group), :]
            stack = jnp.concatenate(
                [piece_rows[:, j * width : (j + 1) * width] for j in range(site)], axis=0
            )
            pick = [
                jnp.concatenate([
                    kr_ref[h, pl.ds(pl.multiple_of(term * block + row * part_rows, part_rows), part_rows), :]
                    for term in range(terms)
                ], axis=0)
                for h in range(2)
            ]
            out = (nn(pick[0], stack) + nn(pick[1], stack)).astype(BF16)
            for term in range(terms):
                for i in range(here):
                    bw_ref[t, pl.ds(term * states + base, group), i * width : (i + 1) * width] = out[
                        term * part_rows + i * group : term * part_rows + (i + 1) * group, :
                    ]
            return carry

        lax.fori_loop(0, states // group, part_chunk, 0)

    summed = total_ref[0]
    for d in range(1, slots):
        flying_at = remote(
            total_ref.at[0], total_ref.at[d], tsems.at[d - 1], tgets.at[d - 1], (sec, slot_row(other_slot(d)))
        )
        flying_at.wait_recv()
        summed = summed + total_ref[d]
    index = slots
    for number, d in enumerate(halvings(sec_count)):
        total_ref[index] = summed
        copy = remote(
            total_ref.at[index], total_ref.at[index + 1], tsems.at[slots - 1 + number],
            tgets.at[slots - 1 + number], (jnp.bitwise_xor(sec, d), row),
        )
        copy.start()
        copy.wait()
        summed = summed + total_ref[index + 1]
        index += 2
    scale = 1.0 / jnp.sqrt(jnp.sum(summed, keepdims=True))

    flying[0].wait_recv()
    for d in range(1, slots):
        go(
            coef_at(slot, mate), coef_at(slot, mate), csems.at[d], cgets.at[d],
            (sec, slot_row(other_slot(d))),
        )
    number = slots
    for d in range(1, mates):
        go(
            coef_at(slot, mate), coef_at(slot, mate), csems.at[number], cgets.at[number],
            (sec, slot * mates + other_mate(d)),
        )
        number += 1
    for e in range(1, slots):
        t = other_slot(slots - e)
        remote(
            coef_at(t, mate), coef_at(t, mate), csems.at[e], cgets.at[e], (sec, slot_row(t))
        ).wait_recv()
        for d in range(1, mates):
            go(
                coef_at(t, mate), coef_at(t, mate), csems.at[number], cgets.at[number],
                (sec, slot * mates + other_mate(d)),
            )
            number += 1

    for d in range(1, slots):
        t = other_slot(slots - d)
        remote(
            msend, mrecv.at[t], msems.at[d - 1], mgets.at[d - 1], (sec, slot_row(t))
        ).wait_recv()
        w_out[t] = tn(mrecv[t], bw_ref[t]) * scale
    w_out[slot] = tn(msend[...], bw_ref[slot]) * scale

    number = slots
    for d in range(1, mates):
        remote(
            coef_at(slot, mate), coef_at(slot, other_mate(mates - d)), csems.at[number],
            cgets.at[number], (sec, slot * mates + other_mate(mates - d)),
        ).wait_recv()
        number += 1
    for e in range(1, slots):
        t = other_slot(slots - e)
        for d in range(1, mates):
            remote(
                coef_at(t, mate), coef_at(t, other_mate(mates - d)), csems.at[number],
                cgets.at[number], (sec, slot * mates + other_mate(mates - d)),
            ).wait_recv()
            number += 1
    for t in range(slots):
        u_out[t] = tn(own_ref[t], crecv[t])
    for copy in flying:
        copy.wait_send()


def solution(mesh):
    row_count, sec_count = mesh.shape["row"], mesh.shape["sec"]

    def on_device(left_block, right_block, left_ops, right_ops, charges, live_states, kept, start):
        slots, rows, states = left_block.shape
        terms, site = left_ops.shape[0], left_ops.shape[1]
        cols, bond, keep = right_block.shape[2], terms * states, start.shape[1]
        block, mates = 256, row_count // slots
        part_cols = cols // row_count
        steps = len(halvings(sec_count))
        coef_copies = slots + slots * (mates - 1)
        dma = pltpu.SemaphoreType.DMA
        return pl.pallas_call(
            functools.partial(gate_kernel, row_count, sec_count),
            out_shape=(
                jax.ShapeDtypeStruct((slots, rows, keep), F32),
                jax.ShapeDtypeStruct((slots, keep, part_cols), F32),
            ),
            in_specs=[ANY] * 2 + [VM] * 2 + [SM] * 3 + [VM],
            out_specs=[VM] * 2,
            scratch_shapes=[
                pltpu.VMEM((slots, rows, states), BF16),
                pltpu.VMEM((rows * row_count, states), BF16),
                pltpu.VMEM((states, cols), BF16),
                pltpu.VMEM((8, 128), BF16),
                pltpu.VMEM((2, block, terms * block), BF16),
                pltpu.VMEM((2, terms * block, block), BF16),
                pltpu.VMEM((bond, rows * row_count), BF16),
                pltpu.VMEM((slots, bond, rows), BF16),
                pltpu.VMEM((bond, cols), BF16),
                pltpu.VMEM((slots, bond, part_cols), BF16),
                pltpu.VMEM((bond, bond), F32),
                pltpu.VMEM((bond, bond), BF16),
                pltpu.VMEM((bond, bond), BF16),
                pltpu.VMEM((bond, bond), BF16),
                pltpu.VMEM((bond, bond), BF16),
                pltpu.VMEM((keep, keep), F32),
                pltpu.VMEM((keep, keep), F32),
                pltpu.VMEM((bond, keep), BF16),
                pltpu.VMEM((slots, bond, keep), BF16),
                pltpu.VMEM((bond, keep), BF16),
                pltpu.VMEM((slots, bond, keep), BF16),
                pltpu.VMEM((slots + 2 * steps, 8, keep), F32),
                dma((2,)),
                dma((slots, PIECES)), dma((slots, PIECES)),
                dma((mates - 1, slots, PIECES)), dma((mates - 1, slots, PIECES)),
                dma((coef_copies,)), dma((coef_copies,)),
                dma((slots - 1,)), dma((slots - 1,)),
                dma((slots - 1 + steps,)), dma((slots - 1 + steps,)),
            ],
            compiler_params=pltpu.CompilerParams(
                collective_id=0, has_side_effects=True, vmem_limit_bytes=56 * 2**20
            ),
        )(left_block, right_block, left_ops, right_ops, charges, live_states, kept, start)

    return jax.shard_map(
        on_device,
        mesh=mesh,
        in_specs=(P("sec", "row", None), P("sec", None, None), P(), P(), P(), P(), P(), P()),
        out_specs=(P("sec", "row", None), P("sec", None, "row")),
        check_vma=False,
    )
```

```python
import functools

import jax
import jax.numpy as jnp
from jax import lax
from jax.experimental import pallas as pl
from jax.experimental.pallas import tpu as pltpu
from jax.sharding import PartitionSpec as P

MESH = pl.DeviceIdType.MESH
HIGHEST = lax.Precision.HIGHEST
F32, BF16 = jnp.float32, jnp.bfloat16
chemical = 0.4
ITERS = 2
PANEL = 16
CHUNKS = 2
PIECES = 2
VM = pl.BlockSpec(memory_space=pltpu.VMEM)
SM = pl.BlockSpec(memory_space=pltpu.SMEM)
ANY = pl.BlockSpec(memory_space=pl.ANY)


def nn(a, b, precision=None):
    return lax.dot_general(
        a, b, (((1,), (0,)), ((), ())), precision=precision, preferred_element_type=F32
    )


def nt(a, b, precision=None):
    return lax.dot_general(
        a, b, (((1,), (1,)), ((), ())), precision=precision, preferred_element_type=F32
    )


def tn(a, b, precision=None):
    return lax.dot_general(
        a, b, (((0,), (0,)), ((), ())), precision=precision, preferred_element_type=F32
    )


def split2(x):
    high = x.astype(BF16)
    return high, (x - high.astype(F32)).astype(BF16)


def split3(x):
    high, rest = x.astype(BF16), None
    rest = x - high.astype(F32)
    mid = rest.astype(BF16)
    return high, mid, (rest - mid.astype(F32)).astype(BF16)


def presplit_nn(parts, x):
    high, low = split2(x)
    both = nn(parts[0], jnp.concatenate([high, low], axis=1))
    width = x.shape[1]
    return both[:, :width] + both[:, width:] + nn(parts[1], high)


def nt3(a, b):
    ah, al = split2(a)
    bh, bl = split2(b)
    return nt(jnp.concatenate([ah, al, ah], axis=1), jnp.concatenate([bh, bh, bl], axis=1))


def iota(shape, dim):
    return lax.broadcasted_iota(jnp.int32, shape, dim)


def spread(ops, row_of, col_of, same):
    site = ops.shape[0]
    pick_rows = (iota((row_of.shape[0], site), 1) == row_of).astype(BF16)
    pick_cols = (iota((site, col_of.shape[1]), 0) == col_of).astype(BF16)
    out = []
    for part in split2(ops):
        wide = nn(nn(pick_rows, part).astype(BF16), pick_cols)
        out.append(jnp.where(same, wide, 0.0).astype(BF16))
    return out


def inverse_factor(gram, s_ref, t_ref):
    size = gram.shape[0]
    s_ref[...] = gram
    t_ref[...] = (iota((size, size), 0) == iota((size, size), 1)).astype(F32)
    sub = iota((PANEL, size), 0)
    lane = iota((PANEL, size), 1)

    def panel(p, carry):
        base = pl.multiple_of(p * PANEL, PANEL)
        upper = s_ref[pl.ds(base, PANEL), :]
        lower = t_ref[pl.ds(base, PANEL), :]
        turned = pltpu.roll(upper, lax.rem(size - base, size), 1)
        cols = [jnp.broadcast_to(turned[:, c : c + 1], (PANEL, size)) for c in range(PANEL)]
        for j in range(PANEL):
            scale = lax.rsqrt(cols[j][j : j + 1, :])
            below = jnp.where(sub > j, cols[j] * scale, 0.0)
            at_j = sub == j

            def eliminate(x):
                pivot = x[j : j + 1, :] * scale
                return jnp.where(at_j, pivot, x - below * pivot)

            upper, lower = eliminate(upper), eliminate(lower)
            cols = [eliminate(c) if i > j else c for i, c in enumerate(cols)]
        t_ref[pl.ds(base, PANEL), :] = lower
        u3, l3 = split3(upper), split3(lower)
        later = lane >= base + PANEL
        m3 = [jnp.where(later, x.astype(F32), 0.0).astype(BF16) for x in u3]
        pairs = ((0, 0), (0, 1), (1, 0), (1, 1), (0, 2), (2, 0))
        lhs = jnp.concatenate([m3[i] for i, _ in pairs], axis=0)
        rhs = jnp.concatenate([jnp.concatenate([u3[k], l3[k]], axis=1) for _, k in pairs], axis=0)
        change = tn(lhs, rhs)
        s_ref[...] = s_ref[...] - change[:, :size]
        t_ref[...] = t_ref[...] - change[:, size:]
        return carry

    lax.fori_loop(0, size // PANEL, panel, 0)


def gate_kernel(
    row_count, sec_count, left_hbm, right_hbm, lops_hbm, rops_hbm, charges_hbm, live_hbm, kept_hbm,
    start_hbm, u_hbm, w_hbm, lops_ref, rops_ref, charges_ref, live_ref, kept_ref, start_ref, u_out, w_out,
    lown, lrecv, rown, kl_ref, kr_ref, at_ref, own_ref, b_ref, bw_ref, ga_ref, gah_ref, gal_ref,
    gbh_ref, gbl_ref, s_ref, t_ref, csend, crecv, msend, mrecv, total_ref,
    local, lsend, lget, fsend, fget, csems, cgets, msems, mgets, tsems, tgets,
):
    slots, rows, states = left_hbm.shape
    terms, site = lops_ref.shape[0], lops_ref.shape[1]
    cols = right_hbm.shape[2]
    width = cols // site
    group = 256 // site
    block = group * site
    bond = terms * states
    keep = start_ref.shape[1]
    sector_count = slots * sec_count
    mates = row_count // slots
    here = site // row_count
    piece = rows // PIECES
    half = sec_count // 2

    sec, row = lax.axis_index("sec"), lax.axis_index("row")
    slot, mate = row // mates, row % mates
    partner = jnp.bitwise_xor(sec, half)
    home = sec * slots + slot
    mirror = lax.rem(home + sector_count // 2, sector_count)

    def slot_row(t):
        return t * mates + mate

    def other_slot(d):
        return lax.rem(slot + d, slots)

    def other_mate(d):
        return lax.rem(mate + d, mates)

    greeted = [(sec, slot * mates + other_mate(d)) for d in range(1, mates)]
    greeted += [
        (jnp.bitwise_xor(sec, d), slot_row(other_slot(e)))
        for d in range(sec_count) for e in range(slots) if d or e
    ]
    barrier = pltpu.get_barrier_semaphore()
    for device in greeted:
        pl.semaphore_signal(barrier, inc=1, device_id=device, device_id_type=MESH)

    near = [
        pltpu.make_async_copy(source, target, local.at[i])
        for i, (source, target) in enumerate((
            (rops_hbm, rops_ref), (lops_hbm, lops_ref), (charges_hbm, charges_ref), (live_hbm, live_ref),
            (kept_hbm, kept_ref), (start_hbm, start_ref), (left_hbm, lown),
        ))
    ]
    near += [
        pltpu.make_async_copy(right_hbm.at[other_slot(e)], rown.at[e], local.at[len(near) + e])
        for e in range(slots)
    ]
    for copy in near:
        copy.start()
    near[0].wait()

    r0, c0 = iota((block, 1), 0), iota((1, block), 1)
    for t in range(terms):
        parts = spread(rops_ref[t], r0 // group, c0 // group, (r0 % group) == (c0 % group))
        for h in range(2):
            kr_ref[h, t * block : (t + 1) * block, :] = parts[h]

    pl.semaphore_wait(barrier, len(greeted))

    def remote(source, target, send, recv, device):
        return pltpu.make_async_remote_copy(
            src_ref=source, dst_ref=target, send_sem=send, recv_sem=recv,
            device_id=device, device_id_type=MESH,
        )

    def rows_at(owner, k):
        return pl.ds(pl.multiple_of(owner * rows + k * piece, piece), piece)

    sent = []
    for k in range(PIECES):
        for t in range(slots):
            copy = remote(
                left_hbm.at[t, pl.ds(k * piece, piece), :], lrecv.at[rows_at(row, k), :],
                lsend.at[t, k], lget.at[slot, k], (partner, slot_row(t)),
            )
            copy.start()
            sent.append(copy)

    for copy in near[1:]:
        copy.wait()
    for t in range(terms):
        parts = spread(lops_ref[t].T, r0 % site, c0 % site, (r0 // site) == (c0 // site))
        for h in range(2):
            kl_ref[h, :, t * block : (t + 1) * block] = parts[h]

    def right_chunk(c, carry):
        base = pl.multiple_of(c * group, group)
        part = rown[0, pl.ds(base, group), :]
        stack = jnp.concatenate([part[:, j * width : (j + 1) * width] for j in range(site)], axis=0)
        out = (nn(kr_ref[0], stack) + nn(kr_ref[1], stack)).astype(BF16)
        for t in range(terms):
            for i in range(site):
                b_ref[pl.ds(t * states + base, group), i * width : (i + 1) * width] = out[
                    t * block + i * group : t * block + (i + 1) * group, :
                ]
        return carry

    lax.fori_loop(0, states // group, right_chunk, 0)
    gbh_ref[...], gbl_ref[...] = split2(nt(b_ref[...], b_ref[...]))

    def gate_left(part, first, limit, store):
        part = jnp.where(iota((block, states), 0) + first < limit, part.astype(F32), 0.0)
        turned = part.T.astype(BF16)
        out = nn(turned, kl_ref[0]) + nn(turned, kl_ref[1])
        for t in range(terms):
            store(t, out[:, t * block : (t + 1) * block].astype(BF16))

    limit = live_ref[mirror] * site
    forwarded = []
    for k in range(PIECES):
        arrived = []
        for t in range(slots):
            owner = slot_row(t)
            place = lrecv.at[rows_at(owner, k), :]
            remote(place, place, lsend.at[t, k], lget.at[t, k], (partner, owner)).wait_recv()
            for d in range(1, mates):
                copy = remote(
                    place, place, fsend.at[d - 1, t, k], fget.at[d - 1, t, k],
                    (sec, slot * mates + other_mate(d)),
                )
                copy.start()
                forwarded.append(copy)
            arrived.append((owner, None))
        for d in range(1, mates):
            for t in range(slots):
                owner = t * mates + other_mate(mates - d)
                place = lrecv.at[rows_at(owner, k), :]
                arrived.append((owner, remote(
                    place, place, fsend.at[d - 1, t, k], fget.at[d - 1, t, k],
                    (sec, slot * mates + other_mate(mates - d)),
                )))
        for index, (owner, copy) in enumerate(arrived):
            if copy is not None:
                copy.wait_recv()
            for q in range(piece // block):
                column = ((k * row_count + index) * (piece // block) + q) * block

                def store(t, value):
                    at_ref[t * states : (t + 1) * states, column : column + block] = value

                first = owner * rows + k * piece + q * block
                gate_left(lrecv[pl.ds(pl.multiple_of(first, block), block), :], first, limit, store)
        span = row_count * piece
        gram = nt(at_ref[:, k * span : (k + 1) * span], at_ref[:, k * span : (k + 1) * span])
        ga_ref[...] = gram if k == 0 else ga_ref[...] + gram
    gah_ref[...], gal_ref[...] = split2(ga_ref[...])
    for copy in sent + forwarded:
        copy.wait_send()

    weight = jnp.exp(jnp.full((1, states), charges_ref[home], jnp.int32).astype(F32) * (-chemical))
    coef = (iota((bond, keep), 0) == start_ref[pl.ds(mirror, 1), :]).astype(F32)
    for round_index in range(ITERS + 1):
        if round_index < ITERS:
            image = presplit_nn((gah_ref[...], gal_ref[...]), coef)
        else:
            image = nn(ga_ref[...], coef, HIGHEST)
        inverse_factor(tn(coef, image, HIGHEST), s_ref, t_ref)
        if round_index < ITERS:
            image = nt3(image, t_ref[...])
            coef = presplit_nn((gbh_ref[...], gbl_ref[...]), image) * (weight * weight)
    kept_here = iota((bond, keep), 1) < kept_ref[home]
    csend[...] = jnp.where(kept_here, nt3(coef, t_ref[...]), 0.0).astype(BF16)
    out = jnp.where(kept_here, nt3(image, t_ref[...]) * weight, 0.0)
    msend[...] = out.astype(BF16)

    part = bond // mates
    bit = part // PIECES

    def coef_rows(m, k):
        return pl.ds(pl.multiple_of(m * part + k * bit, bit), bit)

    def coef_at(t, m, k):
        return crecv.at[t, coef_rows(m, k), :]

    flying = []

    def go(*args):
        copy = remote(*args)
        copy.start()
        flying.append(copy)

    for k in range(PIECES):
        go(
            csend.at[coef_rows(mate, k), :], coef_at(slot, mate, k), csems.at[0, k], cgets.at[0, k],
            (partner, row),
        )
    per = out * presplit_nn((gbh_ref[...], gbl_ref[...]), out)
    for d in range(1, slots):
        go(msend, mrecv.at[slot], msems.at[d - 1], mgets.at[d - 1], (sec, slot_row(other_slot(d))))
    total_ref[0] = jnp.sum(per, axis=0, keepdims=True)
    for d in range(sec_count):
        for e in range(slots):
            if d or e:
                index = d * slots + e
                go(
                    total_ref.at[0], total_ref.at[index], tsems.at[index], tgets.at[index],
                    (jnp.bitwise_xor(sec, d), slot_row(other_slot(e))),
                )

    def own_chunk(c, carry):
        t = c // (rows // block)
        q = lax.rem(c, rows // block)
        first = pl.multiple_of(q * block, block)

        def store(term, value):
            own_ref[t, term * states : (term + 1) * states, pl.ds(first, block)] = value

        owner = sec * slots + t
        gate_left(
            lown[t, pl.ds(first, block), :], row * rows + first, live_ref[owner] * site, store
        )
        return carry

    lax.fori_loop(0, slots * (rows // block), own_chunk, 0)

    part_rows = here * group
    part_cols = cols // row_count
    bw_ref[0] = b_ref[:, pl.ds(pl.multiple_of(row * part_cols, part_cols), part_cols)]

    def part_chunk(c, carry):
        e = 1 + c // (states // group)
        base = pl.multiple_of(lax.rem(c, states // group) * group, group)
        piece_rows = rown[e, pl.ds(base, group), :]
        stack = jnp.concatenate([piece_rows[:, j * width : (j + 1) * width] for j in range(site)], axis=0)
        pick = [
            jnp.concatenate([
                kr_ref[h, pl.ds(pl.multiple_of(term * block + row * part_rows, part_rows), part_rows), :]
                for term in range(terms)
            ], axis=0)
            for h in range(2)
        ]
        out = (nn(pick[0], stack) + nn(pick[1], stack)).astype(BF16)
        for term in range(terms):
            for i in range(here):
                bw_ref[e, pl.ds(term * states + base, group), i * width : (i + 1) * width] = out[
                    term * part_rows + i * group : term * part_rows + (i + 1) * group, :
                ]
        return carry

    lax.fori_loop(0, (slots - 1) * (states // group), part_chunk, 0)

    def pass_on(t, m, k, index):
        for d in range(1, mates):
            go(
                coef_at(t, m, k), coef_at(t, m, k), csems.at[index + d - 1, k], cgets.at[index + d - 1, k],
                (sec, slot * mates + other_mate(d)),
            )

    for k in range(PIECES):
        flying[k].wait_recv()
        for e in range(1, slots):
            go(
                coef_at(slot, mate, k), coef_at(slot, mate, k), csems.at[e, k], cgets.at[e, k],
                (sec, slot_row(other_slot(e))),
            )
        pass_on(slot, mate, k, slots)
    for k in range(PIECES):
        for e in range(1, slots):
            t = other_slot(slots - e)
            remote(
                coef_at(t, mate, k), coef_at(t, mate, k), csems.at[e, k], cgets.at[e, k], (sec, slot_row(t))
            ).wait_recv()
            pass_on(t, mate, k, slots + e * (mates - 1))

    wide = [tn(msend[...], bw_ref[0])]
    for d in range(1, slots):
        t = other_slot(slots - d)
        remote(
            msend, mrecv.at[t], msems.at[d - 1], mgets.at[d - 1], (sec, slot_row(t))
        ).wait_recv()
        wide.append(tn(mrecv[t], bw_ref[slots - d]))
    summed = total_ref[0]
    for d in range(sec_count):
        for e in range(slots):
            if d or e:
                index = d * slots + e
                remote(
                    total_ref.at[0], total_ref.at[index], tsems.at[index], tgets.at[index],
                    (jnp.bitwise_xor(sec, d), slot_row(other_slot(slots - e))),
                ).wait_recv()
                summed = summed + total_ref[index]
    scale = 1.0 / jnp.sqrt(jnp.sum(summed, keepdims=True))
    leaving = []

    def leave(source, target):
        copy = pltpu.make_async_copy(source, target, local.at[len(leaving)])
        copy.start()
        leaving.append(copy)

    for d in range(slots):
        t = other_slot(slots - d)
        w_out[d] = wide[d] * scale
        leave(w_out.at[d], w_hbm.at[t])

    for e in range(slots):
        t = other_slot(slots - e)
        for k in range(PIECES):
            for d in range(1, mates):
                index = slots + e * (mates - 1) + d - 1
                m = other_mate(mates - d)
                remote(
                    coef_at(t, m, k), coef_at(t, m, k), csems.at[index, k], cgets.at[index, k],
                    (sec, slot * mates + m),
                ).wait_recv()
        u_out[e] = tn(own_ref[t], crecv[t])
        leave(u_out.at[e], u_hbm.at[t])
    for copy in flying:
        copy.wait_send()
    for copy in leaving:
        copy.wait()


def solution(mesh):
    row_count, sec_count = mesh.shape["row"], mesh.shape["sec"]

    def on_device(left_block, right_block, left_ops, right_ops, charges, live_states, kept, start):
        slots, rows, states = left_block.shape
        terms, site = left_ops.shape[0], left_ops.shape[1]
        cols, bond, keep = right_block.shape[2], terms * states, start.shape[1]
        block, mates = 256, row_count // slots
        part_cols = cols // row_count
        coef_copies = slots + slots * (mates - 1)
        peers = slots * sec_count
        dma = pltpu.SemaphoreType.DMA
        return pl.pallas_call(
            functools.partial(gate_kernel, row_count, sec_count),
            out_shape=(
                jax.ShapeDtypeStruct((slots, rows, keep), F32),
                jax.ShapeDtypeStruct((slots, keep, part_cols), F32),
            ),
            in_specs=[ANY] * 8,
            out_specs=[ANY] * 2,
            scratch_shapes=[
                pltpu.VMEM(left_ops.shape, F32),
                pltpu.VMEM(right_ops.shape, F32),
                pltpu.SMEM(charges.shape, jnp.int32),
                pltpu.SMEM(live_states.shape, jnp.int32),
                pltpu.SMEM(kept.shape, jnp.int32),
                pltpu.VMEM(start.shape, jnp.int32),
                pltpu.VMEM((slots, rows, keep), F32),
                pltpu.VMEM((slots, keep, part_cols), F32),
                pltpu.VMEM((slots, rows, states), BF16),
                pltpu.VMEM((rows * row_count, states), BF16),
                pltpu.VMEM((slots, states, cols), BF16),
                pltpu.VMEM((2, block, terms * block), BF16),
                pltpu.VMEM((2, terms * block, block), BF16),
                pltpu.VMEM((bond, rows * row_count), BF16),
                pltpu.VMEM((slots, bond, rows), BF16),
                pltpu.VMEM((bond, cols), BF16),
                pltpu.VMEM((slots, bond, part_cols), BF16),
                pltpu.VMEM((bond, bond), F32),
                pltpu.VMEM((bond, bond), BF16),
                pltpu.VMEM((bond, bond), BF16),
                pltpu.VMEM((bond, bond), BF16),
                pltpu.VMEM((bond, bond), BF16),
                pltpu.VMEM((keep, keep), F32),
                pltpu.VMEM((keep, keep), F32),
                pltpu.VMEM((bond, keep), BF16),
                pltpu.VMEM((slots, bond, keep), BF16),
                pltpu.VMEM((bond, keep), BF16),
                pltpu.VMEM((slots, bond, keep), BF16),
                pltpu.VMEM((peers, 1, keep), F32),
                dma((7 + slots,)),
                dma((slots, PIECES)), dma((slots, PIECES)),
                dma((mates - 1, slots, PIECES)), dma((mates - 1, slots, PIECES)),
                dma((coef_copies, PIECES)), dma((coef_copies, PIECES)),
                dma((slots - 1,)), dma((slots - 1,)),
                dma((peers,)), dma((peers,)),
            ],
            compiler_params=pltpu.CompilerParams(
                collective_id=0, has_side_effects=True, vmem_limit_bytes=56 * 2**20
            ),
        )(left_block, right_block, left_ops, right_ops, charges, live_states, kept, start)

    return jax.shard_map(
        on_device,
        mesh=mesh,
        in_specs=(P("sec", "row", None), P("sec", None, None), P(), P(), P(), P(), P(), P()),
        out_specs=(P("sec", "row", None), P("sec", None, "row")),
        check_vma=False,
    )
```

```python
import functools

import jax
import jax.numpy as jnp
from jax import lax
from jax.experimental import pallas as pl
from jax.experimental.pallas import tpu as pltpu
from jax.sharding import PartitionSpec as P

MESH = pl.DeviceIdType.MESH
HIGHEST = lax.Precision.HIGHEST
F32, BF16 = jnp.float32, jnp.bfloat16
chemical = 0.4
ITERS = 2
PANEL = 32
TILE = 8
PIECES = 4
BITS = 2
VM = pl.BlockSpec(memory_space=pltpu.VMEM)
SM = pl.BlockSpec(memory_space=pltpu.SMEM)
ANY = pl.BlockSpec(memory_space=pl.ANY)


def nn(a, b, precision=None):
    return lax.dot_general(
        a, b, (((1,), (0,)), ((), ())), precision=precision, preferred_element_type=F32
    )


def nt(a, b, precision=None):
    return lax.dot_general(
        a, b, (((1,), (1,)), ((), ())), precision=precision, preferred_element_type=F32
    )


def tn(a, b, precision=None):
    return lax.dot_general(
        a, b, (((0,), (0,)), ((), ())), precision=precision, preferred_element_type=F32
    )


def split2(x):
    high = x.astype(BF16)
    return high, (x - high.astype(F32)).astype(BF16)


def split3(x):
    high, rest = x.astype(BF16), None
    rest = x - high.astype(F32)
    mid = rest.astype(BF16)
    return high, mid, (rest - mid.astype(F32)).astype(BF16)


def presplit_nn(parts, x):
    high, low = split2(x)
    both = nn(parts[0], jnp.concatenate([high, low], axis=1))
    width = x.shape[1]
    return both[:, :width] + both[:, width:] + nn(parts[1], high)


def nt3(a, b):
    ah, al = split2(a)
    bh, bl = split2(b)
    return nt(jnp.concatenate([ah, al, ah], axis=1), jnp.concatenate([bh, bh, bl], axis=1))


def tn3(a, b):
    ah, al = split2(a)
    bh, bl = split2(b)
    return tn(jnp.concatenate([ah, al, ah], axis=0), jnp.concatenate([bh, bh, bl], axis=0))


def iota(shape, dim):
    return lax.broadcasted_iota(jnp.int32, shape, dim)


def spread(ops, row_of, col_of, same):
    site = ops.shape[0]
    pick_rows = (iota((row_of.shape[0], site), 1) == row_of).astype(BF16)
    pick_cols = (iota((site, col_of.shape[1]), 0) == col_of).astype(BF16)
    out = []
    for part in split2(ops):
        wide = nn(nn(pick_rows, part).astype(BF16), pick_cols)
        out.append(jnp.where(same, wide, 0.0).astype(BF16))
    return out


def eliminate_panel(x, base):
    size = x.shape[1]
    tiles = PANEL // TILE
    sub, lane = iota((TILE, size), 0), iota((TILE, size), 1)
    inside = (lane >= base) & (lane < base + PANEL)
    cols = [
        {
            h: jnp.broadcast_to(x[h * TILE : (h + 1) * TILE, base + c : base + c + 1], (TILE, size))
            for h in range(c // TILE, tiles)
        }
        for c in range(PANEL)
    ]
    rows = [
        jnp.where(inside, (lane - (base + h * TILE) == sub).astype(F32), x[h * TILE : (h + 1) * TILE])
        for h in range(tiles)
    ]
    for j in range(0, PANEL, 2):
        own, q = j // TILE, j % TILE
        first, second = cols[j], cols[j + 1]
        a, b, d = first[own][q : q + 1], first[own][q + 1 : q + 2], second[own][q + 1 : q + 2]
        root = lax.rsqrt(a * d - b * b)
        inverse = root * root
        aa, bb, dd = a * inverse, b * inverse, d * inverse
        w1 = {h: first[h] * dd - second[h] * bb for h in range(own, tiles)}
        w2 = {h: second[h] * aa - first[h] * bb for h in range(own, tiles)}
        for i in range(j + 2, PANEL):
            at, r = i // TILE, i % TILE
            s1, s2 = first[at][r : r + 1], second[at][r : r + 1]
            cols[i] = {h: cols[i][h] - w1[h] * s1 - w2[h] * s2 for h in range(at, tiles)}
        scale = lax.rsqrt(a)
        x1, x2 = rows[own][q : q + 1], rows[own][q + 1 : q + 2]
        for h in range(own + 1, tiles):
            rows[h] = rows[h] - w1[h] * x1 - w2[h] * x2
        later = rows[own]
        if q + 2 < TILE:
            later = later - jnp.where(sub > q + 1, w1[own], 0.0) * x1 - jnp.where(sub > q + 1, w2[own], 0.0) * x2
        top = x1 * scale
        bottom = (x2 - x1 * (b * scale * scale)) * (a * scale * root)
        rows[own] = jnp.where(sub == q, top, jnp.where(sub == q + 1, bottom, later))
    return jnp.concatenate(rows, axis=0)


def inverse_factor(gram, s_ref, t_ref):
    size = gram.shape[0]
    s_ref[...] = gram
    lane = iota((PANEL, size), 1)
    for base in range(0, size, PANEL):
        after = base + PANEL
        x = eliminate_panel(s_ref[base:after, :], base)
        t_ref[base:after, :] = jnp.where(lane < after, x, 0.0)
        if after == size:
            break
        parts = split3(x)
        masked = [jnp.where(lane >= after, y.astype(F32), 0.0).astype(BF16) for y in parts]
        pairs = ((0, 0), (0, 1), (1, 0), (1, 1), (0, 2), (2, 0))
        change = tn(
            jnp.concatenate([masked[i] for i, _ in pairs], axis=0),
            jnp.concatenate([parts[k] for _, k in pairs], axis=0),
        )
        inside = (lane[0:1] >= base) & (lane[0:1] < after)
        s_ref[after:, :] = jnp.where(inside, 0.0, s_ref[after:, :]) - change[after:, :]


def gate_kernel(
    row_count, sec_count, left_hbm, right_hbm, lops_hbm, rops_hbm, charges_hbm, live_hbm, kept_hbm,
    start_hbm, u_hbm, w_hbm, lops_ref, rops_ref, charges_ref, live_ref, kept_ref, start_ref, u_out, w_out,
    lown, lrecv, rown, kl_ref, kr_ref, at_ref, own_ref, b_ref, bw_ref, ga_ref, gah_ref, gal_ref,
    gbh_ref, gbl_ref, s_ref, t_ref, csend, crecv, msend, mrecv, total_ref,
    local, lsend, lget, fsend, fget, csems, cgets, msems, mgets, tsems, tgets,
):
    slots, rows, states = left_hbm.shape
    terms, site = lops_ref.shape[0], lops_ref.shape[1]
    cols = right_hbm.shape[2]
    width = cols // site
    group = 256 // site
    block = group * site
    bond = terms * states
    keep = start_ref.shape[1]
    sector_count = slots * sec_count
    mates = row_count // slots
    here = site // row_count
    piece = rows // PIECES
    half = sec_count // 2

    sec, row = lax.axis_index("sec"), lax.axis_index("row")
    slot, mate = row // mates, row % mates
    partner = jnp.bitwise_xor(sec, half)
    home = sec * slots + slot
    mirror = lax.rem(home + sector_count // 2, sector_count)

    def slot_row(t):
        return t * mates + mate

    def other_slot(d):
        return lax.rem(slot + d, slots)

    def other_mate(d):
        return lax.rem(mate + d, mates)

    greeted = [(sec, slot * mates + other_mate(d)) for d in range(1, mates)]
    greeted += [
        (jnp.bitwise_xor(sec, d), slot_row(other_slot(e)))
        for d in range(sec_count) for e in range(slots) if d or e
    ]
    barrier = pltpu.get_barrier_semaphore()
    for device in greeted:
        pl.semaphore_signal(barrier, inc=1, device_id=device, device_id_type=MESH)

    near = [
        pltpu.make_async_copy(source, target, local.at[i])
        for i, (source, target) in enumerate((
            (rops_hbm, rops_ref), (lops_hbm, lops_ref), (charges_hbm, charges_ref), (live_hbm, live_ref),
            (kept_hbm, kept_ref), (start_hbm, start_ref), (left_hbm, lown),
        ))
    ]
    near += [
        pltpu.make_async_copy(right_hbm.at[other_slot(e)], rown.at[e], local.at[len(near) + e])
        for e in range(slots)
    ]
    for copy in near:
        copy.start()
    near[0].wait()

    r0, c0 = iota((block, 1), 0), iota((1, block), 1)
    for t in range(terms):
        parts = spread(rops_ref[t], r0 // group, c0 // group, (r0 % group) == (c0 % group))
        for h in range(2):
            kr_ref[h, t * block : (t + 1) * block, :] = parts[h]

    pl.semaphore_wait(barrier, len(greeted))

    def remote(source, target, send, recv, device):
        return pltpu.make_async_remote_copy(
            src_ref=source, dst_ref=target, send_sem=send, recv_sem=recv,
            device_id=device, device_id_type=MESH,
        )

    def rows_at(owner, k):
        return pl.ds(pl.multiple_of(owner * rows + k * piece, piece), piece)

    sent = []
    for k in range(PIECES):
        for t in range(slots):
            copy = remote(
                left_hbm.at[t, pl.ds(k * piece, piece), :], lrecv.at[rows_at(row, k), :],
                lsend.at[t, k], lget.at[slot, k], (partner, slot_row(t)),
            )
            copy.start()
            sent.append(copy)

    for copy in near[1:]:
        copy.wait()
    for t in range(terms):
        parts = spread(lops_ref[t].T, r0 % site, c0 % site, (r0 // site) == (c0 // site))
        for h in range(2):
            kl_ref[h, :, t * block : (t + 1) * block] = parts[h]

    def right_chunk(c, carry):
        base = pl.multiple_of(c * group, group)
        part = rown[0, pl.ds(base, group), :]
        stack = jnp.concatenate([part[:, j * width : (j + 1) * width] for j in range(site)], axis=0)
        out = (nn(kr_ref[0], stack) + nn(kr_ref[1], stack)).astype(BF16)
        for t in range(terms):
            for i in range(site):
                b_ref[pl.ds(t * states + base, group), i * width : (i + 1) * width] = out[
                    t * block + i * group : t * block + (i + 1) * group, :
                ]
        return carry

    lax.fori_loop(0, states // group, right_chunk, 0)
    gbh_ref[...], gbl_ref[...] = split2(nt(b_ref[...], b_ref[...]))

    def gate_left(parts, firsts, limit, store):
        parts = [
            jnp.where(iota(part.shape, 0) + first < limit, part.astype(F32), 0.0)
            for part, first in zip(parts, firsts)
        ]
        turned = jnp.concatenate(parts, axis=0).T.astype(BF16)
        out = nn(turned, kl_ref[0]) + nn(turned, kl_ref[1])
        for t in range(terms):
            store(t, out[:, t * block : (t + 1) * block].astype(BF16))

    def own_chunk(c, carry):
        t = c // (rows // block)
        q = lax.rem(c, rows // block)
        first = pl.multiple_of(q * block, block)

        def store(term, value):
            own_ref[t, term * states : (term + 1) * states, pl.ds(first, block)] = value

        owner = sec * slots + t
        gate_left(
            [lown[t, pl.ds(first, block), :]], [row * rows + first], live_ref[owner] * site, store
        )
        return carry

    lax.fori_loop(0, slots * (rows // block), own_chunk, 0)

    limit = live_ref[mirror] * site
    forwarded = []
    ready = block // piece
    span = row_count * piece
    def arrive(k):
        owners = []
        for t in range(slots):
            owner = slot_row(t)
            place = lrecv.at[rows_at(owner, k), :]
            remote(place, place, lsend.at[t, k], lget.at[t, k], (partner, owner)).wait_recv()
            for d in range(1, mates):
                copy = remote(
                    place, place, fsend.at[d - 1, t, k], fget.at[d - 1, t, k],
                    (sec, slot * mates + other_mate(d)),
                )
                copy.start()
                forwarded.append(copy)
            owners.append(owner)
        return owners

    def arrive_from_mates(k):
        owners = []
        for d in range(1, mates):
            for t in range(slots):
                owner = t * mates + other_mate(mates - d)
                place = lrecv.at[rows_at(owner, k), :]
                remote(
                    place, place, fsend.at[d - 1, t, k], fget.at[d - 1, t, k],
                    (sec, slot * mates + other_mate(mates - d)),
                ).wait_recv()
                owners.append(owner)
        return owners

    def gate_pieces(owners, k, column):
        for index in range(0, len(owners), ready):
            firsts = [owner * rows + k * piece for owner in owners[index : index + ready]]
            place = column + index * piece

            def store(t, value):
                at_ref[t * states : (t + 1) * states, place : place + block] = value

            gate_left(
                [lrecv[pl.ds(pl.multiple_of(first, piece), piece), :] for first in firsts],
                firsts, limit, store,
            )

    gram = None
    for k in range(PIECES + 1):
        if k < PIECES:
            gate_pieces(arrive(k), k, k * span)
        if k:
            gate_pieces(arrive_from_mates(k - 1), k - 1, (k - 1) * span + slots * piece)
            done = at_ref[:, (k - 1) * span : k * span]
            gram = nt(done, done) if gram is None else ga_ref[...] + nt(done, done)
            if k < PIECES:
                ga_ref[...] = gram
    gah_ref[...], gal_ref[...] = split2(gram)
    for copy in sent + forwarded:
        copy.wait_send()

    weight = jnp.exp(jnp.full((1, states), charges_ref[home], jnp.int32).astype(F32) * (-chemical))
    coef = (iota((bond, keep), 0) == start_ref[pl.ds(mirror, 1), :]).astype(F32)
    for round_index in range(ITERS + 1):
        image = presplit_nn((gah_ref[...], gal_ref[...]), coef)
        norm = lax.rsqrt(jnp.sum(coef * image, axis=0, keepdims=True))
        coef, image = coef * norm, image * norm
        inverse_factor(tn3(coef, image), s_ref, t_ref)
        if round_index < ITERS:
            image = nt3(image, t_ref[...])
            coef = presplit_nn((gbh_ref[...], gbl_ref[...]), image) * (weight * weight)
    kept_here = iota((bond, keep), 1) < kept_ref[home]
    csend[...] = jnp.where(kept_here, nt3(coef, t_ref[...]), 0.0).astype(BF16)
    out = jnp.where(kept_here, nt3(image, t_ref[...]) * weight, 0.0)
    msend[...] = out.astype(BF16)

    part = bond // mates
    bit = part // BITS

    def coef_rows(m, k):
        return pl.ds(pl.multiple_of(m * part + k * bit, bit), bit)

    def coef_at(t, m, k):
        return crecv.at[t, coef_rows(m, k), :]

    flying = []

    def go(*args):
        copy = remote(*args)
        copy.start()
        flying.append(copy)

    for k in range(BITS):
        go(
            csend.at[coef_rows(mate, k), :], coef_at(slot, mate, k), csems.at[0, k], cgets.at[0, k],
            (partner, row),
        )
    per = out * presplit_nn((gbh_ref[...], gbl_ref[...]), out)
    for d in range(1, slots):
        go(msend, mrecv.at[slot], msems.at[d - 1], mgets.at[d - 1], (sec, slot_row(other_slot(d))))
    total_ref[0] = jnp.sum(per, axis=0, keepdims=True)
    for d in range(sec_count):
        for e in range(slots):
            if d or e:
                index = d * slots + e
                go(
                    total_ref.at[0], total_ref.at[index], tsems.at[index], tgets.at[index],
                    (jnp.bitwise_xor(sec, d), slot_row(other_slot(e))),
                )

    part_rows = here * group
    part_cols = cols // row_count
    bw_ref[0] = b_ref[:, pl.ds(pl.multiple_of(row * part_cols, part_cols), part_cols)]

    def part_chunk(c, carry):
        e = 1 + c // (states // group)
        base = pl.multiple_of(lax.rem(c, states // group) * group, group)
        piece_rows = rown[e, pl.ds(base, group), :]
        stack = jnp.concatenate([piece_rows[:, j * width : (j + 1) * width] for j in range(site)], axis=0)
        pick = [
            jnp.concatenate([
                kr_ref[h, pl.ds(pl.multiple_of(term * block + row * part_rows, part_rows), part_rows), :]
                for term in range(terms)
            ], axis=0)
            for h in range(2)
        ]
        out = (nn(pick[0], stack) + nn(pick[1], stack)).astype(BF16)
        for term in range(terms):
            for i in range(here):
                bw_ref[e, pl.ds(term * states + base, group), i * width : (i + 1) * width] = out[
                    term * part_rows + i * group : term * part_rows + (i + 1) * group, :
                ]
        return carry

    lax.fori_loop(0, (slots - 1) * (states // group), part_chunk, 0)

    def pass_on(t, m, k, index):
        for d in range(1, mates):
            go(
                coef_at(t, m, k), coef_at(t, m, k), csems.at[index + d - 1, k], cgets.at[index + d - 1, k],
                (sec, slot * mates + other_mate(d)),
            )

    for k in range(BITS):
        flying[k].wait_recv()
        for e in range(1, slots):
            go(
                coef_at(slot, mate, k), coef_at(slot, mate, k), csems.at[e, k], cgets.at[e, k],
                (sec, slot_row(other_slot(e))),
            )
        pass_on(slot, mate, k, slots)
    wide = [tn(msend[...], bw_ref[0])]
    for k in range(BITS):
        for e in range(1, slots):
            t = other_slot(slots - e)
            remote(
                coef_at(t, mate, k), coef_at(t, mate, k), csems.at[e, k], cgets.at[e, k], (sec, slot_row(t))
            ).wait_recv()
            pass_on(t, mate, k, slots + e * (mates - 1))

    for d in range(1, slots):
        t = other_slot(slots - d)
        remote(
            msend, mrecv.at[t], msems.at[d - 1], mgets.at[d - 1], (sec, slot_row(t))
        ).wait_recv()
        wide.append(tn(mrecv[t], bw_ref[slots - d]))
    summed = total_ref[0]
    for d in range(sec_count):
        for e in range(slots):
            if d or e:
                index = d * slots + e
                remote(
                    total_ref.at[0], total_ref.at[index], tsems.at[index], tgets.at[index],
                    (jnp.bitwise_xor(sec, d), slot_row(other_slot(slots - e))),
                ).wait_recv()
                summed = summed + total_ref[index]
    scale = 1.0 / jnp.sqrt(jnp.sum(summed, keepdims=True))
    leaving = []

    def leave(source, target):
        copy = pltpu.make_async_copy(source, target, local.at[len(leaving)])
        copy.start()
        leaving.append(copy)

    for d in range(slots):
        t = other_slot(slots - d)
        w_out[d] = wide[d] * scale
        leave(w_out.at[d], w_hbm.at[t])

    for e in range(slots):
        t = other_slot(slots - e)
        for k in range(BITS):
            for d in range(1, mates):
                index = slots + e * (mates - 1) + d - 1
                m = other_mate(mates - d)
                remote(
                    coef_at(t, m, k), coef_at(t, m, k), csems.at[index, k], cgets.at[index, k],
                    (sec, slot * mates + m),
                ).wait_recv()
        u_out[e] = tn(own_ref[t], crecv[t])
        leave(u_out.at[e], u_hbm.at[t])
    for copy in flying:
        copy.wait_send()
    for copy in leaving:
        copy.wait()


def solution(mesh):
    row_count, sec_count = mesh.shape["row"], mesh.shape["sec"]

    def on_device(left_block, right_block, left_ops, right_ops, charges, live_states, kept, start):
        slots, rows, states = left_block.shape
        terms, site = left_ops.shape[0], left_ops.shape[1]
        cols, bond, keep = right_block.shape[2], terms * states, start.shape[1]
        block, mates = 256, row_count // slots
        part_cols = cols // row_count
        coef_copies = slots + slots * (mates - 1)
        peers = slots * sec_count
        dma = pltpu.SemaphoreType.DMA
        return pl.pallas_call(
            functools.partial(gate_kernel, row_count, sec_count),
            out_shape=(
                jax.ShapeDtypeStruct((slots, rows, keep), F32),
                jax.ShapeDtypeStruct((slots, keep, part_cols), F32),
            ),
            in_specs=[ANY] * 8,
            out_specs=[ANY] * 2,
            scratch_shapes=[
                pltpu.VMEM(left_ops.shape, F32),
                pltpu.VMEM(right_ops.shape, F32),
                pltpu.SMEM(charges.shape, jnp.int32),
                pltpu.SMEM(live_states.shape, jnp.int32),
                pltpu.SMEM(kept.shape, jnp.int32),
                pltpu.VMEM(start.shape, jnp.int32),
                pltpu.VMEM((slots, rows, keep), F32),
                pltpu.VMEM((slots, keep, part_cols), F32),
                pltpu.VMEM((slots, rows, states), BF16),
                pltpu.VMEM((rows * row_count, states), BF16),
                pltpu.VMEM((slots, states, cols), BF16),
                pltpu.VMEM((2, block, terms * block), BF16),
                pltpu.VMEM((2, terms * block, block), BF16),
                pltpu.VMEM((bond, rows * row_count), BF16),
                pltpu.VMEM((slots, bond, rows), BF16),
                pltpu.VMEM((bond, cols), BF16),
                pltpu.VMEM((slots, bond, part_cols), BF16),
                pltpu.VMEM((bond, bond), F32),
                pltpu.VMEM((bond, bond), BF16),
                pltpu.VMEM((bond, bond), BF16),
                pltpu.VMEM((bond, bond), BF16),
                pltpu.VMEM((bond, bond), BF16),
                pltpu.VMEM((keep, keep), F32),
                pltpu.VMEM((keep, keep), F32),
                pltpu.VMEM((bond, keep), BF16),
                pltpu.VMEM((slots, bond, keep), BF16),
                pltpu.VMEM((bond, keep), BF16),
                pltpu.VMEM((slots, bond, keep), BF16),
                pltpu.VMEM((peers, 1, keep), F32),
                dma((7 + slots,)),
                dma((slots, PIECES)), dma((slots, PIECES)),
                dma((mates - 1, slots, PIECES)), dma((mates - 1, slots, PIECES)),
                dma((coef_copies, BITS)), dma((coef_copies, BITS)),
                dma((slots - 1,)), dma((slots - 1,)),
                dma((peers,)), dma((peers,)),
            ],
            compiler_params=pltpu.CompilerParams(
                collective_id=0, has_side_effects=True, vmem_limit_bytes=56 * 2**20
            ),
        )(left_block, right_block, left_ops, right_ops, charges, live_states, kept, start)

    return jax.shard_map(
        on_device,
        mesh=mesh,
        in_specs=(P("sec", "row", None), P("sec", None, None), P(), P(), P(), P(), P(), P()),
        out_specs=(P("sec", "row", None), P("sec", None, "row")),
        check_vma=False,
    )
```

```python
import functools

import jax
import jax.numpy as jnp
from jax import lax
from jax.experimental import pallas as pl
from jax.experimental.pallas import tpu as pltpu
from jax.sharding import PartitionSpec as P

MESH = pl.DeviceIdType.MESH
HIGHEST = lax.Precision.HIGHEST
F32, BF16 = jnp.float32, jnp.bfloat16
chemical = 0.4
ITERS = 2
PANEL = 32
TILE = 8
RING = 4
PIECES = 4
BITS = 2
VM = pl.BlockSpec(memory_space=pltpu.VMEM)
SM = pl.BlockSpec(memory_space=pltpu.SMEM)
ANY = pl.BlockSpec(memory_space=pl.ANY)


def nn(a, b, precision=None):
    return lax.dot_general(
        a, b, (((1,), (0,)), ((), ())), precision=precision, preferred_element_type=F32
    )


def nt(a, b, precision=None):
    return lax.dot_general(
        a, b, (((1,), (1,)), ((), ())), precision=precision, preferred_element_type=F32
    )


def tn(a, b, precision=None):
    return lax.dot_general(
        a, b, (((0,), (0,)), ((), ())), precision=precision, preferred_element_type=F32
    )


def split2(x):
    high = x.astype(BF16)
    return high, (x - high.astype(F32)).astype(BF16)


def split3(x):
    high, rest = x.astype(BF16), None
    rest = x - high.astype(F32)
    mid = rest.astype(BF16)
    return high, mid, (rest - mid.astype(F32)).astype(BF16)


def presplit_nn(parts, x):
    high, low = split2(x)
    both = nn(parts[0], jnp.concatenate([high, low], axis=1))
    width = x.shape[1]
    return both[:, :width] + both[:, width:] + nn(parts[1], high)


def nt3(a, b):
    ah, al = split2(a)
    bh, bl = split2(b)
    return nt(jnp.concatenate([ah, al, ah], axis=1), jnp.concatenate([bh, bh, bl], axis=1))


def tn3(a, b):
    ah, al = split2(a)
    bh, bl = split2(b)
    return tn(jnp.concatenate([ah, al, ah], axis=0), jnp.concatenate([bh, bh, bl], axis=0))


def iota(shape, dim):
    return lax.broadcasted_iota(jnp.int32, shape, dim)


def spread(ops, row_of, col_of, same):
    site = ops.shape[0]
    pick_rows = (iota((row_of.shape[0], site), 1) == row_of).astype(BF16)
    pick_cols = (iota((site, col_of.shape[1]), 0) == col_of).astype(BF16)
    out = []
    for part in split2(ops):
        wide = nn(nn(pick_rows, part).astype(BF16), pick_cols)
        out.append(jnp.where(same, wide, 0.0).astype(BF16))
    return out


def eliminate_panel(x, base, ring_ref):
    size = x.shape[1]
    tiles = PANEL // TILE
    sub, lane = iota((TILE, size), 0), iota((TILE, size), 1)
    inside = (lane >= base) & (lane < base + PANEL)
    cols = [
        {
            h: jnp.broadcast_to(x[h * TILE : (h + 1) * TILE, base + c : base + c + 1], (TILE, size))
            for h in range(c // TILE, tiles)
        }
        for c in range(PANEL)
    ]
    rows = [
        jnp.where(inside, (lane - (base + h * TILE) == sub).astype(F32), x[h * TILE : (h + 1) * TILE])
        for h in range(tiles)
    ]
    for j in range(0, PANEL, 2):
        own, q = j // TILE, j % TILE
        first, second = cols[j], cols[j + 1]
        a, b, d = first[own][q : q + 1], first[own][q + 1 : q + 2], second[own][q + 1 : q + 2]
        held = j // 2 % RING
        for h in range(own, tiles):
            ring_ref[held, 0, h * TILE : (h + 1) * TILE, :] = first[h]
            ring_ref[held, 1, h * TILE : (h + 1) * TILE, :] = second[h]
        root = lax.rsqrt(a * d - b * b)
        inverse = root * root
        aa, bb, dd = a * inverse, b * inverse, d * inverse
        w1 = {h: first[h] * dd - second[h] * bb for h in range(own, tiles)}
        w2 = {h: second[h] * aa - first[h] * bb for h in range(own, tiles)}
        for i in range(j + 2, PANEL):
            at, r = i // TILE, i % TILE
            if i < j + 4:
                s1, s2 = first[at][r : r + 1], second[at][r : r + 1]
            else:
                s1, s2 = [ring_ref[held, n, pl.ds(i, TILE, stride=0), :] for n in range(2)]
            cols[i] = {h: cols[i][h] - w1[h] * s1 - w2[h] * s2 for h in range(at, tiles)}
        scale = lax.rsqrt(a)
        x1, x2 = rows[own][q : q + 1], rows[own][q + 1 : q + 2]
        for h in range(own + 1, tiles):
            rows[h] = rows[h] - w1[h] * x1 - w2[h] * x2
        later = rows[own]
        if q + 2 < TILE:
            later = later - jnp.where(sub > q + 1, w1[own], 0.0) * x1 - jnp.where(sub > q + 1, w2[own], 0.0) * x2
        top = x1 * scale
        bottom = (x2 - x1 * (b * scale * scale)) * (a * scale * root)
        rows[own] = jnp.where(sub == q, top, jnp.where(sub == q + 1, bottom, later))
    return jnp.concatenate(rows, axis=0)


def inverse_factor(gram, s_ref, t_ref, ring_ref):
    size = gram.shape[0]
    s_ref[...] = gram
    lane = iota((PANEL, size), 1)
    for base in range(0, size, PANEL):
        after = base + PANEL
        x = eliminate_panel(s_ref[base:after, :], base, ring_ref)
        t_ref[base:after, :] = jnp.where(lane < after, x, 0.0)
        if after == size:
            break
        parts = split3(x)
        masked = [jnp.where(lane >= after, y.astype(F32), 0.0).astype(BF16) for y in parts]
        pairs = ((0, 0), (0, 1), (1, 0), (1, 1), (0, 2), (2, 0))
        change = tn(
            jnp.concatenate([masked[i] for i, _ in pairs], axis=0),
            jnp.concatenate([parts[k] for _, k in pairs], axis=0),
        )
        inside = (lane[0:1] >= base) & (lane[0:1] < after)
        s_ref[after:, :] = jnp.where(inside, 0.0, s_ref[after:, :]) - change[after:, :]


def low_part(count):
    bits = count.bit_length() - 1
    return 1 << (bits // 2)


def gate_kernel(
    row_count, sec_count, left_hbm, right_hbm, lops_hbm, rops_hbm, charges_hbm, live_hbm, kept_hbm,
    start_hbm, u_hbm, w_hbm, lops_ref, rops_ref, charges_ref, live_ref, kept_ref, start_ref, u_out, w_out,
    lown, lrecv, rown, kl_ref, kr_ref, at_ref, own_ref, b_ref, bw_ref, ga_ref, gah_ref, gal_ref,
    gbh_ref, gbl_ref, s_ref, t_ref, ring_ref, csend, crecv, msend, mrecv, total_ref,
    local, lsend, lget, fsend, fget, csems, cgets, msems, mgets, tsems, tgets,
):
    slots, rows, states = left_hbm.shape
    terms, site = lops_ref.shape[0], lops_ref.shape[1]
    cols = right_hbm.shape[2]
    width = cols // site
    group = 256 // site
    block = group * site
    bond = terms * states
    keep = start_ref.shape[1]
    sector_count = slots * sec_count
    mates = row_count // slots
    here = site // row_count
    piece = rows // PIECES
    half = sec_count // 2

    sec, row = lax.axis_index("sec"), lax.axis_index("row")
    slot, mate = row // mates, row % mates
    partner = jnp.bitwise_xor(sec, half)
    home = sec * slots + slot
    mirror = lax.rem(home + sector_count // 2, sector_count)

    def slot_row(t):
        return t * mates + mate

    def other_slot(d):
        return lax.rem(slot + d, slots)

    def other_mate(d):
        return lax.rem(mate + d, mates)

    greeted = [(sec, slot * mates + other_mate(d)) for d in range(1, mates)]
    near_count = low_part(sec_count)
    far_count = sec_count // near_count
    greeted += [
        (jnp.bitwise_xor(sec, d), slot_row(other_slot(e)))
        for d in range(near_count) for e in range(slots) if d or e
    ]
    greeted += [(jnp.bitwise_xor(sec, h * near_count), row) for h in range(1, far_count)]
    greeted += [(partner, slot_row(other_slot(e))) for e in range(1, slots)]
    barrier = pltpu.get_barrier_semaphore()
    for device in greeted:
        pl.semaphore_signal(barrier, inc=1, device_id=device, device_id_type=MESH)

    near = [
        pltpu.make_async_copy(source, target, local.at[i])
        for i, (source, target) in enumerate((
            (rops_hbm, rops_ref), (lops_hbm, lops_ref), (charges_hbm, charges_ref), (live_hbm, live_ref),
            (kept_hbm, kept_ref), (start_hbm, start_ref), (left_hbm, lown),
        ))
    ]
    near += [
        pltpu.make_async_copy(right_hbm.at[other_slot(e)], rown.at[e], local.at[len(near) + e])
        for e in range(slots)
    ]
    for copy in near:
        copy.start()
    near[0].wait()

    r0, c0 = iota((block, 1), 0), iota((1, block), 1)
    for t in range(terms):
        parts = spread(rops_ref[t], r0 // group, c0 // group, (r0 % group) == (c0 % group))
        for h in range(2):
            kr_ref[h, t * block : (t + 1) * block, :] = parts[h]

    pl.semaphore_wait(barrier, len(greeted))

    def remote(source, target, send, recv, device):
        return pltpu.make_async_remote_copy(
            src_ref=source, dst_ref=target, send_sem=send, recv_sem=recv,
            device_id=device, device_id_type=MESH,
        )

    def rows_at(owner, k):
        return pl.ds(pl.multiple_of(owner * rows + k * piece, piece), piece)

    sent = []
    for k in range(PIECES):
        for t in range(slots):
            copy = remote(
                left_hbm.at[t, pl.ds(k * piece, piece), :], lrecv.at[rows_at(row, k), :],
                lsend.at[t, k], lget.at[slot, k], (partner, slot_row(t)),
            )
            copy.start()
            sent.append(copy)

    for copy in near[1:]:
        copy.wait()
    for t in range(terms):
        parts = spread(lops_ref[t].T, r0 % site, c0 % site, (r0 // site) == (c0 // site))
        for h in range(2):
            kl_ref[h, :, t * block : (t + 1) * block] = parts[h]

    def right_chunk(c, carry):
        base = pl.multiple_of(c * group, group)
        part = rown[0, pl.ds(base, group), :]
        stack = jnp.concatenate([part[:, j * width : (j + 1) * width] for j in range(site)], axis=0)
        out = (nn(kr_ref[0], stack) + nn(kr_ref[1], stack)).astype(BF16)
        for t in range(terms):
            for i in range(site):
                b_ref[pl.ds(t * states + base, group), i * width : (i + 1) * width] = out[
                    t * block + i * group : t * block + (i + 1) * group, :
                ]
        return carry

    lax.fori_loop(0, states // group, right_chunk, 0)
    gbh_ref[...], gbl_ref[...] = split2(nt(b_ref[...], b_ref[...]))

    def gate_left(parts, firsts, limit, store):
        parts = [
            jnp.where(iota(part.shape, 0) + first < limit, part.astype(F32), 0.0)
            for part, first in zip(parts, firsts)
        ]
        turned = jnp.concatenate(parts, axis=0).T.astype(BF16)
        out = nn(turned, kl_ref[0]) + nn(turned, kl_ref[1])
        for t in range(terms):
            store(t, out[:, t * block : (t + 1) * block].astype(BF16))

    def own_chunk(c, carry):
        t = c // (rows // block)
        q = lax.rem(c, rows // block)
        first = pl.multiple_of(q * block, block)

        def store(term, value):
            own_ref[t, term * states : (term + 1) * states, pl.ds(first, block)] = value

        owner = sec * slots + t
        gate_left(
            [lown[t, pl.ds(first, block), :]], [row * rows + first], live_ref[owner] * site, store
        )
        return carry

    lax.fori_loop(0, slots * (rows // block), own_chunk, 0)

    limit = live_ref[mirror] * site
    forwarded = []
    ready = block // piece
    span = row_count * piece
    def arrive(k):
        owners = []
        for t in range(slots):
            owner = slot_row(t)
            place = lrecv.at[rows_at(owner, k), :]
            remote(place, place, lsend.at[t, k], lget.at[t, k], (partner, owner)).wait_recv()
            for d in range(1, mates):
                copy = remote(
                    place, place, fsend.at[d - 1, t, k], fget.at[d - 1, t, k],
                    (sec, slot * mates + other_mate(d)),
                )
                copy.start()
                forwarded.append(copy)
            owners.append(owner)
        return owners

    def arrive_from_mates(k):
        owners = []
        for d in range(1, mates):
            for t in range(slots):
                owner = t * mates + other_mate(mates - d)
                place = lrecv.at[rows_at(owner, k), :]
                remote(
                    place, place, fsend.at[d - 1, t, k], fget.at[d - 1, t, k],
                    (sec, slot * mates + other_mate(mates - d)),
                ).wait_recv()
                owners.append(owner)
        return owners

    def gate_pieces(owners, k, column):
        for index in range(0, len(owners), ready):
            firsts = [owner * rows + k * piece for owner in owners[index : index + ready]]
            place = column + index * piece

            def store(t, value):
                at_ref[t * states : (t + 1) * states, place : place + block] = value

            gate_left(
                [lrecv[pl.ds(pl.multiple_of(first, piece), piece), :] for first in firsts],
                firsts, limit, store,
            )

    gram = None
    for k in range(PIECES + 1):
        if k < PIECES:
            gate_pieces(arrive(k), k, k * span)
        if k:
            gate_pieces(arrive_from_mates(k - 1), k - 1, (k - 1) * span + slots * piece)
            done = at_ref[:, (k - 1) * span : k * span]
            gram = nt(done, done) if gram is None else ga_ref[...] + nt(done, done)
            if k < PIECES:
                ga_ref[...] = gram
    gah_ref[...], gal_ref[...] = split2(gram)
    for copy in sent + forwarded:
        copy.wait_send()

    weight = jnp.exp(jnp.full((1, states), charges_ref[home], jnp.int32).astype(F32) * (-chemical))
    coef = (iota((bond, keep), 0) == start_ref[pl.ds(mirror, 1), :]).astype(F32)
    for round_index in range(ITERS + 1):
        image = presplit_nn((gah_ref[...], gal_ref[...]), coef)
        norm = lax.rsqrt(jnp.sum(coef * image, axis=0, keepdims=True))
        coef, image = coef * norm, image * norm
        inverse_factor(tn3(coef, image), s_ref, t_ref, ring_ref)
        if round_index < ITERS:
            image = nt3(image, t_ref[...])
            coef = presplit_nn((gbh_ref[...], gbl_ref[...]), image) * (weight * weight)
    kept_here = iota((bond, keep), 1) < kept_ref[home]
    csend[...] = jnp.where(kept_here, nt3(coef, t_ref[...]), 0.0).astype(BF16)

    part = bond // mates
    bit = part // BITS

    def coef_rows(m, k):
        return pl.ds(pl.multiple_of(m * part + k * bit, bit), bit)

    def coef_at(t, m, k):
        return crecv.at[t, coef_rows(m, k), :]

    def m_rows(m):
        return pl.ds(pl.multiple_of(m * part, part), part)

    flying = []

    def go(*args):
        copy = remote(*args)
        copy.start()
        flying.append(copy)

    out = jnp.where(kept_here, nt3(image, t_ref[...]) * weight, 0.0)
    for k in range(BITS):
        go(
            csend.at[coef_rows(mate, k), :], coef_at(slot, mate, k), csems.at[0, k], cgets.at[0, k],
            (partner, row),
        )
    msend[...] = out.astype(BF16)
    per = out * presplit_nn((gbh_ref[...], gbl_ref[...]), out)
    for e in range(1, slots):
        go(
            msend.at[m_rows(mate), :], mrecv.at[slot, m_rows(mate), :], msems.at[e - 1], mgets.at[e - 1],
            (sec, slot_row(other_slot(e))),
        )
    total_ref[0] = jnp.sum(per, axis=0, keepdims=True)

    def add_totals(start, peers):
        for n, device in enumerate(peers):
            index = start + 1 + n
            go(total_ref.at[start], total_ref.at[index], tsems.at[index], tgets.at[index], device)

    def sum_totals(start, peers):
        summed = total_ref[start]
        for n, device in enumerate(peers):
            index = start + 1 + n
            remote(
                total_ref.at[start], total_ref.at[index], tsems.at[index], tgets.at[index], device
            ).wait_recv()
            summed = summed + total_ref[index]
        return summed

    near_peers = [
        (jnp.bitwise_xor(sec, d), slot_row(other_slot(e)))
        for d in range(near_count) for e in range(slots) if d or e
    ]
    far_peers = [(jnp.bitwise_xor(sec, h * near_count), row) for h in range(1, far_count)]
    add_totals(0, near_peers)

    part_rows = here * group
    part_cols = cols // row_count
    bw_ref[0] = b_ref[:, pl.ds(pl.multiple_of(row * part_cols, part_cols), part_cols)]

    def part_chunk(c, carry):
        e = 1 + c // (states // group)
        base = pl.multiple_of(lax.rem(c, states // group) * group, group)
        piece_rows = rown[e, pl.ds(base, group), :]
        stack = jnp.concatenate([piece_rows[:, j * width : (j + 1) * width] for j in range(site)], axis=0)
        pick = [
            jnp.concatenate([
                kr_ref[h, pl.ds(pl.multiple_of(term * block + row * part_rows, part_rows), part_rows), :]
                for term in range(terms)
            ], axis=0)
            for h in range(2)
        ]
        out = (nn(pick[0], stack) + nn(pick[1], stack)).astype(BF16)
        for term in range(terms):
            for i in range(here):
                bw_ref[e, pl.ds(term * states + base, group), i * width : (i + 1) * width] = out[
                    term * part_rows + i * group : term * part_rows + (i + 1) * group, :
                ]
        return carry

    lax.fori_loop(0, (slots - 1) * (states // group), part_chunk, 0)

    def pass_on(t, m, k, index):
        for d in range(1, mates):
            go(
                coef_at(t, m, k), coef_at(t, m, k), csems.at[index + d - 1, k], cgets.at[index + d - 1, k],
                (sec, slot * mates + other_mate(d)),
            )

    far_start = len(near_peers) + 1
    total_ref[far_start] = sum_totals(0, near_peers)
    add_totals(far_start, far_peers)
    for k in range(BITS):
        flying[k].wait_recv()
        for e in range(1, slots):
            go(
                coef_at(slot, mate, k), coef_at(slot, mate, k), csems.at[e, k], cgets.at[e, k],
                (sec, slot_row(other_slot(e))),
            )
        pass_on(slot, mate, k, slots)
    number = slots - 1
    for e in range(1, slots):
        t = other_slot(slots - e)
        place = mrecv.at[t, m_rows(mate), :]
        remote(place, place, msems.at[e - 1], mgets.at[e - 1], (sec, slot_row(t))).wait_recv()
        for d in range(1, mates):
            go(place, place, msems.at[number], mgets.at[number], (sec, slot * mates + other_mate(d)))
            number += 1
    wide = [tn(msend[...], bw_ref[0])]
    for k in range(BITS):
        for e in range(1, slots):
            t = other_slot(slots - e)
            remote(
                coef_at(t, mate, k), coef_at(t, mate, k), csems.at[e, k], cgets.at[e, k], (sec, slot_row(t))
            ).wait_recv()
            pass_on(t, mate, k, slots + e * (mates - 1))
    number = slots - 1
    for e in range(1, slots):
        t = other_slot(slots - e)
        for d in range(1, mates):
            m = other_mate(mates - d)
            place = mrecv.at[t, m_rows(m), :]
            remote(place, place, msems.at[number], mgets.at[number], (sec, slot * mates + m)).wait_recv()
            number += 1
        wide.append(tn(mrecv[t], bw_ref[slots - e]))
    scale = 1.0 / jnp.sqrt(jnp.sum(sum_totals(far_start, far_peers), keepdims=True))
    leaving = []

    def leave(source, target):
        copy = pltpu.make_async_copy(source, target, local.at[len(leaving)])
        copy.start()
        leaving.append(copy)

    for d in range(slots):
        t = other_slot(slots - d)
        w_out[d] = wide[d] * scale
        leave(w_out.at[d], w_hbm.at[t])

    for e in range(slots):
        t = other_slot(slots - e)
        for k in range(BITS):
            for d in range(1, mates):
                index = slots + e * (mates - 1) + d - 1
                m = other_mate(mates - d)
                remote(
                    coef_at(t, m, k), coef_at(t, m, k), csems.at[index, k], cgets.at[index, k],
                    (sec, slot * mates + m),
                ).wait_recv()
        u_out[e] = tn(own_ref[t], crecv[t])
        leave(u_out.at[e], u_hbm.at[t])
    for copy in flying:
        copy.wait_send()
    for copy in leaving:
        copy.wait()


def solution(mesh):
    row_count, sec_count = mesh.shape["row"], mesh.shape["sec"]

    def on_device(left_block, right_block, left_ops, right_ops, charges, live_states, kept, start):
        slots, rows, states = left_block.shape
        terms, site = left_ops.shape[0], left_ops.shape[1]
        cols, bond, keep = right_block.shape[2], terms * states, start.shape[1]
        block, mates = 256, row_count // slots
        part_cols = cols // row_count
        coef_copies = slots + slots * (mates - 1)
        m_copies = (slots - 1) * mates
        near_count = low_part(sec_count)
        peers = slots * near_count + sec_count // near_count
        dma = pltpu.SemaphoreType.DMA
        return pl.pallas_call(
            functools.partial(gate_kernel, row_count, sec_count),
            out_shape=(
                jax.ShapeDtypeStruct((slots, rows, keep), F32),
                jax.ShapeDtypeStruct((slots, keep, part_cols), F32),
            ),
            in_specs=[ANY] * 8,
            out_specs=[ANY] * 2,
            scratch_shapes=[
                pltpu.VMEM(left_ops.shape, F32),
                pltpu.VMEM(right_ops.shape, F32),
                pltpu.SMEM(charges.shape, jnp.int32),
                pltpu.SMEM(live_states.shape, jnp.int32),
                pltpu.SMEM(kept.shape, jnp.int32),
                pltpu.VMEM(start.shape, jnp.int32),
                pltpu.VMEM((slots, rows, keep), F32),
                pltpu.VMEM((slots, keep, part_cols), F32),
                pltpu.VMEM((slots, rows, states), BF16),
                pltpu.VMEM((rows * row_count, states), BF16),
                pltpu.VMEM((slots, states, cols), BF16),
                pltpu.VMEM((2, block, terms * block), BF16),
                pltpu.VMEM((2, terms * block, block), BF16),
                pltpu.VMEM((bond, rows * row_count), BF16),
                pltpu.VMEM((slots, bond, rows), BF16),
                pltpu.VMEM((bond, cols), BF16),
                pltpu.VMEM((slots, bond, part_cols), BF16),
                pltpu.VMEM((bond, bond), F32),
                pltpu.VMEM((bond, bond), BF16),
                pltpu.VMEM((bond, bond), BF16),
                pltpu.VMEM((bond, bond), BF16),
                pltpu.VMEM((bond, bond), BF16),
                pltpu.VMEM((keep, keep), F32),
                pltpu.VMEM((keep, keep), F32),
                pltpu.VMEM((RING, 2, PANEL, keep), F32),
                pltpu.VMEM((bond, keep), BF16),
                pltpu.VMEM((slots, bond, keep), BF16),
                pltpu.VMEM((bond, keep), BF16),
                pltpu.VMEM((slots, bond, keep), BF16),
                pltpu.VMEM((peers, 1, keep), F32),
                dma((7 + slots,)),
                dma((slots, PIECES)), dma((slots, PIECES)),
                dma((mates - 1, slots, PIECES)), dma((mates - 1, slots, PIECES)),
                dma((coef_copies, BITS)), dma((coef_copies, BITS)),
                dma((m_copies,)), dma((m_copies,)),
                dma((peers,)), dma((peers,)),
            ],
            compiler_params=pltpu.CompilerParams(
                collective_id=0, has_side_effects=True, vmem_limit_bytes=56 * 2**20
            ),
        )(left_block, right_block, left_ops, right_ops, charges, live_states, kept, start)

    return jax.shard_map(
        on_device,
        mesh=mesh,
        in_specs=(P("sec", "row", None), P("sec", None, None), P(), P(), P(), P(), P(), P()),
        out_specs=(P("sec", "row", None), P("sec", None, "row")),
        check_vma=False,
    )
```

```python
import functools

import jax
import jax.numpy as jnp
from jax import lax
from jax.experimental import pallas as pl
from jax.experimental.pallas import tpu as pltpu
from jax.sharding import PartitionSpec as P

MESH = pl.DeviceIdType.MESH
HIGHEST = lax.Precision.HIGHEST
F32, BF16 = jnp.float32, jnp.bfloat16
chemical = 0.4
ITERS = 2
PANEL = 32
TILE = 8
RING = 4
PIECES = 4
BITS = 2
VM = pl.BlockSpec(memory_space=pltpu.VMEM)
SM = pl.BlockSpec(memory_space=pltpu.SMEM)
ANY = pl.BlockSpec(memory_space=pl.ANY)
HBM = pl.BlockSpec(memory_space=pltpu.HBM)


def nn(a, b, precision=None):
    return lax.dot_general(
        a, b, (((1,), (0,)), ((), ())), precision=precision, preferred_element_type=F32
    )


def nt(a, b, precision=None):
    return lax.dot_general(
        a, b, (((1,), (1,)), ((), ())), precision=precision, preferred_element_type=F32
    )


def tn(a, b, precision=None):
    return lax.dot_general(
        a, b, (((0,), (0,)), ((), ())), precision=precision, preferred_element_type=F32
    )


def split2(x):
    high = x.astype(BF16)
    return high, (x - high.astype(F32)).astype(BF16)


def split3(x):
    high, rest = x.astype(BF16), None
    rest = x - high.astype(F32)
    mid = rest.astype(BF16)
    return high, mid, (rest - mid.astype(F32)).astype(BF16)


def presplit_nn(parts, x):
    high, low = split2(x)
    both = nn(parts[0], jnp.concatenate([high, low], axis=1))
    width = x.shape[1]
    return both[:, :width] + both[:, width:] + nn(parts[1], high)


def nt3(a, b):
    ah, al = split2(a)
    bh, bl = split2(b)
    return nt(jnp.concatenate([ah, al, ah], axis=1), jnp.concatenate([bh, bh, bl], axis=1))


def tn3(a, b):
    ah, al = split2(a)
    bh, bl = split2(b)
    return tn(jnp.concatenate([ah, al, ah], axis=0), jnp.concatenate([bh, bh, bl], axis=0))


def iota(shape, dim):
    return lax.broadcasted_iota(jnp.int32, shape, dim)


def spread(ops, row_of, col_of, same):
    site = ops.shape[0]
    pick_rows = (iota((row_of.shape[0], site), 1) == row_of).astype(BF16)
    pick_cols = (iota((site, col_of.shape[1]), 0) == col_of).astype(BF16)
    out = []
    for part in split2(ops):
        wide = nn(nn(pick_rows, part).astype(BF16), pick_cols)
        out.append(jnp.where(same, wide, 0.0).astype(BF16))
    return out


def eliminate_panel(x, base, ring_ref):
    size = x.shape[1]
    tiles = PANEL // TILE
    sub, lane = iota((TILE, size), 0), iota((TILE, size), 1)
    inside = (lane >= base) & (lane < base + PANEL)
    cols = [
        {
            h: jnp.broadcast_to(x[h * TILE : (h + 1) * TILE, base + c : base + c + 1], (TILE, size))
            for h in range(c // TILE, tiles)
        }
        for c in range(PANEL)
    ]
    rows = [
        jnp.where(inside, (lane - (base + h * TILE) == sub).astype(F32), x[h * TILE : (h + 1) * TILE])
        for h in range(tiles)
    ]
    for j in range(0, PANEL, 2):
        own, q = j // TILE, j % TILE
        first, second = cols[j], cols[j + 1]
        a, b, d = first[own][q : q + 1], first[own][q + 1 : q + 2], second[own][q + 1 : q + 2]
        held = j // 2 % RING
        for h in range(own, tiles):
            ring_ref[held, 0, h * TILE : (h + 1) * TILE, :] = first[h]
            ring_ref[held, 1, h * TILE : (h + 1) * TILE, :] = second[h]
        root = lax.rsqrt(a * d - b * b)
        inverse = root * root
        aa, bb, dd = a * inverse, b * inverse, d * inverse
        w1 = {h: first[h] * dd - second[h] * bb for h in range(own, tiles)}
        w2 = {h: second[h] * aa - first[h] * bb for h in range(own, tiles)}
        for i in range(j + 2, PANEL):
            at, r = i // TILE, i % TILE
            if i < j + 4:
                s1, s2 = first[at][r : r + 1], second[at][r : r + 1]
            else:
                s1, s2 = [ring_ref[held, n, pl.ds(i, TILE, stride=0), :] for n in range(2)]
            cols[i] = {h: cols[i][h] - w1[h] * s1 - w2[h] * s2 for h in range(at, tiles)}
        scale = lax.rsqrt(a)
        x1, x2 = rows[own][q : q + 1], rows[own][q + 1 : q + 2]
        for h in range(own + 1, tiles):
            rows[h] = rows[h] - w1[h] * x1 - w2[h] * x2
        later = rows[own]
        if q + 2 < TILE:
            later = later - jnp.where(sub > q + 1, w1[own], 0.0) * x1 - jnp.where(sub > q + 1, w2[own], 0.0) * x2
        top = x1 * scale
        bottom = (x2 - x1 * (b * scale * scale)) * (a * scale * root)
        rows[own] = jnp.where(sub == q, top, jnp.where(sub == q + 1, bottom, later))
    return jnp.concatenate(rows, axis=0)


def inverse_factor(gram, s_ref, t_ref, ring_ref):
    size = gram.shape[0]
    s_ref[...] = gram
    lane = iota((PANEL, size), 1)
    for base in range(0, size, PANEL):
        after = base + PANEL
        x = eliminate_panel(s_ref[base:after, :], base, ring_ref)
        t_ref[base:after, :] = jnp.where(lane < after, x, 0.0)
        if after == size:
            break
        parts = split3(x)
        masked = [jnp.where(lane >= after, y.astype(F32), 0.0).astype(BF16) for y in parts]
        pairs = ((0, 0), (0, 1), (1, 0), (1, 1), (0, 2), (2, 0))
        change = tn(
            jnp.concatenate([masked[i] for i, _ in pairs], axis=0),
            jnp.concatenate([parts[k] for _, k in pairs], axis=0),
        )
        inside = (lane[0:1] >= base) & (lane[0:1] < after)
        s_ref[after:, :] = jnp.where(inside, 0.0, s_ref[after:, :]) - change[after:, :]


def low_part(count):
    bits = count.bit_length() - 1
    return 1 << (bits // 2)


def gate_kernel(
    row_count, sec_count, left_hbm, right_hbm, lops_hbm, rops_hbm, charges_hbm, live_hbm, kept_hbm,
    start_hbm, u_out, w_out, lops_ref, rops_ref, charges_ref, live_ref, kept_ref, start_ref,
    lown, lrecv, rown, kl_ref, kr_ref, at_ref, own_ref, b_ref, bw_ref, ga_ref, gah_ref, gal_ref,
    gbh_ref, gbl_ref, s_ref, t_ref, ring_ref, csend, crecv, msend, mrecv, total_ref,
    local, lsend, lget, fsend, fget, csems, cgets, msems, mgets, tsems, tgets,
):
    slots, rows, states = left_hbm.shape
    terms, site = lops_ref.shape[0], lops_ref.shape[1]
    cols = right_hbm.shape[2]
    width = cols // site
    group = 256 // site
    block = group * site
    bond = terms * states
    keep = start_ref.shape[1]
    sector_count = slots * sec_count
    mates = row_count // slots
    here = site // row_count
    piece = rows // PIECES
    half = sec_count // 2

    sec, row = lax.axis_index("sec"), lax.axis_index("row")
    slot, mate = row // mates, row % mates
    partner = jnp.bitwise_xor(sec, half)
    home = sec * slots + slot
    mirror = lax.rem(home + sector_count // 2, sector_count)

    def slot_row(t):
        return t * mates + mate

    def other_slot(d):
        return lax.rem(slot + d, slots)

    def other_mate(d):
        return lax.rem(mate + d, mates)

    greeted = [(sec, slot * mates + other_mate(d)) for d in range(1, mates)]
    near_count = low_part(sec_count)
    far_count = sec_count // near_count
    greeted += [
        (jnp.bitwise_xor(sec, d), slot_row(other_slot(e)))
        for d in range(near_count) for e in range(slots) if d or e
    ]
    greeted += [(jnp.bitwise_xor(sec, h * near_count), row) for h in range(1, far_count)]
    greeted += [(partner, slot_row(other_slot(e))) for e in range(1, slots)]
    barrier = pltpu.get_barrier_semaphore()
    for device in greeted:
        pl.semaphore_signal(barrier, inc=1, device_id=device, device_id_type=MESH)

    near = [
        pltpu.make_async_copy(source, target, local.at[i])
        for i, (source, target) in enumerate((
            (rops_hbm, rops_ref), (lops_hbm, lops_ref), (charges_hbm, charges_ref), (live_hbm, live_ref),
            (kept_hbm, kept_ref), (start_hbm, start_ref), (left_hbm, lown),
        ))
    ]
    near += [
        pltpu.make_async_copy(right_hbm.at[other_slot(e)], rown.at[e], local.at[len(near) + e])
        for e in range(slots)
    ]
    for copy in near:
        copy.start()
    near[0].wait()

    r0, c0 = iota((block, 1), 0), iota((1, block), 1)
    for t in range(terms):
        parts = spread(rops_ref[t], r0 // group, c0 // group, (r0 % group) == (c0 % group))
        for h in range(2):
            kr_ref[h, t * block : (t + 1) * block, :] = parts[h]

    pl.semaphore_wait(barrier, len(greeted))

    def remote(source, target, send, recv, device):
        return pltpu.make_async_remote_copy(
            src_ref=source, dst_ref=target, send_sem=send, recv_sem=recv,
            device_id=device, device_id_type=MESH,
        )

    def rows_at(owner, k):
        return pl.ds(pl.multiple_of(owner * rows + k * piece, piece), piece)

    sent = []
    for k in range(PIECES):
        for t in range(slots):
            copy = remote(
                left_hbm.at[t, pl.ds(k * piece, piece), :], lrecv.at[rows_at(row, k), :],
                lsend.at[t, k], lget.at[slot, k], (partner, slot_row(t)),
            )
            copy.start()
            sent.append(copy)

    for copy in near[1:]:
        copy.wait()
    for t in range(terms):
        parts = spread(lops_ref[t].T, r0 % site, c0 % site, (r0 // site) == (c0 // site))
        for h in range(2):
            kl_ref[h, :, t * block : (t + 1) * block] = parts[h]

    def right_chunk(c, carry):
        base = pl.multiple_of(c * group, group)
        part = rown[0, pl.ds(base, group), :]
        stack = jnp.concatenate([part[:, j * width : (j + 1) * width] for j in range(site)], axis=0)
        out = (nn(kr_ref[0], stack) + nn(kr_ref[1], stack)).astype(BF16)
        for t in range(terms):
            for i in range(site):
                b_ref[pl.ds(t * states + base, group), i * width : (i + 1) * width] = out[
                    t * block + i * group : t * block + (i + 1) * group, :
                ]
        return carry

    lax.fori_loop(0, states // group, right_chunk, 0)
    gbh_ref[...], gbl_ref[...] = split2(nt(b_ref[...], b_ref[...]))

    def gate_left(parts, firsts, limit, store):
        parts = [
            jnp.where(iota(part.shape, 0) + first < limit, part.astype(F32), 0.0)
            for part, first in zip(parts, firsts)
        ]
        turned = jnp.concatenate(parts, axis=0).T.astype(BF16)
        out = nn(turned, kl_ref[0]) + nn(turned, kl_ref[1])
        for t in range(terms):
            store(t, out[:, t * block : (t + 1) * block].astype(BF16))

    def own_chunk(c, carry):
        t = c // (rows // block)
        q = lax.rem(c, rows // block)
        first = pl.multiple_of(q * block, block)

        def store(term, value):
            own_ref[t, term * states : (term + 1) * states, pl.ds(first, block)] = value

        owner = sec * slots + t
        gate_left(
            [lown[t, pl.ds(first, block), :]], [row * rows + first], live_ref[owner] * site, store
        )
        return carry

    lax.fori_loop(0, slots * (rows // block), own_chunk, 0)

    limit = live_ref[mirror] * site
    forwarded = []
    ready = block // piece
    span = row_count * piece
    def arrive(k):
        owners = []
        for t in range(slots):
            owner = slot_row(t)
            place = lrecv.at[rows_at(owner, k), :]
            remote(place, place, lsend.at[t, k], lget.at[t, k], (partner, owner)).wait_recv()
            for d in range(1, mates):
                copy = remote(
                    place, place, fsend.at[d - 1, t, k], fget.at[d - 1, t, k],
                    (sec, slot * mates + other_mate(d)),
                )
                copy.start()
                forwarded.append(copy)
            owners.append(owner)
        return owners

    def arrive_from_mates(k):
        owners = []
        for d in range(1, mates):
            for t in range(slots):
                owner = t * mates + other_mate(mates - d)
                place = lrecv.at[rows_at(owner, k), :]
                remote(
                    place, place, fsend.at[d - 1, t, k], fget.at[d - 1, t, k],
                    (sec, slot * mates + other_mate(mates - d)),
                ).wait_recv()
                owners.append(owner)
        return owners

    def gate_pieces(owners, k, column):
        for index in range(0, len(owners), ready):
            firsts = [owner * rows + k * piece for owner in owners[index : index + ready]]
            place = column + index * piece

            def store(t, value):
                at_ref[t * states : (t + 1) * states, place : place + block] = value

            gate_left(
                [lrecv[pl.ds(pl.multiple_of(first, piece), piece), :] for first in firsts],
                firsts, limit, store,
            )

    gram = None
    for k in range(PIECES + 1):
        if k < PIECES:
            gate_pieces(arrive(k), k, k * span)
        if k:
            gate_pieces(arrive_from_mates(k - 1), k - 1, (k - 1) * span + slots * piece)
            done = at_ref[:, (k - 1) * span : k * span]
            gram = nt(done, done) if gram is None else ga_ref[...] + nt(done, done)
            if k < PIECES:
                ga_ref[...] = gram
    gah_ref[...], gal_ref[...] = split2(gram)
    for copy in sent + forwarded:
        copy.wait_send()

    weight = jnp.exp(jnp.full((1, states), charges_ref[home], jnp.int32).astype(F32) * (-chemical))
    coef = (iota((bond, keep), 0) == start_ref[pl.ds(mirror, 1), :]).astype(F32)
    for round_index in range(ITERS + 1):
        image = presplit_nn((gah_ref[...], gal_ref[...]), coef)
        norm = lax.rsqrt(jnp.sum(coef * image, axis=0, keepdims=True))
        coef, image = coef * norm, image * norm
        inverse_factor(tn3(coef, image), s_ref, t_ref, ring_ref)
        if round_index < ITERS:
            image = nt3(image, t_ref[...])
            coef = presplit_nn((gbh_ref[...], gbl_ref[...]), image) * (weight * weight)
    kept_here = iota((bond, keep), 1) < kept_ref[home]
    csend[...] = jnp.where(kept_here, nt3(coef, t_ref[...]), 0.0).astype(BF16)

    part = bond // mates
    bit = part // BITS

    def coef_rows(m, k):
        return pl.ds(pl.multiple_of(m * part + k * bit, bit), bit)

    def coef_at(t, m, k):
        return crecv.at[t, coef_rows(m, k), :]

    def m_rows(m):
        return pl.ds(pl.multiple_of(m * part, part), part)

    flying = []

    def go(*args):
        copy = remote(*args)
        copy.start()
        flying.append(copy)

    out = jnp.where(kept_here, nt3(image, t_ref[...]) * weight, 0.0)
    for k in range(BITS):
        go(
            csend.at[coef_rows(mate, k), :], coef_at(slot, mate, k), csems.at[0, k], cgets.at[0, k],
            (partner, row),
        )
    msend[...] = out.astype(BF16)
    per = out * presplit_nn((gbh_ref[...], gbl_ref[...]), out)
    for e in range(1, slots):
        go(
            msend.at[m_rows(mate), :], mrecv.at[slot, m_rows(mate), :], msems.at[e - 1], mgets.at[e - 1],
            (sec, slot_row(other_slot(e))),
        )
    total_ref[0] = jnp.sum(per, axis=0, keepdims=True)

    def add_totals(start, peers):
        for n, device in enumerate(peers):
            index = start + 1 + n
            go(total_ref.at[start], total_ref.at[index], tsems.at[index], tgets.at[index], device)

    def sum_totals(start, peers):
        summed = total_ref[start]
        for n, device in enumerate(peers):
            index = start + 1 + n
            remote(
                total_ref.at[start], total_ref.at[index], tsems.at[index], tgets.at[index], device
            ).wait_recv()
            summed = summed + total_ref[index]
        return summed

    near_peers = [
        (jnp.bitwise_xor(sec, d), slot_row(other_slot(e)))
        for d in range(near_count) for e in range(slots) if d or e
    ]
    far_peers = [(jnp.bitwise_xor(sec, h * near_count), row) for h in range(1, far_count)]
    add_totals(0, near_peers)

    part_rows = here * group
    part_cols = cols // row_count
    bw_ref[0] = b_ref[:, pl.ds(pl.multiple_of(row * part_cols, part_cols), part_cols)]

    def part_chunk(c, carry):
        e = 1 + c // (states // group)
        base = pl.multiple_of(lax.rem(c, states // group) * group, group)
        piece_rows = rown[e, pl.ds(base, group), :]
        stack = jnp.concatenate([piece_rows[:, j * width : (j + 1) * width] for j in range(site)], axis=0)
        pick = [
            jnp.concatenate([
                kr_ref[h, pl.ds(pl.multiple_of(term * block + row * part_rows, part_rows), part_rows), :]
                for term in range(terms)
            ], axis=0)
            for h in range(2)
        ]
        out = (nn(pick[0], stack) + nn(pick[1], stack)).astype(BF16)
        for term in range(terms):
            for i in range(here):
                bw_ref[e, pl.ds(term * states + base, group), i * width : (i + 1) * width] = out[
                    term * part_rows + i * group : term * part_rows + (i + 1) * group, :
                ]
        return carry

    lax.fori_loop(0, (slots - 1) * (states // group), part_chunk, 0)

    def pass_on(t, m, k, index):
        for d in range(1, mates):
            go(
                coef_at(t, m, k), coef_at(t, m, k), csems.at[index + d - 1, k], cgets.at[index + d - 1, k],
                (sec, slot * mates + other_mate(d)),
            )

    far_start = len(near_peers) + 1
    total_ref[far_start] = sum_totals(0, near_peers)
    add_totals(far_start, far_peers)
    for k in range(BITS):
        flying[k].wait_recv()
        for e in range(1, slots):
            go(
                coef_at(slot, mate, k), coef_at(slot, mate, k), csems.at[e, k], cgets.at[e, k],
                (sec, slot_row(other_slot(e))),
            )
        pass_on(slot, mate, k, slots)
    number = slots - 1
    for e in range(1, slots):
        t = other_slot(slots - e)
        place = mrecv.at[t, m_rows(mate), :]
        remote(place, place, msems.at[e - 1], mgets.at[e - 1], (sec, slot_row(t))).wait_recv()
        for d in range(1, mates):
            go(place, place, msems.at[number], mgets.at[number], (sec, slot * mates + other_mate(d)))
            number += 1
    wide = [tn(msend[...], bw_ref[0])]
    for k in range(BITS):
        for e in range(1, slots):
            t = other_slot(slots - e)
            remote(
                coef_at(t, mate, k), coef_at(t, mate, k), csems.at[e, k], cgets.at[e, k], (sec, slot_row(t))
            ).wait_recv()
            pass_on(t, mate, k, slots + e * (mates - 1))
    number = slots - 1
    for e in range(1, slots):
        t = other_slot(slots - e)
        for d in range(1, mates):
            m = other_mate(mates - d)
            place = mrecv.at[t, m_rows(m), :]
            remote(place, place, msems.at[number], mgets.at[number], (sec, slot * mates + m)).wait_recv()
            number += 1
        wide.append(tn(mrecv[t], bw_ref[slots - e]))
    scale = 1.0 / jnp.sqrt(jnp.sum(sum_totals(far_start, far_peers), keepdims=True))
    for d in range(slots):
        w_out[other_slot(slots - d)] = wide[d] * scale

    for e in range(slots):
        t = other_slot(slots - e)
        for k in range(BITS):
            for d in range(1, mates):
                index = slots + e * (mates - 1) + d - 1
                m = other_mate(mates - d)
                remote(
                    coef_at(t, m, k), coef_at(t, m, k), csems.at[index, k], cgets.at[index, k],
                    (sec, slot * mates + m),
                ).wait_recv()
        u_out[t] = tn(own_ref[t], crecv[t])
    for copy in flying:
        copy.wait_send()


def solution(mesh):
    row_count, sec_count = mesh.shape["row"], mesh.shape["sec"]

    def on_device(left_block, right_block, left_ops, right_ops, charges, live_states, kept, start):
        slots, rows, states = left_block.shape
        terms, site = left_ops.shape[0], left_ops.shape[1]
        cols, bond, keep = right_block.shape[2], terms * states, start.shape[1]
        block, mates = 256, row_count // slots
        part_cols = cols // row_count
        coef_copies = slots + slots * (mates - 1)
        m_copies = (slots - 1) * mates
        near_count = low_part(sec_count)
        peers = slots * near_count + sec_count // near_count
        dma = pltpu.SemaphoreType.DMA
        u_shape, w_shape = (slots, rows, keep), (slots, keep, part_cols)
        return pl.pallas_call(
            functools.partial(gate_kernel, row_count, sec_count),
            out_shape=(pltpu.VMEM(u_shape, F32), pltpu.VMEM(w_shape, F32)),
            in_specs=[HBM] * 8,
            out_specs=[VM] * 2,
            scratch_shapes=[
                pltpu.VMEM(left_ops.shape, F32),
                pltpu.VMEM(right_ops.shape, F32),
                pltpu.SMEM(charges.shape, jnp.int32),
                pltpu.SMEM(live_states.shape, jnp.int32),
                pltpu.SMEM(kept.shape, jnp.int32),
                pltpu.VMEM(start.shape, jnp.int32),
                pltpu.VMEM((slots, rows, states), BF16),
                pltpu.VMEM((rows * row_count, states), BF16),
                pltpu.VMEM((slots, states, cols), BF16),
                pltpu.VMEM((2, block, terms * block), BF16),
                pltpu.VMEM((2, terms * block, block), BF16),
                pltpu.VMEM((bond, rows * row_count), BF16),
                pltpu.VMEM((slots, bond, rows), BF16),
                pltpu.VMEM((bond, cols), BF16),
                pltpu.VMEM((slots, bond, part_cols), BF16),
                pltpu.VMEM((bond, bond), F32),
                pltpu.VMEM((bond, bond), BF16),
                pltpu.VMEM((bond, bond), BF16),
                pltpu.VMEM((bond, bond), BF16),
                pltpu.VMEM((bond, bond), BF16),
                pltpu.VMEM((keep, keep), F32),
                pltpu.VMEM((keep, keep), F32),
                pltpu.VMEM((RING, 2, PANEL, keep), F32),
                pltpu.VMEM((bond, keep), BF16),
                pltpu.VMEM((slots, bond, keep), BF16),
                pltpu.VMEM((bond, keep), BF16),
                pltpu.VMEM((slots, bond, keep), BF16),
                pltpu.VMEM((peers, 1, keep), F32),
                dma((7 + slots,)),
                dma((slots, PIECES)), dma((slots, PIECES)),
                dma((mates - 1, slots, PIECES)), dma((mates - 1, slots, PIECES)),
                dma((coef_copies, BITS)), dma((coef_copies, BITS)),
                dma((m_copies,)), dma((m_copies,)),
                dma((peers,)), dma((peers,)),
            ],
            compiler_params=pltpu.CompilerParams(
                collective_id=0, has_side_effects=True, vmem_limit_bytes=62 * 2**20
            ),
        )(left_block, right_block, left_ops, right_ops, charges, live_states, kept, start)
    return jax.shard_map(
        on_device,
        mesh=mesh,
        in_specs=(P("sec", "row", None), P("sec", None, None), P(), P(), P(), P(), P(), P()),
        out_specs=(P("sec", "row", None), P("sec", None, "row")),
        check_vma=False,
    )
```

```python
import functools

import jax
import jax.numpy as jnp
from jax import lax
from jax.experimental import pallas as pl
from jax.experimental.pallas import tpu as pltpu
from jax.sharding import PartitionSpec as P

MESH = pl.DeviceIdType.MESH
HIGHEST = lax.Precision.HIGHEST
F32, BF16 = jnp.float32, jnp.bfloat16
chemical = 0.4
ITERS = 2
PANEL = 32
TILE = 8
RING = 4
PIECES = 4
BITS = 2
VM = pl.BlockSpec(memory_space=pltpu.VMEM)
SM = pl.BlockSpec(memory_space=pltpu.SMEM)
ANY = pl.BlockSpec(memory_space=pl.ANY)
HBM = pl.BlockSpec(memory_space=pltpu.HBM)


def nn(a, b, precision=None):
    return lax.dot_general(
        a, b, (((1,), (0,)), ((), ())), precision=precision, preferred_element_type=F32
    )


def nt(a, b, precision=None):
    return lax.dot_general(
        a, b, (((1,), (1,)), ((), ())), precision=precision, preferred_element_type=F32
    )


def tn(a, b, precision=None):
    return lax.dot_general(
        a, b, (((0,), (0,)), ((), ())), precision=precision, preferred_element_type=F32
    )


def split2(x):
    high = x.astype(BF16)
    return high, (x - high.astype(F32)).astype(BF16)


def split3(x):
    high, rest = x.astype(BF16), None
    rest = x - high.astype(F32)
    mid = rest.astype(BF16)
    return high, mid, (rest - mid.astype(F32)).astype(BF16)


def presplit_nn(parts, x):
    high, low = split2(x)
    both = nn(parts[0], jnp.concatenate([high, low], axis=1))
    width = x.shape[1]
    return both[:, :width] + both[:, width:] + nn(parts[1], high)


def nt3(a, b):
    ah, al = split2(a)
    bh, bl = split2(b)
    return nt(jnp.concatenate([ah, al, ah], axis=1), jnp.concatenate([bh, bh, bl], axis=1))


def tn3(a, b):
    ah, al = split2(a)
    bh, bl = split2(b)
    return tn(jnp.concatenate([ah, al, ah], axis=0), jnp.concatenate([bh, bh, bl], axis=0))


def iota(shape, dim):
    return lax.broadcasted_iota(jnp.int32, shape, dim)


def spread(ops, row_of, col_of, same):
    site = ops.shape[0]
    pick_rows = (iota((row_of.shape[0], site), 1) == row_of).astype(BF16)
    pick_cols = (iota((site, col_of.shape[1]), 0) == col_of).astype(BF16)
    out = []
    for part in split2(ops):
        wide = nn(nn(pick_rows, part).astype(BF16), pick_cols)
        out.append(jnp.where(same, wide, 0.0).astype(BF16))
    return out


def eliminate_panel(x, base, ring_ref):
    size = x.shape[1]
    tiles = PANEL // TILE
    sub, lane = iota((TILE, size), 0), iota((TILE, size), 1)
    inside = (lane >= base) & (lane < base + PANEL)
    cols = [
        {
            h: jnp.broadcast_to(x[h * TILE : (h + 1) * TILE, base + c : base + c + 1], (TILE, size))
            for h in range(c // TILE, tiles)
        }
        for c in range(PANEL)
    ]
    rows = [
        jnp.where(inside, (lane - (base + h * TILE) == sub).astype(F32), x[h * TILE : (h + 1) * TILE])
        for h in range(tiles)
    ]
    for j in range(0, PANEL, 2):
        own, q = j // TILE, j % TILE
        first, second = cols[j], cols[j + 1]
        a, b, d = first[own][q : q + 1], first[own][q + 1 : q + 2], second[own][q + 1 : q + 2]
        held = j // 2 % RING
        for h in range(own, tiles):
            ring_ref[held, 0, h * TILE : (h + 1) * TILE, :] = first[h]
            ring_ref[held, 1, h * TILE : (h + 1) * TILE, :] = second[h]
        root = lax.rsqrt(a * d - b * b)
        inverse = root * root
        aa, bb, dd = a * inverse, b * inverse, d * inverse
        w1 = {h: first[h] * dd - second[h] * bb for h in range(own, tiles)}
        w2 = {h: second[h] * aa - first[h] * bb for h in range(own, tiles)}
        for i in range(j + 2, PANEL):
            at, r = i // TILE, i % TILE
            if i < j + 4:
                s1, s2 = first[at][r : r + 1], second[at][r : r + 1]
            else:
                s1, s2 = [ring_ref[held, n, pl.ds(i, TILE, stride=0), :] for n in range(2)]
            cols[i] = {h: cols[i][h] - w1[h] * s1 - w2[h] * s2 for h in range(at, tiles)}
        scale = lax.rsqrt(a)
        x1, x2 = rows[own][q : q + 1], rows[own][q + 1 : q + 2]
        for h in range(own + 1, tiles):
            rows[h] = rows[h] - w1[h] * x1 - w2[h] * x2
        later = rows[own]
        if q + 2 < TILE:
            later = later - jnp.where(sub > q + 1, w1[own], 0.0) * x1 - jnp.where(sub > q + 1, w2[own], 0.0) * x2
        top = x1 * scale
        bottom = (x2 - x1 * (b * scale * scale)) * (a * scale * root)
        rows[own] = jnp.where(sub == q, top, jnp.where(sub == q + 1, bottom, later))
    return jnp.concatenate(rows, axis=0)


def inverse_factor(gram, s_ref, t_ref, ring_ref):
    size = gram.shape[0]
    s_ref[...] = gram
    lane = iota((PANEL, size), 1)
    for base in range(0, size, PANEL):
        after = base + PANEL
        x = eliminate_panel(s_ref[base:after, :], base, ring_ref)
        t_ref[base:after, :] = jnp.where(lane < after, x, 0.0)
        if after == size:
            break
        parts = split3(x)
        masked = [jnp.where(lane >= after, y.astype(F32), 0.0).astype(BF16) for y in parts]
        pairs = ((0, 0), (0, 1), (1, 0), (1, 1), (0, 2), (2, 0))
        change = tn(
            jnp.concatenate([masked[i] for i, _ in pairs], axis=0),
            jnp.concatenate([parts[k] for _, k in pairs], axis=0),
        )
        inside = (lane[0:1] >= base) & (lane[0:1] < after)
        s_ref[after:, :] = jnp.where(inside, 0.0, s_ref[after:, :]) - change[after:, :]


def low_part(count):
    bits = count.bit_length() - 1
    return 1 << (bits // 2)


def gate_kernel(
    row_count, sec_count, left_hbm, right_hbm, lops_hbm, rops_hbm, charges_hbm, live_hbm, kept_hbm,
    start_hbm, u_out, w_out, lops_ref, rops_ref, charges_ref, live_ref, kept_ref, start_ref,
    lown, lrecv, rown, kl_ref, kr_ref, at_ref, own_ref, b_ref, bw_ref, ga_ref, gah_ref, gal_ref,
    gbh_ref, gbl_ref, s_ref, t_ref, ring_ref, coef_ref, csend, crecv, msend, mrecv, total_ref,
    local, lsend, lget, fsend, fget, csems, cgets, msems, mgets, tsems, tgets,
):
    slots, rows, states = left_hbm.shape
    terms, site = lops_ref.shape[0], lops_ref.shape[1]
    cols = right_hbm.shape[2]
    width = cols // site
    group = 256 // site
    block = group * site
    bond = terms * states
    keep = start_ref.shape[1]
    sector_count = slots * sec_count
    mates = row_count // slots
    here = site // row_count
    piece = rows // PIECES
    half = sec_count // 2

    sec, row = lax.axis_index("sec"), lax.axis_index("row")
    slot, mate = row // mates, row % mates
    partner = jnp.bitwise_xor(sec, half)
    home = sec * slots + slot
    mirror = lax.rem(home + sector_count // 2, sector_count)

    def slot_row(t):
        return t * mates + mate

    def other_slot(d):
        return lax.rem(slot + d, slots)

    def other_mate(d):
        return lax.rem(mate + d, mates)

    greeted = [(sec, slot * mates + other_mate(d)) for d in range(1, mates)]
    near_count = low_part(sec_count)
    far_count = sec_count // near_count
    greeted += [
        (jnp.bitwise_xor(sec, d), slot_row(other_slot(e)))
        for d in range(near_count) for e in range(slots) if d or e
    ]
    greeted += [(jnp.bitwise_xor(sec, h * near_count), row) for h in range(1, far_count)]
    greeted += [(partner, slot_row(other_slot(e))) for e in range(1, slots)]
    barrier = pltpu.get_barrier_semaphore()
    for device in greeted:
        pl.semaphore_signal(barrier, inc=1, device_id=device, device_id_type=MESH)

    near = [
        pltpu.make_async_copy(source, target, local.at[i])
        for i, (source, target) in enumerate((
            (rops_hbm, rops_ref), (lops_hbm, lops_ref), (charges_hbm, charges_ref), (live_hbm, live_ref),
            (kept_hbm, kept_ref), (start_hbm, start_ref), (left_hbm, lown),
        ))
    ]
    near += [
        pltpu.make_async_copy(right_hbm.at[other_slot(e)], rown.at[e], local.at[len(near) + e])
        for e in range(slots)
    ]
    for copy in near:
        copy.start()
    near[0].wait()

    r0, c0 = iota((block, 1), 0), iota((1, block), 1)
    for t in range(terms):
        parts = spread(rops_ref[t], r0 // group, c0 // group, (r0 % group) == (c0 % group))
        for h in range(2):
            kr_ref[h, t * block : (t + 1) * block, :] = parts[h]

    pl.semaphore_wait(barrier, len(greeted))

    def remote(source, target, send, recv, device):
        return pltpu.make_async_remote_copy(
            src_ref=source, dst_ref=target, send_sem=send, recv_sem=recv,
            device_id=device, device_id_type=MESH,
        )

    def rows_at(owner, k):
        return pl.ds(pl.multiple_of(owner * rows + k * piece, piece), piece)

    sent = []
    for k in range(PIECES):
        for t in range(slots):
            copy = remote(
                left_hbm.at[t, pl.ds(k * piece, piece), :], lrecv.at[rows_at(row, k), :],
                lsend.at[t, k], lget.at[slot, k], (partner, slot_row(t)),
            )
            copy.start()
            sent.append(copy)

    for copy in near[1:]:
        copy.wait()
    for t in range(terms):
        parts = spread(lops_ref[t].T, r0 % site, c0 % site, (r0 // site) == (c0 // site))
        for h in range(2):
            kl_ref[h, :, t * block : (t + 1) * block] = parts[h]

    def right_chunk(c, carry):
        base = pl.multiple_of(c * group, group)
        part = rown[0, pl.ds(base, group), :]
        stack = jnp.concatenate([part[:, j * width : (j + 1) * width] for j in range(site)], axis=0)
        out = (nn(kr_ref[0], stack) + nn(kr_ref[1], stack)).astype(BF16)
        for t in range(terms):
            for i in range(site):
                b_ref[pl.ds(t * states + base, group), i * width : (i + 1) * width] = out[
                    t * block + i * group : t * block + (i + 1) * group, :
                ]
        return carry

    lax.fori_loop(0, states // group, right_chunk, 0)
    gbh_ref[...], gbl_ref[...] = split2(nt(b_ref[...], b_ref[...]))

    def gate_left(parts, firsts, limit, store):
        parts = [
            jnp.where(iota(part.shape, 0) + first < limit, part.astype(F32), 0.0)
            for part, first in zip(parts, firsts)
        ]
        turned = jnp.concatenate(parts, axis=0).T.astype(BF16)
        out = nn(turned, kl_ref[0]) + nn(turned, kl_ref[1])
        for t in range(terms):
            store(t, out[:, t * block : (t + 1) * block].astype(BF16))

    def own_chunk(c, carry):
        t = c // (rows // block)
        q = lax.rem(c, rows // block)
        first = pl.multiple_of(q * block, block)

        def store(term, value):
            own_ref[t, pl.ds(first, block), term * states : (term + 1) * states] = value.T

        owner = sec * slots + t
        gate_left(
            [lown[t, pl.ds(first, block), :]], [row * rows + first], live_ref[owner] * site, store
        )
        return carry

    lax.fori_loop(0, slots * (rows // block), own_chunk, 0)

    limit = live_ref[mirror] * site
    forwarded = []
    ready = block // piece
    span = row_count * piece
    def arrive(k):
        owners = []
        for t in range(slots):
            owner = slot_row(t)
            place = lrecv.at[rows_at(owner, k), :]
            remote(place, place, lsend.at[t, k], lget.at[t, k], (partner, owner)).wait_recv()
            for d in range(1, mates):
                copy = remote(
                    place, place, fsend.at[d - 1, t, k], fget.at[d - 1, t, k],
                    (sec, slot * mates + other_mate(d)),
                )
                copy.start()
                forwarded.append(copy)
            owners.append(owner)
        return owners

    def arrive_from_mates(k):
        owners = []
        for d in range(1, mates):
            for t in range(slots):
                owner = t * mates + other_mate(mates - d)
                place = lrecv.at[rows_at(owner, k), :]
                remote(
                    place, place, fsend.at[d - 1, t, k], fget.at[d - 1, t, k],
                    (sec, slot * mates + other_mate(mates - d)),
                ).wait_recv()
                owners.append(owner)
        return owners

    def gate_pieces(owners, k, column):
        for index in range(0, len(owners), ready):
            firsts = [owner * rows + k * piece for owner in owners[index : index + ready]]
            place = column + index * piece

            def store(t, value):
                at_ref[t * states : (t + 1) * states, place : place + block] = value

            gate_left(
                [lrecv[pl.ds(pl.multiple_of(first, piece), piece), :] for first in firsts],
                firsts, limit, store,
            )

    gram = None
    for k in range(PIECES + 1):
        if k < PIECES:
            gate_pieces(arrive(k), k, k * span)
        if k:
            gate_pieces(arrive_from_mates(k - 1), k - 1, (k - 1) * span + slots * piece)
            done = at_ref[:, (k - 1) * span : k * span]
            gram = nt(done, done) if gram is None else ga_ref[...] + nt(done, done)
            if k < PIECES:
                ga_ref[...] = gram
    gah_ref[...], gal_ref[...] = split2(gram)
    for copy in sent + forwarded:
        copy.wait_send()

    weight = jnp.exp(jnp.full((1, states), charges_ref[home], jnp.int32).astype(F32) * (-chemical))
    coef = (iota((bond, keep), 0) == start_ref[pl.ds(mirror, 1), :]).astype(F32)
    for round_index in range(ITERS + 1):
        image = presplit_nn((gah_ref[...], gal_ref[...]), coef)
        norm = lax.rsqrt(jnp.sum(coef * image, axis=0, keepdims=True))
        coef, image = coef * norm, image * norm
        inverse_factor(tn3(coef, image), s_ref, t_ref, ring_ref)
        if round_index < ITERS:
            image = nt3(image, t_ref[...])
            coef = presplit_nn((gbh_ref[...], gbl_ref[...]), image) * (weight * weight)
    kept_here = iota((bond, keep), 1) < kept_ref[home]
    part = bond // mates
    bit = part // BITS

    def coef_rows(m, k):
        return pl.ds(pl.multiple_of(m * part + k * bit, bit), bit)

    def coef_at(t, m, k):
        return crecv.at[t, coef_rows(m, k), :]

    def m_rows(m):
        return pl.ds(pl.multiple_of(m * part, part), part)

    coef_ref[...] = coef
    kept_part = iota((part, keep), 1) < kept_ref[home]
    csend[...] = jnp.where(kept_part, nt3(coef_ref[m_rows(mate), :], t_ref[...]), 0.0).astype(BF16)

    flying = []

    def go(*args):
        copy = remote(*args)
        copy.start()
        flying.append(copy)

    for k in range(BITS):
        go(
            csend.at[pl.ds(k * bit, bit), :], coef_at(slot, mate, k), csems.at[0, k], cgets.at[0, k],
            (partner, row),
        )
    out = jnp.where(kept_here, nt3(image, t_ref[...]) * weight, 0.0)
    msend[...] = out.astype(BF16)
    per = out * presplit_nn((gbh_ref[...], gbl_ref[...]), out)
    total_ref[0] = jnp.sum(per, axis=0, keepdims=True)

    def add_totals(start, peers):
        for n, device in enumerate(peers):
            index = start + 1 + n
            go(total_ref.at[start], total_ref.at[index], tsems.at[index], tgets.at[index], device)

    def sum_totals(start, peers):
        summed = total_ref[start]
        for n, device in enumerate(peers):
            index = start + 1 + n
            remote(
                total_ref.at[start], total_ref.at[index], tsems.at[index], tgets.at[index], device
            ).wait_recv()
            summed = summed + total_ref[index]
        return summed

    near_peers = [
        (jnp.bitwise_xor(sec, d), slot_row(other_slot(e)))
        for d in range(near_count) for e in range(slots) if d or e
    ]
    far_peers = [(jnp.bitwise_xor(sec, h * near_count), row) for h in range(1, far_count)]
    add_totals(0, near_peers)
    for e in range(1, slots):
        go(
            msend.at[m_rows(mate), :], mrecv.at[slot, m_rows(mate), :], msems.at[e - 1], mgets.at[e - 1],
            (sec, slot_row(other_slot(e))),
        )

    part_rows = here * group
    part_cols = cols // row_count
    bw_ref[0] = b_ref[:, pl.ds(pl.multiple_of(row * part_cols, part_cols), part_cols)]

    def part_chunk(c, carry):
        e = 1 + c // (states // group)
        base = pl.multiple_of(lax.rem(c, states // group) * group, group)
        piece_rows = rown[e, pl.ds(base, group), :]
        stack = jnp.concatenate([piece_rows[:, j * width : (j + 1) * width] for j in range(site)], axis=0)
        pick = [
            jnp.concatenate([
                kr_ref[h, pl.ds(pl.multiple_of(term * block + row * part_rows, part_rows), part_rows), :]
                for term in range(terms)
            ], axis=0)
            for h in range(2)
        ]
        out = (nn(pick[0], stack) + nn(pick[1], stack)).astype(BF16)
        for term in range(terms):
            for i in range(here):
                bw_ref[e, pl.ds(term * states + base, group), i * width : (i + 1) * width] = out[
                    term * part_rows + i * group : term * part_rows + (i + 1) * group, :
                ]
        return carry

    lax.fori_loop(0, (slots - 1) * (states // group), part_chunk, 0)

    def pass_on(t, m, k, index):
        for d in range(1, mates):
            go(
                coef_at(t, m, k), coef_at(t, m, k), csems.at[index + d - 1, k], cgets.at[index + d - 1, k],
                (sec, slot * mates + other_mate(d)),
            )

    far_start = len(near_peers) + 1
    for k in range(BITS):
        flying[k].wait_recv()
        for e in range(1, slots):
            go(
                coef_at(slot, mate, k), coef_at(slot, mate, k), csems.at[e, k], cgets.at[e, k],
                (sec, slot_row(other_slot(e))),
            )
        pass_on(slot, mate, k, slots)
        if k == 0:
            total_ref[far_start] = sum_totals(0, near_peers)
            add_totals(far_start, far_peers)
    number = slots - 1
    for e in range(1, slots):
        t = other_slot(slots - e)
        place = mrecv.at[t, m_rows(mate), :]
        remote(place, place, msems.at[e - 1], mgets.at[e - 1], (sec, slot_row(t))).wait_recv()
        for d in range(1, mates):
            go(place, place, msems.at[number], mgets.at[number], (sec, slot * mates + other_mate(d)))
            number += 1
    def from_mates(e):
        t = other_slot(slots - e)
        for k in range(BITS):
            for d in range(1, mates):
                index = slots + e * (mates - 1) + d - 1
                m = other_mate(mates - d)
                remote(
                    coef_at(t, m, k), coef_at(t, m, k), csems.at[index, k], cgets.at[index, k],
                    (sec, slot * mates + m),
                ).wait_recv()

    wide = [tn(msend[...], bw_ref[0])]
    from_mates(0)
    u_out[slot] = nn(own_ref[slot], crecv[slot])
    for k in range(BITS):
        for e in range(1, slots):
            t = other_slot(slots - e)
            remote(
                coef_at(t, mate, k), coef_at(t, mate, k), csems.at[e, k], cgets.at[e, k], (sec, slot_row(t))
            ).wait_recv()
            pass_on(t, mate, k, slots + e * (mates - 1))
    number = slots - 1
    for e in range(1, slots):
        t = other_slot(slots - e)
        for d in range(1, mates):
            m = other_mate(mates - d)
            place = mrecv.at[t, m_rows(m), :]
            remote(place, place, msems.at[number], mgets.at[number], (sec, slot * mates + m)).wait_recv()
            number += 1
        wide.append(tn(mrecv[t], bw_ref[slots - e]))
    scale = 1.0 / jnp.sqrt(jnp.sum(sum_totals(far_start, far_peers), keepdims=True))
    for d in range(slots):
        w_out[other_slot(slots - d)] = wide[d] * scale

    for e in range(1, slots):
        t = other_slot(slots - e)
        from_mates(e)
        u_out[t] = nn(own_ref[t], crecv[t])
    for copy in flying:
        copy.wait_send()


def solution(mesh):
    row_count, sec_count = mesh.shape["row"], mesh.shape["sec"]

    def on_device(left_block, right_block, left_ops, right_ops, charges, live_states, kept, start):
        slots, rows, states = left_block.shape
        terms, site = left_ops.shape[0], left_ops.shape[1]
        cols, bond, keep = right_block.shape[2], terms * states, start.shape[1]
        block, mates = 256, row_count // slots
        part_cols = cols // row_count
        coef_copies = slots + slots * (mates - 1)
        m_copies = (slots - 1) * mates
        near_count = low_part(sec_count)
        peers = slots * near_count + sec_count // near_count
        dma = pltpu.SemaphoreType.DMA
        u_shape, w_shape = (slots, rows, keep), (slots, keep, part_cols)
        return pl.pallas_call(
            functools.partial(gate_kernel, row_count, sec_count),
            out_shape=(pltpu.VMEM(u_shape, F32), pltpu.VMEM(w_shape, F32)),
            in_specs=[HBM] * 8,
            out_specs=[VM] * 2,
            scratch_shapes=[
                pltpu.VMEM(left_ops.shape, F32),
                pltpu.VMEM(right_ops.shape, F32),
                pltpu.SMEM(charges.shape, jnp.int32),
                pltpu.SMEM(live_states.shape, jnp.int32),
                pltpu.SMEM(kept.shape, jnp.int32),
                pltpu.VMEM(start.shape, jnp.int32),
                pltpu.VMEM((slots, rows, states), BF16),
                pltpu.VMEM((rows * row_count, states), BF16),
                pltpu.VMEM((slots, states, cols), BF16),
                pltpu.VMEM((2, block, terms * block), BF16),
                pltpu.VMEM((2, terms * block, block), BF16),
                pltpu.VMEM((bond, rows * row_count), BF16),
                pltpu.VMEM((slots, rows, bond), BF16),
                pltpu.VMEM((bond, cols), BF16),
                pltpu.VMEM((slots, bond, part_cols), BF16),
                pltpu.VMEM((bond, bond), F32),
                pltpu.VMEM((bond, bond), BF16),
                pltpu.VMEM((bond, bond), BF16),
                pltpu.VMEM((bond, bond), BF16),
                pltpu.VMEM((bond, bond), BF16),
                pltpu.VMEM((keep, keep), F32),
                pltpu.VMEM((keep, keep), F32),
                pltpu.VMEM((RING, 2, PANEL, keep), F32),
                pltpu.VMEM((bond, keep), F32),
                pltpu.VMEM((bond // mates, keep), BF16),
                pltpu.VMEM((slots, bond, keep), BF16),
                pltpu.VMEM((bond, keep), BF16),
                pltpu.VMEM((slots, bond, keep), BF16),
                pltpu.VMEM((peers, 1, keep), F32),
                dma((7 + slots,)),
                dma((slots, PIECES)), dma((slots, PIECES)),
                dma((mates - 1, slots, PIECES)), dma((mates - 1, slots, PIECES)),
                dma((coef_copies, BITS)), dma((coef_copies, BITS)),
                dma((m_copies,)), dma((m_copies,)),
                dma((peers,)), dma((peers,)),
            ],
            compiler_params=pltpu.CompilerParams(
                collective_id=0, has_side_effects=True, vmem_limit_bytes=62 * 2**20
            ),
        )(left_block, right_block, left_ops, right_ops, charges, live_states, kept, start)
    return jax.shard_map(
        on_device,
        mesh=mesh,
        in_specs=(P("sec", "row", None), P("sec", None, None), P(), P(), P(), P(), P(), P()),
        out_specs=(P("sec", "row", None), P("sec", None, "row")),
        check_vma=False,
    )
```

```python
import functools

import jax
import jax.numpy as jnp
from jax import lax
from jax.experimental import pallas as pl
from jax.experimental.pallas import tpu as pltpu
from jax.sharding import PartitionSpec as P

MESH = pl.DeviceIdType.MESH
HIGHEST = lax.Precision.HIGHEST
F32, BF16 = jnp.float32, jnp.bfloat16
chemical = 0.4
ITERS = 2
PANEL = 32
TILE = 8
RING = 4
PIECES = 4
BITS = 2
VM = pl.BlockSpec(memory_space=pltpu.VMEM)
SM = pl.BlockSpec(memory_space=pltpu.SMEM)
ANY = pl.BlockSpec(memory_space=pl.ANY)
HBM = pl.BlockSpec(memory_space=pltpu.HBM)


def nn(a, b, precision=None):
    return lax.dot_general(
        a, b, (((1,), (0,)), ((), ())), precision=precision, preferred_element_type=F32
    )


def nt(a, b, precision=None):
    return lax.dot_general(
        a, b, (((1,), (1,)), ((), ())), precision=precision, preferred_element_type=F32
    )


def tn(a, b, precision=None):
    return lax.dot_general(
        a, b, (((0,), (0,)), ((), ())), precision=precision, preferred_element_type=F32
    )


def split2(x):
    high = x.astype(BF16)
    return high, (x - high.astype(F32)).astype(BF16)


def split3(x):
    high, rest = x.astype(BF16), None
    rest = x - high.astype(F32)
    mid = rest.astype(BF16)
    return high, mid, (rest - mid.astype(F32)).astype(BF16)


def presplit_nn(parts, x):
    high, low = split2(x)
    both = nn(parts[0], jnp.concatenate([high, low], axis=1))
    width = x.shape[1]
    return both[:, :width] + both[:, width:] + nn(parts[1], high)


def nt3(a, b):
    ah, al = split2(a)
    bh, bl = split2(b)
    return nt(jnp.concatenate([ah, al, ah], axis=1), jnp.concatenate([bh, bh, bl], axis=1))


def tn3(a, b):
    ah, al = split2(a)
    bh, bl = split2(b)
    return tn(jnp.concatenate([ah, al, ah], axis=0), jnp.concatenate([bh, bh, bl], axis=0))


def iota(shape, dim):
    return lax.broadcasted_iota(jnp.int32, shape, dim)


def spread(ops, row_of, col_of, same):
    site = ops.shape[0]
    pick_rows = (iota((row_of.shape[0], site), 1) == row_of).astype(BF16)
    pick_cols = (iota((site, col_of.shape[1]), 0) == col_of).astype(BF16)
    out = []
    for part in split2(ops):
        wide = nn(nn(pick_rows, part).astype(BF16), pick_cols)
        out.append(jnp.where(same, wide, 0.0).astype(BF16))
    return out


def eliminate_panel(x, base, ring_ref):
    size = x.shape[1]
    tiles = PANEL // TILE
    sub, lane = iota((TILE, size), 0), iota((TILE, size), 1)
    inside = (lane >= base) & (lane < base + PANEL)
    cols = [
        {
            h: jnp.broadcast_to(x[h * TILE : (h + 1) * TILE, base + c : base + c + 1], (TILE, size))
            for h in range(c // TILE, tiles)
        }
        for c in range(PANEL)
    ]
    rows = [
        jnp.where(inside, (lane - (base + h * TILE) == sub).astype(F32), x[h * TILE : (h + 1) * TILE])
        for h in range(tiles)
    ]
    for j in range(0, PANEL, 2):
        own, q = j // TILE, j % TILE
        first, second = cols[j], cols[j + 1]
        a, b, d = first[own][q : q + 1], first[own][q + 1 : q + 2], second[own][q + 1 : q + 2]
        held = j // 2 % RING
        for h in range(own, tiles):
            ring_ref[held, 0, h * TILE : (h + 1) * TILE, :] = first[h]
            ring_ref[held, 1, h * TILE : (h + 1) * TILE, :] = second[h]
        root = lax.rsqrt(a * d - b * b)
        inverse = root * root
        aa, bb, dd = a * inverse, b * inverse, d * inverse
        w1 = {h: first[h] * dd - second[h] * bb for h in range(own, tiles)}
        w2 = {h: second[h] * aa - first[h] * bb for h in range(own, tiles)}
        for i in range(j + 2, PANEL):
            at, r = i // TILE, i % TILE
            if i < j + 4:
                s1, s2 = first[at][r : r + 1], second[at][r : r + 1]
            else:
                s1, s2 = [ring_ref[held, n, pl.ds(i, TILE, stride=0), :] for n in range(2)]
            cols[i] = {h: cols[i][h] - w1[h] * s1 - w2[h] * s2 for h in range(at, tiles)}
        scale = lax.rsqrt(a)
        x1, x2 = rows[own][q : q + 1], rows[own][q + 1 : q + 2]
        for h in range(own + 1, tiles):
            rows[h] = rows[h] - w1[h] * x1 - w2[h] * x2
        later = rows[own]
        if q + 2 < TILE:
            later = later - jnp.where(sub > q + 1, w1[own], 0.0) * x1 - jnp.where(sub > q + 1, w2[own], 0.0) * x2
        top = x1 * scale
        bottom = (x2 - x1 * (b * scale * scale)) * (a * scale * root)
        rows[own] = jnp.where(sub == q, top, jnp.where(sub == q + 1, bottom, later))
    return jnp.concatenate(rows, axis=0)


def inverse_factor(gram, s_ref, t_ref, ring_ref, beside=None):
    size = gram.shape[0]
    s_ref[...] = gram
    lane = iota((PANEL, size), 1)
    for base in range(0, size, PANEL):
        after = base + PANEL
        if beside is not None:
            beside(base // PANEL)
        x = eliminate_panel(s_ref[base:after, :], base, ring_ref)
        t_ref[base:after, :] = jnp.where(lane < after, x, 0.0)
        if after == size:
            break
        parts = split3(x)
        masked = [jnp.where(lane >= after, y.astype(F32), 0.0).astype(BF16) for y in parts]
        pairs = ((0, 0), (0, 1), (1, 0), (1, 1), (0, 2), (2, 0))
        change = tn(
            jnp.concatenate([masked[i] for i, _ in pairs], axis=0),
            jnp.concatenate([parts[k] for _, k in pairs], axis=0),
        )
        inside = (lane[0:1] >= base) & (lane[0:1] < after)
        s_ref[after:, :] = jnp.where(inside, 0.0, s_ref[after:, :]) - change[after:, :]


def low_part(count):
    bits = count.bit_length() - 1
    return 1 << (bits // 2)


def gate_kernel(
    row_count, sec_count, left_hbm, right_hbm, lops_hbm, rops_hbm, charges_hbm, live_hbm, kept_hbm,
    start_hbm, u_out, w_out, lops_ref, rops_ref, charges_ref, live_ref, kept_ref, start_ref,
    lown, lrecv, rown, kl_ref, kr_ref, at_ref, own_ref, b_ref, bw_ref, ga_ref, gah_ref, gal_ref,
    gbh_ref, gbl_ref, s_ref, t_ref, ring_ref, coef_ref, csend, crecv, msend, mrecv, total_ref,
    local, lsend, lget, fsend, fget, csems, cgets, msems, mgets, tsems, tgets,
):
    slots, rows, states = left_hbm.shape
    terms, site = lops_ref.shape[0], lops_ref.shape[1]
    cols = right_hbm.shape[2]
    width = cols // site
    group = 256 // site
    block = group * site
    bond = terms * states
    keep = start_ref.shape[1]
    sector_count = slots * sec_count
    mates = row_count // slots
    here = site // row_count
    piece = rows // PIECES
    half = sec_count // 2

    sec, row = lax.axis_index("sec"), lax.axis_index("row")
    slot, mate = row // mates, row % mates
    partner = jnp.bitwise_xor(sec, half)
    home = sec * slots + slot
    mirror = lax.rem(home + sector_count // 2, sector_count)

    def slot_row(t):
        return t * mates + mate

    def other_slot(d):
        return lax.rem(slot + d, slots)

    def other_mate(d):
        return lax.rem(mate + d, mates)

    greeted = [(sec, slot * mates + other_mate(d)) for d in range(1, mates)]
    near_count = low_part(sec_count)
    far_count = sec_count // near_count
    greeted += [
        (jnp.bitwise_xor(sec, d), slot_row(other_slot(e)))
        for d in range(near_count) for e in range(slots) if d or e
    ]
    greeted += [(jnp.bitwise_xor(sec, h * near_count), row) for h in range(1, far_count)]
    greeted += [(partner, slot_row(other_slot(e))) for e in range(1, slots)]
    barrier = pltpu.get_barrier_semaphore()
    for device in greeted:
        pl.semaphore_signal(barrier, inc=1, device_id=device, device_id_type=MESH)

    near = [
        pltpu.make_async_copy(source, target, local.at[i])
        for i, (source, target) in enumerate((
            (rops_hbm, rops_ref), (lops_hbm, lops_ref), (charges_hbm, charges_ref), (live_hbm, live_ref),
            (kept_hbm, kept_ref), (start_hbm, start_ref), (left_hbm, lown),
        ))
    ]
    near += [
        pltpu.make_async_copy(right_hbm.at[other_slot(e)], rown.at[e], local.at[len(near) + e])
        for e in range(slots)
    ]
    for copy in near:
        copy.start()
    near[0].wait()

    r0, c0 = iota((block, 1), 0), iota((1, block), 1)
    for t in range(terms):
        parts = spread(rops_ref[t], r0 // group, c0 // group, (r0 % group) == (c0 % group))
        for h in range(2):
            kr_ref[h, t * block : (t + 1) * block, :] = parts[h]

    pl.semaphore_wait(barrier, len(greeted))

    def remote(source, target, send, recv, device):
        return pltpu.make_async_remote_copy(
            src_ref=source, dst_ref=target, send_sem=send, recv_sem=recv,
            device_id=device, device_id_type=MESH,
        )

    def rows_at(owner, k):
        return pl.ds(pl.multiple_of(owner * rows + k * piece, piece), piece)

    sent = []
    for k in range(PIECES):
        for t in range(slots):
            copy = remote(
                left_hbm.at[t, pl.ds(k * piece, piece), :], lrecv.at[rows_at(row, k), :],
                lsend.at[t, k], lget.at[slot, k], (partner, slot_row(t)),
            )
            copy.start()
            sent.append(copy)

    for copy in near[1:]:
        copy.wait()
    for t in range(terms):
        parts = spread(lops_ref[t].T, r0 % site, c0 % site, (r0 // site) == (c0 // site))
        for h in range(2):
            kl_ref[h, :, t * block : (t + 1) * block] = parts[h]

    def right_chunk(c, carry):
        base = pl.multiple_of(c * group, group)
        part = rown[0, pl.ds(base, group), :]
        stack = jnp.concatenate([part[:, j * width : (j + 1) * width] for j in range(site)], axis=0)
        out = (nn(kr_ref[0], stack) + nn(kr_ref[1], stack)).astype(BF16)
        for t in range(terms):
            for i in range(site):
                b_ref[pl.ds(t * states + base, group), i * width : (i + 1) * width] = out[
                    t * block + i * group : t * block + (i + 1) * group, :
                ]
        return carry

    lax.fori_loop(0, states // group, right_chunk, 0)
    gbh_ref[...], gbl_ref[...] = split2(nt(b_ref[...], b_ref[...]))

    def gate_left(parts, firsts, limit, store):
        parts = [
            jnp.where(iota(part.shape, 0) + first < limit, part.astype(F32), 0.0)
            for part, first in zip(parts, firsts)
        ]
        turned = jnp.concatenate(parts, axis=0).T.astype(BF16)
        out = nn(turned, kl_ref[0]) + nn(turned, kl_ref[1])
        for t in range(terms):
            store(t, out[:, t * block : (t + 1) * block].astype(BF16))

    def own_chunk(c, carry):
        t = c // (rows // block)
        q = lax.rem(c, rows // block)
        first = pl.multiple_of(q * block, block)

        def store(term, value):
            own_ref[t, pl.ds(first, block), term * states : (term + 1) * states] = value.T

        owner = sec * slots + t
        gate_left(
            [lown[t, pl.ds(first, block), :]], [row * rows + first], live_ref[owner] * site, store
        )
        return carry

    lax.fori_loop(0, slots * (rows // block), own_chunk, 0)

    limit = live_ref[mirror] * site
    forwarded = []
    ready = block // piece
    span = row_count * piece
    def arrive(k):
        owners = []
        for t in range(slots):
            owner = slot_row(t)
            place = lrecv.at[rows_at(owner, k), :]
            remote(place, place, lsend.at[t, k], lget.at[t, k], (partner, owner)).wait_recv()
            for d in range(1, mates):
                copy = remote(
                    place, place, fsend.at[d - 1, t, k], fget.at[d - 1, t, k],
                    (sec, slot * mates + other_mate(d)),
                )
                copy.start()
                forwarded.append(copy)
            owners.append(owner)
        return owners

    def arrive_from_mates(k):
        owners = []
        for d in range(1, mates):
            for t in range(slots):
                owner = t * mates + other_mate(mates - d)
                place = lrecv.at[rows_at(owner, k), :]
                remote(
                    place, place, fsend.at[d - 1, t, k], fget.at[d - 1, t, k],
                    (sec, slot * mates + other_mate(mates - d)),
                ).wait_recv()
                owners.append(owner)
        return owners

    def gate_pieces(owners, k, column):
        for index in range(0, len(owners), ready):
            firsts = [owner * rows + k * piece for owner in owners[index : index + ready]]
            place = column + index * piece

            def store(t, value):
                at_ref[t * states : (t + 1) * states, place : place + block] = value

            gate_left(
                [lrecv[pl.ds(pl.multiple_of(first, piece), piece), :] for first in firsts],
                firsts, limit, store,
            )

    gram = None
    for k in range(PIECES + 1):
        if k < PIECES:
            gate_pieces(arrive(k), k, k * span)
        if k:
            gate_pieces(arrive_from_mates(k - 1), k - 1, (k - 1) * span + slots * piece)
            done = at_ref[:, (k - 1) * span : k * span]
            gram = nt(done, done) if gram is None else ga_ref[...] + nt(done, done)
            if k < PIECES:
                ga_ref[...] = gram
    gah_ref[...], gal_ref[...] = split2(gram)
    for copy in sent + forwarded:
        copy.wait_send()

    weight = jnp.exp(jnp.full((1, states), charges_ref[home], jnp.int32).astype(F32) * (-chemical))
    coef = (iota((bond, keep), 0) == start_ref[pl.ds(mirror, 1), :]).astype(F32)
    share = bond * PANEL // keep
    for round_index in range(ITERS + 1):
        image = presplit_nn((gah_ref[...], gal_ref[...]), coef)
        norm = lax.rsqrt(jnp.sum(coef * image, axis=0, keepdims=True))
        coef, image = coef * norm, image * norm

        def following(n):
            span = pl.ds(n * share, share)
            coef_ref[span, :] = presplit_nn((gbh_ref[span, :], gbl_ref[span, :]), image)

        last = round_index == ITERS
        inverse_factor(tn3(coef, image), s_ref, t_ref, ring_ref, None if last else following)
        if not last:
            coef = nt3(coef_ref[...], t_ref[...]) * (weight * weight)
    kept_here = iota((bond, keep), 1) < kept_ref[home]
    part = bond // mates
    bit = part // BITS

    def coef_rows(m, k):
        return pl.ds(pl.multiple_of(m * part + k * bit, bit), bit)

    def coef_at(t, m, k):
        return crecv.at[t, coef_rows(m, k), :]

    def m_rows(m):
        return pl.ds(pl.multiple_of(m * part, part), part)

    coef_ref[...] = coef
    kept_part = iota((part, keep), 1) < kept_ref[home]
    csend[...] = jnp.where(kept_part, nt3(coef_ref[m_rows(mate), :], t_ref[...]), 0.0).astype(BF16)

    flying = []

    def go(*args):
        copy = remote(*args)
        copy.start()
        flying.append(copy)

    for k in range(BITS):
        go(
            csend.at[pl.ds(k * bit, bit), :], coef_at(slot, mate, k), csems.at[0, k], cgets.at[0, k],
            (partner, row),
        )
    out = jnp.where(kept_here, nt3(image, t_ref[...]) * weight, 0.0)
    msend[...] = out.astype(BF16)
    per = out * presplit_nn((gbh_ref[...], gbl_ref[...]), out)
    total_ref[0] = jnp.sum(per, axis=0, keepdims=True)

    def add_totals(start, peers):
        for n, device in enumerate(peers):
            index = start + 1 + n
            go(total_ref.at[start], total_ref.at[index], tsems.at[index], tgets.at[index], device)

    def sum_totals(start, peers):
        summed = total_ref[start]
        for n, device in enumerate(peers):
            index = start + 1 + n
            remote(
                total_ref.at[start], total_ref.at[index], tsems.at[index], tgets.at[index], device
            ).wait_recv()
            summed = summed + total_ref[index]
        return summed

    near_peers = [
        (jnp.bitwise_xor(sec, d), slot_row(other_slot(e)))
        for d in range(near_count) for e in range(slots) if d or e
    ]
    far_peers = [(jnp.bitwise_xor(sec, h * near_count), row) for h in range(1, far_count)]
    add_totals(0, near_peers)
    for e in range(1, slots):
        go(
            msend.at[m_rows(mate), :], mrecv.at[slot, m_rows(mate), :], msems.at[e - 1], mgets.at[e - 1],
            (sec, slot_row(other_slot(e))),
        )

    part_rows = here * group
    part_cols = cols // row_count
    bw_ref[0] = b_ref[:, pl.ds(pl.multiple_of(row * part_cols, part_cols), part_cols)]

    def part_chunk(c, carry):
        e = 1 + c // (states // group)
        base = pl.multiple_of(lax.rem(c, states // group) * group, group)
        piece_rows = rown[e, pl.ds(base, group), :]
        stack = jnp.concatenate([piece_rows[:, j * width : (j + 1) * width] for j in range(site)], axis=0)
        pick = [
            jnp.concatenate([
                kr_ref[h, pl.ds(pl.multiple_of(term * block + row * part_rows, part_rows), part_rows), :]
                for term in range(terms)
            ], axis=0)
            for h in range(2)
        ]
        out = (nn(pick[0], stack) + nn(pick[1], stack)).astype(BF16)
        for term in range(terms):
            for i in range(here):
                bw_ref[e, pl.ds(term * states + base, group), i * width : (i + 1) * width] = out[
                    term * part_rows + i * group : term * part_rows + (i + 1) * group, :
                ]
        return carry

    lax.fori_loop(0, (slots - 1) * (states // group), part_chunk, 0)

    def pass_on(t, m, k, index):
        for d in range(1, mates):
            go(
                coef_at(t, m, k), coef_at(t, m, k), csems.at[index + d - 1, k], cgets.at[index + d - 1, k],
                (sec, slot * mates + other_mate(d)),
            )

    far_start = len(near_peers) + 1
    for k in range(BITS):
        flying[k].wait_recv()
        for e in range(1, slots):
            go(
                coef_at(slot, mate, k), coef_at(slot, mate, k), csems.at[e, k], cgets.at[e, k],
                (sec, slot_row(other_slot(e))),
            )
        pass_on(slot, mate, k, slots)
        if k == 0:
            total_ref[far_start] = sum_totals(0, near_peers)
            add_totals(far_start, far_peers)
    number = slots - 1
    for e in range(1, slots):
        t = other_slot(slots - e)
        place = mrecv.at[t, m_rows(mate), :]
        remote(place, place, msems.at[e - 1], mgets.at[e - 1], (sec, slot_row(t))).wait_recv()
        for d in range(1, mates):
            go(place, place, msems.at[number], mgets.at[number], (sec, slot * mates + other_mate(d)))
            number += 1
    def from_mates(e):
        t = other_slot(slots - e)
        for k in range(BITS):
            for d in range(1, mates):
                index = slots + e * (mates - 1) + d - 1
                m = other_mate(mates - d)
                remote(
                    coef_at(t, m, k), coef_at(t, m, k), csems.at[index, k], cgets.at[index, k],
                    (sec, slot * mates + m),
                ).wait_recv()

    wide = [tn(msend[...], bw_ref[0])]
    from_mates(0)
    u_out[slot] = nn(own_ref[slot], crecv[slot])
    number = slots - 1
    for e in range(1, slots):
        t = other_slot(slots - e)
        for d in range(1, mates):
            m = other_mate(mates - d)
            place = mrecv.at[t, m_rows(m), :]
            remote(place, place, msems.at[number], mgets.at[number], (sec, slot * mates + m)).wait_recv()
            number += 1
        wide.append(tn(mrecv[t], bw_ref[slots - e]))
    for k in range(BITS):
        for e in range(1, slots):
            t = other_slot(slots - e)
            remote(
                coef_at(t, mate, k), coef_at(t, mate, k), csems.at[e, k], cgets.at[e, k], (sec, slot_row(t))
            ).wait_recv()
            pass_on(t, mate, k, slots + e * (mates - 1))
    for e in range(1, slots):
        t = other_slot(slots - e)
        from_mates(e)
        u_out[t] = nn(own_ref[t], crecv[t])
    scale = 1.0 / jnp.sqrt(jnp.sum(sum_totals(far_start, far_peers), keepdims=True))
    for d in range(slots):
        w_out[other_slot(slots - d)] = wide[d] * scale

    for copy in flying:
        copy.wait_send()


def solution(mesh):
    row_count, sec_count = mesh.shape["row"], mesh.shape["sec"]

    def on_device(left_block, right_block, left_ops, right_ops, charges, live_states, kept, start):
        slots, rows, states = left_block.shape
        terms, site = left_ops.shape[0], left_ops.shape[1]
        cols, bond, keep = right_block.shape[2], terms * states, start.shape[1]
        block, mates = 256, row_count // slots
        part_cols = cols // row_count
        coef_copies = slots + slots * (mates - 1)
        m_copies = (slots - 1) * mates
        near_count = low_part(sec_count)
        peers = slots * near_count + sec_count // near_count
        dma = pltpu.SemaphoreType.DMA
        u_shape, w_shape = (slots, rows, keep), (slots, keep, part_cols)
        return pl.pallas_call(
            functools.partial(gate_kernel, row_count, sec_count),
            out_shape=(pltpu.VMEM(u_shape, F32), pltpu.VMEM(w_shape, F32)),
            in_specs=[HBM] * 8,
            out_specs=[VM] * 2,
            scratch_shapes=[
                pltpu.VMEM(left_ops.shape, F32),
                pltpu.VMEM(right_ops.shape, F32),
                pltpu.SMEM(charges.shape, jnp.int32),
                pltpu.SMEM(live_states.shape, jnp.int32),
                pltpu.SMEM(kept.shape, jnp.int32),
                pltpu.VMEM(start.shape, jnp.int32),
                pltpu.VMEM((slots, rows, states), BF16),
                pltpu.VMEM((rows * row_count, states), BF16),
                pltpu.VMEM((slots, states, cols), BF16),
                pltpu.VMEM((2, block, terms * block), BF16),
                pltpu.VMEM((2, terms * block, block), BF16),
                pltpu.VMEM((bond, rows * row_count), BF16),
                pltpu.VMEM((slots, rows, bond), BF16),
                pltpu.VMEM((bond, cols), BF16),
                pltpu.VMEM((slots, bond, part_cols), BF16),
                pltpu.VMEM((bond, bond), F32),
                pltpu.VMEM((bond, bond), BF16),
                pltpu.VMEM((bond, bond), BF16),
                pltpu.VMEM((bond, bond), BF16),
                pltpu.VMEM((bond, bond), BF16),
                pltpu.VMEM((keep, keep), F32),
                pltpu.VMEM((keep, keep), F32),
                pltpu.VMEM((RING, 2, PANEL, keep), F32),
                pltpu.VMEM((bond, keep), F32),
                pltpu.VMEM((bond // mates, keep), BF16),
                pltpu.VMEM((slots, bond, keep), BF16),
                pltpu.VMEM((bond, keep), BF16),
                pltpu.VMEM((slots, bond, keep), BF16),
                pltpu.VMEM((peers, 1, keep), F32),
                dma((7 + slots,)),
                dma((slots, PIECES)), dma((slots, PIECES)),
                dma((mates - 1, slots, PIECES)), dma((mates - 1, slots, PIECES)),
                dma((coef_copies, BITS)), dma((coef_copies, BITS)),
                dma((m_copies,)), dma((m_copies,)),
                dma((peers,)), dma((peers,)),
            ],
            compiler_params=pltpu.CompilerParams(
                collective_id=0, has_side_effects=True, vmem_limit_bytes=62 * 2**20
            ),
        )(left_block, right_block, left_ops, right_ops, charges, live_states, kept, start)
    return jax.shard_map(
        on_device,
        mesh=mesh,
        in_specs=(P("sec", "row", None), P("sec", None, None), P(), P(), P(), P(), P(), P()),
        out_specs=(P("sec", "row", None), P("sec", None, "row")),
        check_vma=False,
    )
```

```python
import functools

import jax
import jax.numpy as jnp
from jax import lax
from jax.experimental import pallas as pl
from jax.experimental.pallas import tpu as pltpu
from jax.sharding import PartitionSpec as P

MESH = pl.DeviceIdType.MESH
HIGHEST = lax.Precision.HIGHEST
F32, BF16 = jnp.float32, jnp.bfloat16
chemical = 0.4
ITERS = 2
PANEL = 32
TILE = 8
RING = 4
PIECES = 4
BITS = 2
VM = pl.BlockSpec(memory_space=pltpu.VMEM)
SM = pl.BlockSpec(memory_space=pltpu.SMEM)
ANY = pl.BlockSpec(memory_space=pl.ANY)
HBM = pl.BlockSpec(memory_space=pltpu.HBM)


def nn(a, b, precision=None):
    return lax.dot_general(
        a, b, (((1,), (0,)), ((), ())), precision=precision, preferred_element_type=F32
    )


def nt(a, b, precision=None):
    return lax.dot_general(
        a, b, (((1,), (1,)), ((), ())), precision=precision, preferred_element_type=F32
    )


def tn(a, b, precision=None):
    return lax.dot_general(
        a, b, (((0,), (0,)), ((), ())), precision=precision, preferred_element_type=F32
    )


def split2(x):
    high = x.astype(BF16)
    return high, (x - high.astype(F32)).astype(BF16)


def split3(x):
    high, rest = x.astype(BF16), None
    rest = x - high.astype(F32)
    mid = rest.astype(BF16)
    return high, mid, (rest - mid.astype(F32)).astype(BF16)


def presplit_nn(parts, x):
    high, low = split2(x)
    both = nn(parts[0], jnp.concatenate([high, low], axis=1))
    width = x.shape[1]
    return both[:, :width] + both[:, width:] + nn(parts[1], high)


def nt3(a, b):
    ah, al = split2(a)
    bh, bl = split2(b)
    return nt(jnp.concatenate([ah, al, ah], axis=1), jnp.concatenate([bh, bh, bl], axis=1))


def tn3(a, b):
    ah, al = split2(a)
    bh, bl = split2(b)
    return tn(jnp.concatenate([ah, al, ah], axis=0), jnp.concatenate([bh, bh, bl], axis=0))


def iota(shape, dim):
    return lax.broadcasted_iota(jnp.int32, shape, dim)


def spread(ops, row_of, col_of, same):
    site = ops.shape[0]
    pick_rows = (iota((row_of.shape[0], site), 1) == row_of).astype(BF16)
    pick_cols = (iota((site, col_of.shape[1]), 0) == col_of).astype(BF16)
    out = []
    for part in split2(ops):
        wide = nn(nn(pick_rows, part).astype(BF16), pick_cols)
        out.append(jnp.where(same, wide, 0.0).astype(BF16))
    return out


def eliminate_panel(x, base, ring_ref):
    size = x.shape[1]
    tiles = PANEL // TILE
    sub, lane = iota((TILE, size), 0), iota((TILE, size), 1)
    inside = (lane >= base) & (lane < base + PANEL)
    cols = [
        {
            h: jnp.broadcast_to(x[h * TILE : (h + 1) * TILE, base + c : base + c + 1], (TILE, size))
            for h in range(c // TILE, tiles)
        }
        for c in range(PANEL)
    ]
    rows = [
        jnp.where(inside, (lane - (base + h * TILE) == sub).astype(F32), x[h * TILE : (h + 1) * TILE])
        for h in range(tiles)
    ]
    for j in range(0, PANEL, 2):
        own, q = j // TILE, j % TILE
        first, second = cols[j], cols[j + 1]
        a, b, d = first[own][q : q + 1], first[own][q + 1 : q + 2], second[own][q + 1 : q + 2]
        held = j // 2 % RING
        for h in range(own, tiles):
            ring_ref[held, 0, h * TILE : (h + 1) * TILE, :] = first[h]
            ring_ref[held, 1, h * TILE : (h + 1) * TILE, :] = second[h]
        root = lax.rsqrt(a * d - b * b)
        inverse = root * root
        aa, bb, dd = a * inverse, b * inverse, d * inverse
        w1 = {h: first[h] * dd - second[h] * bb for h in range(own, tiles)}
        w2 = {h: second[h] * aa - first[h] * bb for h in range(own, tiles)}
        for i in range(j + 2, PANEL):
            at, r = i // TILE, i % TILE
            if i < j + 4:
                s1, s2 = first[at][r : r + 1], second[at][r : r + 1]
            else:
                s1, s2 = [ring_ref[held, n, pl.ds(i, TILE, stride=0), :] for n in range(2)]
            cols[i] = {h: cols[i][h] - w1[h] * s1 - w2[h] * s2 for h in range(at, tiles)}
        scale = lax.rsqrt(a)
        x1, x2 = rows[own][q : q + 1], rows[own][q + 1 : q + 2]
        for h in range(own + 1, tiles):
            rows[h] = rows[h] - w1[h] * x1 - w2[h] * x2
        later = rows[own]
        if q + 2 < TILE:
            later = later - jnp.where(sub > q + 1, w1[own], 0.0) * x1 - jnp.where(sub > q + 1, w2[own], 0.0) * x2
        top = x1 * scale
        bottom = (x2 - x1 * (b * scale * scale)) * (a * scale * root)
        rows[own] = jnp.where(sub == q, top, jnp.where(sub == q + 1, bottom, later))
    return jnp.concatenate(rows, axis=0)


def inverse_factor(gram, s_ref, t_ref, ring_ref, beside=None):
    size = gram.shape[0]
    s_ref[...] = gram
    lane = iota((PANEL, size), 1)
    for base in range(0, size, PANEL):
        after = base + PANEL
        if beside is not None:
            beside(base // PANEL)
        x = eliminate_panel(s_ref[base:after, :], base, ring_ref)
        t_ref[base:after, :] = jnp.where(lane < after, x, 0.0)
        if after == size:
            break
        parts = split3(x)
        masked = [jnp.where(lane >= after, y.astype(F32), 0.0).astype(BF16) for y in parts]
        pairs = ((0, 0), (0, 1), (1, 0), (1, 1), (0, 2), (2, 0))
        change = tn(
            jnp.concatenate([masked[i] for i, _ in pairs], axis=0),
            jnp.concatenate([parts[k] for _, k in pairs], axis=0),
        )
        inside = (lane[0:1] >= base) & (lane[0:1] < after)
        s_ref[after:, :] = jnp.where(inside, 0.0, s_ref[after:, :]) - change[after:, :]


def low_part(count):
    bits = count.bit_length() - 1
    return 1 << (bits // 2)


def gate_kernel(
    row_count, sec_count, left_hbm, right_hbm, lops_hbm, rops_hbm, charges_hbm, live_hbm, kept_hbm,
    start_hbm, u_out, w_out, lops_ref, rops_ref, charges_ref, live_ref, kept_ref, start_ref,
    lown, lrecv, rown, kl_ref, kr_ref, at_ref, own_ref, b_ref, bw_ref, ga_ref, gah_ref, gal_ref,
    gbh_ref, gbl_ref, s_ref, t_ref, ring_ref, coef_ref, csend, crecv, msend, mrecv, total_ref,
    local, lsend, lget, fsend, fget, csems, cgets, msems, mgets, tsems, tgets,
):
    slots, rows, states = left_hbm.shape
    terms, site = lops_ref.shape[0], lops_ref.shape[1]
    cols = right_hbm.shape[2]
    width = cols // site
    group = 256 // site
    block = group * site
    bond = terms * states
    keep = start_ref.shape[1]
    sector_count = slots * sec_count
    mates = row_count // slots
    here = site // row_count
    piece = rows // PIECES
    half = sec_count // 2

    sec, row = lax.axis_index("sec"), lax.axis_index("row")
    slot, mate = row // mates, row % mates
    partner = jnp.bitwise_xor(sec, half)
    home = sec * slots + slot
    mirror = lax.rem(home + sector_count // 2, sector_count)

    def slot_row(t):
        return t * mates + mate

    def other_slot(d):
        return lax.rem(slot + d, slots)

    def other_mate(d):
        return lax.rem(mate + d, mates)

    greeted = [(sec, slot * mates + other_mate(d)) for d in range(1, mates)]
    near_count = low_part(sec_count)
    far_count = sec_count // near_count
    greeted += [
        (jnp.bitwise_xor(sec, d), slot_row(other_slot(e)))
        for d in range(near_count) for e in range(slots) if d or e
    ]
    greeted += [(jnp.bitwise_xor(sec, h * near_count), row) for h in range(1, far_count)]
    greeted += [(partner, slot_row(other_slot(e))) for e in range(1, slots)]
    barrier = pltpu.get_barrier_semaphore()
    for device in greeted:
        pl.semaphore_signal(barrier, inc=1, device_id=device, device_id_type=MESH)

    near = [
        pltpu.make_async_copy(source, target, local.at[i])
        for i, (source, target) in enumerate((
            (rops_hbm, rops_ref), (lops_hbm, lops_ref), (charges_hbm, charges_ref), (live_hbm, live_ref),
            (kept_hbm, kept_ref), (start_hbm, start_ref), (left_hbm, lown),
        ))
    ]
    near += [
        pltpu.make_async_copy(right_hbm.at[other_slot(e)], rown.at[e], local.at[len(near) + e])
        for e in range(slots)
    ]
    for copy in near:
        copy.start()
    near[0].wait()

    r0, c0 = iota((block, 1), 0), iota((1, block), 1)
    for t in range(terms):
        parts = spread(rops_ref[t], r0 // group, c0 // group, (r0 % group) == (c0 % group))
        for h in range(2):
            kr_ref[h, t * block : (t + 1) * block, :] = parts[h]

    pl.semaphore_wait(barrier, len(greeted))

    def remote(source, target, send, recv, device):
        return pltpu.make_async_remote_copy(
            src_ref=source, dst_ref=target, send_sem=send, recv_sem=recv,
            device_id=device, device_id_type=MESH,
        )

    def rows_at(owner, k):
        return pl.ds(pl.multiple_of(owner * rows + k * piece, piece), piece)

    sent = []
    for k in range(PIECES):
        for t in range(slots):
            copy = remote(
                left_hbm.at[t, pl.ds(k * piece, piece), :], lrecv.at[rows_at(row, k), :],
                lsend.at[t, k], lget.at[slot, k], (partner, slot_row(t)),
            )
            copy.start()
            sent.append(copy)

    for copy in near[1:]:
        copy.wait()
    for t in range(terms):
        parts = spread(lops_ref[t].T, r0 % site, c0 % site, (r0 // site) == (c0 // site))
        for h in range(2):
            kl_ref[h, :, t * block : (t + 1) * block] = parts[h]

    def right_chunk(c, carry):
        base = pl.multiple_of(c * group, group)
        part = rown[0, pl.ds(base, group), :]
        stack = jnp.concatenate([part[:, j * width : (j + 1) * width] for j in range(site)], axis=0)
        out = (nn(kr_ref[0], stack) + nn(kr_ref[1], stack)).astype(BF16)
        for t in range(terms):
            for i in range(site):
                b_ref[pl.ds(t * states + base, group), i * width : (i + 1) * width] = out[
                    t * block + i * group : t * block + (i + 1) * group, :
                ]
        return carry

    lax.fori_loop(0, states // group, right_chunk, 0)
    gbh_ref[...], gbl_ref[...] = split2(nt(b_ref[...], b_ref[...]))

    def gate_left(blocks, limit, store):
        turned = jnp.concatenate([
            jnp.concatenate([
                jnp.where(iota(part.shape, 0) + first < limit, part.astype(F32), 0.0)
                for part, first in parts
            ], axis=0).T.astype(BF16)
            for parts in blocks
        ], axis=0)
        out = nn(turned, kl_ref[0]) + nn(turned, kl_ref[1])
        for n in range(len(blocks)):
            for t in range(terms):
                store(n, t, out[n * states : (n + 1) * states, t * block : (t + 1) * block].astype(BF16))

    def own_slot(t, carry):
        def store(n, term, value):
            own_ref[t, n * block : (n + 1) * block, term * states : (term + 1) * states] = value.T

        gate_left(
            [
                [(lown[t, first : first + block, :], row * rows + first)]
                for first in range(0, rows, block)
            ],
            live_ref[sec * slots + t] * site, store,
        )
        return carry

    lax.fori_loop(0, slots, own_slot, 0)

    limit = live_ref[mirror] * site
    forwarded = []
    ready = block // piece
    span = row_count * piece
    def arrive(k):
        owners = []
        for t in range(slots):
            owner = slot_row(t)
            place = lrecv.at[rows_at(owner, k), :]
            remote(place, place, lsend.at[t, k], lget.at[t, k], (partner, owner)).wait_recv()
            for d in range(1, mates):
                copy = remote(
                    place, place, fsend.at[d - 1, t, k], fget.at[d - 1, t, k],
                    (sec, slot * mates + other_mate(d)),
                )
                copy.start()
                forwarded.append(copy)
            owners.append(owner)
        return owners

    def arrive_from_mates(k):
        owners = []
        for d in range(1, mates):
            for t in range(slots):
                owner = t * mates + other_mate(mates - d)
                place = lrecv.at[rows_at(owner, k), :]
                remote(
                    place, place, fsend.at[d - 1, t, k], fget.at[d - 1, t, k],
                    (sec, slot * mates + other_mate(mates - d)),
                ).wait_recv()
                owners.append(owner)
        return owners

    def blocks_of(owners, k):
        firsts = [owner * rows + k * piece for owner in owners]
        parts = [(lrecv[pl.ds(pl.multiple_of(first, piece), piece), :], first) for first in firsts]
        return [parts[index : index + ready] for index in range(0, len(parts), ready)]

    gram = None
    for k in range(PIECES + 1):
        blocks, places = [], []
        if k < PIECES:
            blocks = blocks_of(arrive(k), k)
            places = [k * span + n * block for n in range(len(blocks))]
        if k:
            late = blocks_of(arrive_from_mates(k - 1), k - 1)
            blocks = blocks + late
            places += [(k - 1) * span + slots * piece + n * block for n in range(len(late))]

        def store(n, t, value):
            at_ref[t * states : (t + 1) * states, places[n] : places[n] + block] = value

        gate_left(blocks, limit, store)
        if k:
            done = at_ref[:, (k - 1) * span : k * span]
            gram = nt(done, done) if gram is None else ga_ref[...] + nt(done, done)
            if k < PIECES:
                ga_ref[...] = gram
    gah_ref[...], gal_ref[...] = split2(gram)
    for copy in sent + forwarded:
        copy.wait_send()

    weight = jnp.exp(jnp.full((1, states), charges_ref[home], jnp.int32).astype(F32) * (-chemical))
    coef = (iota((bond, keep), 0) == start_ref[pl.ds(mirror, 1), :]).astype(F32)
    share = bond * PANEL // keep
    for round_index in range(ITERS + 1):
        image = presplit_nn((gah_ref[...], gal_ref[...]), coef)
        norm = lax.rsqrt(jnp.sum(coef * image, axis=0, keepdims=True))
        coef, image = coef * norm, image * norm

        def following(n):
            span = pl.ds(n * share, share)
            coef_ref[span, :] = presplit_nn((gbh_ref[span, :], gbl_ref[span, :]), image)

        last = round_index == ITERS
        inverse_factor(tn3(coef, image), s_ref, t_ref, ring_ref, None if last else following)
        if not last:
            coef = nt3(coef_ref[...], t_ref[...]) * (weight * weight)
    kept_here = iota((bond, keep), 1) < kept_ref[home]
    part = bond // mates
    bit = part // BITS

    def coef_rows(m, k):
        return pl.ds(pl.multiple_of(m * part + k * bit, bit), bit)

    def coef_at(t, m, k):
        return crecv.at[t, coef_rows(m, k), :]

    def m_rows(m):
        return pl.ds(pl.multiple_of(m * part, part), part)

    coef_ref[...] = coef
    kept_part = iota((part, keep), 1) < kept_ref[home]
    csend[...] = jnp.where(kept_part, nt3(coef_ref[m_rows(mate), :], t_ref[...]), 0.0).astype(BF16)

    flying = []

    def go(*args):
        copy = remote(*args)
        copy.start()
        flying.append(copy)

    for k in range(BITS):
        go(
            csend.at[pl.ds(k * bit, bit), :], coef_at(slot, mate, k), csems.at[0, k], cgets.at[0, k],
            (partner, row),
        )
    out = jnp.where(kept_here, nt3(image, t_ref[...]) * weight, 0.0)
    msend[...] = out.astype(BF16)
    per = out * presplit_nn((gbh_ref[...], gbl_ref[...]), out)
    total_ref[0] = jnp.sum(per, axis=0, keepdims=True)

    def add_totals(start, peers):
        for n, device in enumerate(peers):
            index = start + 1 + n
            go(total_ref.at[start], total_ref.at[index], tsems.at[index], tgets.at[index], device)

    def sum_totals(start, peers):
        summed = total_ref[start]
        for n, device in enumerate(peers):
            index = start + 1 + n
            remote(
                total_ref.at[start], total_ref.at[index], tsems.at[index], tgets.at[index], device
            ).wait_recv()
            summed = summed + total_ref[index]
        return summed

    near_peers = [
        (jnp.bitwise_xor(sec, d), slot_row(other_slot(e)))
        for d in range(near_count) for e in range(slots) if d or e
    ]
    far_peers = [(jnp.bitwise_xor(sec, h * near_count), row) for h in range(1, far_count)]
    add_totals(0, near_peers)
    for e in range(1, slots):
        go(
            msend.at[m_rows(mate), :], mrecv.at[slot, m_rows(mate), :], msems.at[e - 1], mgets.at[e - 1],
            (sec, slot_row(other_slot(e))),
        )

    part_rows = here * group
    part_cols = cols // row_count
    bw_ref[0] = b_ref[:, pl.ds(pl.multiple_of(row * part_cols, part_cols), part_cols)]

    def part_chunk(c, carry):
        e = 1 + c // (states // group)
        base = pl.multiple_of(lax.rem(c, states // group) * group, group)
        piece_rows = rown[e, pl.ds(base, group), :]
        stack = jnp.concatenate([piece_rows[:, j * width : (j + 1) * width] for j in range(site)], axis=0)
        pick = [
            jnp.concatenate([
                kr_ref[h, pl.ds(pl.multiple_of(term * block + row * part_rows, part_rows), part_rows), :]
                for term in range(terms)
            ], axis=0)
            for h in range(2)
        ]
        out = (nn(pick[0], stack) + nn(pick[1], stack)).astype(BF16)
        for term in range(terms):
            for i in range(here):
                bw_ref[e, pl.ds(term * states + base, group), i * width : (i + 1) * width] = out[
                    term * part_rows + i * group : term * part_rows + (i + 1) * group, :
                ]
        return carry

    lax.fori_loop(0, (slots - 1) * (states // group), part_chunk, 0)

    def pass_on(t, m, k, index):
        for d in range(1, mates):
            go(
                coef_at(t, m, k), coef_at(t, m, k), csems.at[index + d - 1, k], cgets.at[index + d - 1, k],
                (sec, slot * mates + other_mate(d)),
            )

    far_start = len(near_peers) + 1
    for k in range(BITS):
        flying[k].wait_recv()
        for e in range(1, slots):
            go(
                coef_at(slot, mate, k), coef_at(slot, mate, k), csems.at[e, k], cgets.at[e, k],
                (sec, slot_row(other_slot(e))),
            )
        pass_on(slot, mate, k, slots)
        if k == 0:
            total_ref[far_start] = sum_totals(0, near_peers)
            add_totals(far_start, far_peers)
    number = slots - 1
    for e in range(1, slots):
        t = other_slot(slots - e)
        place = mrecv.at[t, m_rows(mate), :]
        remote(place, place, msems.at[e - 1], mgets.at[e - 1], (sec, slot_row(t))).wait_recv()
        for d in range(1, mates):
            go(place, place, msems.at[number], mgets.at[number], (sec, slot * mates + other_mate(d)))
            number += 1
    def from_mates(e):
        t = other_slot(slots - e)
        for k in range(BITS):
            for d in range(1, mates):
                index = slots + e * (mates - 1) + d - 1
                m = other_mate(mates - d)
                remote(
                    coef_at(t, m, k), coef_at(t, m, k), csems.at[index, k], cgets.at[index, k],
                    (sec, slot * mates + m),
                ).wait_recv()

    wide = [tn(msend[...], bw_ref[0])]
    from_mates(0)
    u_out[slot] = nn(own_ref[slot], crecv[slot])
    number = slots - 1
    for e in range(1, slots):
        t = other_slot(slots - e)
        for d in range(1, mates):
            m = other_mate(mates - d)
            place = mrecv.at[t, m_rows(m), :]
            remote(place, place, msems.at[number], mgets.at[number], (sec, slot * mates + m)).wait_recv()
            number += 1
        wide.append(tn(mrecv[t], bw_ref[slots - e]))
    for k in range(BITS):
        for e in range(1, slots):
            t = other_slot(slots - e)
            remote(
                coef_at(t, mate, k), coef_at(t, mate, k), csems.at[e, k], cgets.at[e, k], (sec, slot_row(t))
            ).wait_recv()
            pass_on(t, mate, k, slots + e * (mates - 1))
    for e in range(1, slots):
        t = other_slot(slots - e)
        from_mates(e)
        u_out[t] = nn(own_ref[t], crecv[t])
    scale = 1.0 / jnp.sqrt(jnp.sum(sum_totals(far_start, far_peers), keepdims=True))
    for d in range(slots):
        w_out[other_slot(slots - d)] = wide[d] * scale

    for copy in flying:
        copy.wait_send()


def solution(mesh):
    row_count, sec_count = mesh.shape["row"], mesh.shape["sec"]

    def on_device(left_block, right_block, left_ops, right_ops, charges, live_states, kept, start):
        slots, rows, states = left_block.shape
        terms, site = left_ops.shape[0], left_ops.shape[1]
        cols, bond, keep = right_block.shape[2], terms * states, start.shape[1]
        block, mates = 256, row_count // slots
        part_cols = cols // row_count
        coef_copies = slots + slots * (mates - 1)
        m_copies = (slots - 1) * mates
        near_count = low_part(sec_count)
        peers = slots * near_count + sec_count // near_count
        dma = pltpu.SemaphoreType.DMA
        u_shape, w_shape = (slots, rows, keep), (slots, keep, part_cols)
        return pl.pallas_call(
            functools.partial(gate_kernel, row_count, sec_count),
            out_shape=(pltpu.VMEM(u_shape, F32), pltpu.VMEM(w_shape, F32)),
            in_specs=[HBM] * 8,
            out_specs=[VM] * 2,
            scratch_shapes=[
                pltpu.VMEM(left_ops.shape, F32),
                pltpu.VMEM(right_ops.shape, F32),
                pltpu.SMEM(charges.shape, jnp.int32),
                pltpu.SMEM(live_states.shape, jnp.int32),
                pltpu.SMEM(kept.shape, jnp.int32),
                pltpu.VMEM(start.shape, jnp.int32),
                pltpu.VMEM((slots, rows, states), BF16),
                pltpu.VMEM((rows * row_count, states), BF16),
                pltpu.VMEM((slots, states, cols), BF16),
                pltpu.VMEM((2, block, terms * block), BF16),
                pltpu.VMEM((2, terms * block, block), BF16),
                pltpu.VMEM((bond, rows * row_count), BF16),
                pltpu.VMEM((slots, rows, bond), BF16),
                pltpu.VMEM((bond, cols), BF16),
                pltpu.VMEM((slots, bond, part_cols), BF16),
                pltpu.VMEM((bond, bond), F32),
                pltpu.VMEM((bond, bond), BF16),
                pltpu.VMEM((bond, bond), BF16),
                pltpu.VMEM((bond, bond), BF16),
                pltpu.VMEM((bond, bond), BF16),
                pltpu.VMEM((keep, keep), F32),
                pltpu.VMEM((keep, keep), F32),
                pltpu.VMEM((RING, 2, PANEL, keep), F32),
                pltpu.VMEM((bond, keep), F32),
                pltpu.VMEM((bond // mates, keep), BF16),
                pltpu.VMEM((slots, bond, keep), BF16),
                pltpu.VMEM((bond, keep), BF16),
                pltpu.VMEM((slots, bond, keep), BF16),
                pltpu.VMEM((peers, 1, keep), F32),
                dma((7 + slots,)),
                dma((slots, PIECES)), dma((slots, PIECES)),
                dma((mates - 1, slots, PIECES)), dma((mates - 1, slots, PIECES)),
                dma((coef_copies, BITS)), dma((coef_copies, BITS)),
                dma((m_copies,)), dma((m_copies,)),
                dma((peers,)), dma((peers,)),
            ],
            compiler_params=pltpu.CompilerParams(
                collective_id=0, has_side_effects=True, vmem_limit_bytes=62 * 2**20
            ),
        )(left_block, right_block, left_ops, right_ops, charges, live_states, kept, start)
    return jax.shard_map(
        on_device,
        mesh=mesh,
        in_specs=(P("sec", "row", None), P("sec", None, None), P(), P(), P(), P(), P(), P()),
        out_specs=(P("sec", "row", None), P("sec", None, "row")),
        check_vma=False,
    )
```

```python
import functools

import jax
import jax.numpy as jnp
from jax import lax
from jax.experimental import pallas as pl
from jax.experimental.pallas import tpu as pltpu
from jax.sharding import PartitionSpec as P

MESH = pl.DeviceIdType.MESH
HIGHEST = lax.Precision.HIGHEST
F32, BF16 = jnp.float32, jnp.bfloat16
chemical = 0.4
ITERS = 2
PANEL = 32
TILE = 8
RING = 4
PIECES = 4
BITS = 2
VM = pl.BlockSpec(memory_space=pltpu.VMEM)
SM = pl.BlockSpec(memory_space=pltpu.SMEM)
ANY = pl.BlockSpec(memory_space=pl.ANY)
HBM = pl.BlockSpec(memory_space=pltpu.HBM)


def nn(a, b, precision=None):
    return lax.dot_general(
        a, b, (((1,), (0,)), ((), ())), precision=precision, preferred_element_type=F32
    )


def nt(a, b, precision=None):
    return lax.dot_general(
        a, b, (((1,), (1,)), ((), ())), precision=precision, preferred_element_type=F32
    )


def tn(a, b, precision=None):
    return lax.dot_general(
        a, b, (((0,), (0,)), ((), ())), precision=precision, preferred_element_type=F32
    )


def split2(x):
    high = x.astype(BF16)
    return high, (x - high.astype(F32)).astype(BF16)


def split3(x):
    high, rest = x.astype(BF16), None
    rest = x - high.astype(F32)
    mid = rest.astype(BF16)
    return high, mid, (rest - mid.astype(F32)).astype(BF16)


def presplit_nn(parts, x):
    high, low = split2(x)
    both = nn(parts[0], jnp.concatenate([high, low], axis=1))
    width = x.shape[1]
    return both[:, :width] + both[:, width:] + nn(parts[1], high)


def nt3(a, b):
    ah, al = split2(a)
    bh, bl = split2(b)
    return nt(jnp.concatenate([ah, al, ah], axis=1), jnp.concatenate([bh, bh, bl], axis=1))


def tn3(a, b):
    ah, al = split2(a)
    bh, bl = split2(b)
    return tn(jnp.concatenate([ah, al, ah], axis=0), jnp.concatenate([bh, bh, bl], axis=0))


def iota(shape, dim):
    return lax.broadcasted_iota(jnp.int32, shape, dim)


def spread(ops, row_of, col_of, same):
    site = ops.shape[0]
    pick_rows = (iota((row_of.shape[0], site), 1) == row_of).astype(BF16)
    pick_cols = (iota((site, col_of.shape[1]), 0) == col_of).astype(BF16)
    out = []
    for part in split2(ops):
        wide = nn(nn(pick_rows, part).astype(BF16), pick_cols)
        out.append(jnp.where(same, wide, 0.0).astype(BF16))
    return out


def eliminate_panel(x, base, ring_ref):
    size = x.shape[1]
    tiles = PANEL // TILE
    sub, lane = iota((TILE, size), 0), iota((TILE, size), 1)
    inside = (lane >= base) & (lane < base + PANEL)
    cols = [
        {
            h: jnp.broadcast_to(x[h * TILE : (h + 1) * TILE, base + c : base + c + 1], (TILE, size))
            for h in range(c // TILE, tiles)
        }
        for c in range(PANEL)
    ]
    rows = [
        jnp.where(inside, (lane - (base + h * TILE) == sub).astype(F32), x[h * TILE : (h + 1) * TILE])
        for h in range(tiles)
    ]
    for j in range(0, PANEL, 2):
        own, q = j // TILE, j % TILE
        first, second = cols[j], cols[j + 1]
        a, b, d = first[own][q : q + 1], first[own][q + 1 : q + 2], second[own][q + 1 : q + 2]
        held = j // 2 % RING
        for h in range(own, tiles):
            ring_ref[held, 0, h * TILE : (h + 1) * TILE, :] = first[h]
            ring_ref[held, 1, h * TILE : (h + 1) * TILE, :] = second[h]
        root = lax.rsqrt(a * d - b * b)
        inverse = root * root
        aa, bb, dd = a * inverse, b * inverse, d * inverse
        w1 = {h: first[h] * dd - second[h] * bb for h in range(own, tiles)}
        w2 = {h: second[h] * aa - first[h] * bb for h in range(own, tiles)}
        for i in range(j + 2, PANEL):
            at, r = i // TILE, i % TILE
            if i < j + 4:
                s1, s2 = first[at][r : r + 1], second[at][r : r + 1]
            else:
                s1, s2 = [ring_ref[held, n, pl.ds(i, TILE, stride=0), :] for n in range(2)]
            cols[i] = {h: cols[i][h] - w1[h] * s1 - w2[h] * s2 for h in range(at, tiles)}
        scale = lax.rsqrt(a)
        x1, x2 = rows[own][q : q + 1], rows[own][q + 1 : q + 2]
        for h in range(own + 1, tiles):
            rows[h] = rows[h] - w1[h] * x1 - w2[h] * x2
        later = rows[own]
        if q + 2 < TILE:
            later = later - jnp.where(sub > q + 1, w1[own], 0.0) * x1 - jnp.where(sub > q + 1, w2[own], 0.0) * x2
        top = x1 * scale
        bottom = (x2 - x1 * (b * scale * scale)) * (a * scale * root)
        rows[own] = jnp.where(sub == q, top, jnp.where(sub == q + 1, bottom, later))
    return jnp.concatenate(rows, axis=0)


def inverse_factor(gram, s_ref, t_ref, ring_ref, beside=None):
    size = gram.shape[0]
    s_ref[...] = gram
    lane = iota((PANEL, size), 1)
    for base in range(0, size, PANEL):
        after = base + PANEL
        if beside is not None:
            beside(base // PANEL)
        x = eliminate_panel(s_ref[base:after, :], base, ring_ref)
        t_ref[base:after, :] = jnp.where(lane < after, x, 0.0)
        if after == size:
            break
        parts = split3(x)
        masked = [jnp.where(lane >= after, y.astype(F32), 0.0).astype(BF16) for y in parts]
        pairs = ((0, 0), (0, 1), (1, 0), (1, 1), (0, 2), (2, 0))
        change = tn(
            jnp.concatenate([masked[i] for i, _ in pairs], axis=0),
            jnp.concatenate([parts[k] for _, k in pairs], axis=0),
        )
        inside = (lane[0:1] >= base) & (lane[0:1] < after)
        s_ref[after:, :] = jnp.where(inside, 0.0, s_ref[after:, :]) - change[after:, :]


def low_part(count):
    bits = count.bit_length() - 1
    return 1 << (bits // 2)


def gate_kernel(
    row_count, sec_count, left_hbm, right_hbm, lops_hbm, rops_hbm, charges_hbm, live_hbm, kept_hbm,
    start_hbm, u_out, w_out, lops_ref, rops_ref, charges_ref, live_ref, kept_ref, start_ref,
    lown, lrecv, rown, kl_ref, kr_ref, at_ref, own_ref, b_ref, bw_ref, ga_ref, gah_ref, gal_ref,
    gbh_ref, gbl_ref, s_ref, t_ref, ring_ref, coef_ref, csend, crecv, msend, mrecv, total_ref,
    local, lsend, lget, fsend, fget, csems, cgets, msems, mgets, tsems, tgets,
):
    slots, rows, states = left_hbm.shape
    terms, site = lops_ref.shape[0], lops_ref.shape[1]
    cols = right_hbm.shape[2]
    width = cols // site
    group = 256 // site
    block = group * site
    bond = terms * states
    keep = start_ref.shape[1]
    sector_count = slots * sec_count
    mates = row_count // slots
    here = site // row_count
    piece = rows // PIECES
    half = sec_count // 2

    sec, row = lax.axis_index("sec"), lax.axis_index("row")
    slot, mate = row // mates, row % mates
    partner = jnp.bitwise_xor(sec, half)
    home = sec * slots + slot
    mirror = lax.rem(home + sector_count // 2, sector_count)

    def slot_row(t):
        return t * mates + mate

    def other_slot(d):
        return lax.rem(slot + d, slots)

    def other_mate(d):
        return lax.rem(mate + d, mates)

    greeted = [(sec, slot * mates + other_mate(d)) for d in range(1, mates)]
    near_count = low_part(sec_count)
    far_count = sec_count // near_count
    greeted += [
        (jnp.bitwise_xor(sec, d), slot_row(other_slot(e)))
        for d in range(near_count) for e in range(slots) if d or e
    ]
    greeted += [(jnp.bitwise_xor(sec, h * near_count), row) for h in range(1, far_count)]
    greeted += [(partner, slot_row(other_slot(e))) for e in range(1, slots)]
    barrier = pltpu.get_barrier_semaphore()
    for device in greeted:
        pl.semaphore_signal(barrier, inc=1, device_id=device, device_id_type=MESH)

    near = [
        pltpu.make_async_copy(source, target, local.at[i])
        for i, (source, target) in enumerate((
            (rops_hbm, rops_ref), (lops_hbm, lops_ref), (charges_hbm, charges_ref), (live_hbm, live_ref),
            (kept_hbm, kept_ref), (start_hbm, start_ref), (left_hbm, lown),
        ))
    ]
    near += [
        pltpu.make_async_copy(right_hbm.at[other_slot(e)], rown.at[e], local.at[len(near) + e])
        for e in range(slots)
    ]
    for copy in near:
        copy.start()
    near[0].wait()

    r0, c0 = iota((block, 1), 0), iota((1, block), 1)
    for t in range(terms):
        parts = spread(rops_ref[t], r0 // group, c0 // group, (r0 % group) == (c0 % group))
        for h in range(2):
            kr_ref[h, t * block : (t + 1) * block, :] = parts[h]

    pl.semaphore_wait(barrier, len(greeted))

    def remote(source, target, send, recv, device):
        return pltpu.make_async_remote_copy(
            src_ref=source, dst_ref=target, send_sem=send, recv_sem=recv,
            device_id=device, device_id_type=MESH,
        )

    def rows_at(owner, k):
        return pl.ds(pl.multiple_of(owner * rows + k * piece, piece), piece)

    sent = []
    for k in range(PIECES):
        for t in range(slots):
            copy = remote(
                left_hbm.at[t, pl.ds(k * piece, piece), :], lrecv.at[rows_at(row, k), :],
                lsend.at[t, k], lget.at[slot, k], (partner, slot_row(t)),
            )
            copy.start()
            sent.append(copy)

    for copy in near[1:]:
        copy.wait()
    for t in range(terms):
        parts = spread(lops_ref[t].T, r0 % site, c0 % site, (r0 // site) == (c0 // site))
        for h in range(2):
            kl_ref[h, :, t * block : (t + 1) * block] = parts[h]

    def right_chunk(c, carry):
        base = pl.multiple_of(c * group, group)
        part = rown[0, pl.ds(base, group), :]
        stack = jnp.concatenate([part[:, j * width : (j + 1) * width] for j in range(site)], axis=0)
        out = (nn(kr_ref[0], stack) + nn(kr_ref[1], stack)).astype(BF16)
        for t in range(terms):
            for i in range(site):
                b_ref[pl.ds(t * states + base, group), i * width : (i + 1) * width] = out[
                    t * block + i * group : t * block + (i + 1) * group, :
                ]
        return carry

    lax.fori_loop(0, states // group, right_chunk, 0)
    gbh_ref[...], gbl_ref[...] = split2(nt(b_ref[...], b_ref[...]))

    def gate_left(blocks, limit, store):
        turned = jnp.concatenate([
            jnp.concatenate([
                jnp.where(iota(part.shape, 0) + first < limit, part.astype(F32), 0.0)
                for part, first in parts
            ], axis=0).T.astype(BF16)
            for parts in blocks
        ], axis=0)
        out = nn(turned, kl_ref[0]) + nn(turned, kl_ref[1])
        for n in range(len(blocks)):
            for t in range(terms):
                store(n, t, out[n * states : (n + 1) * states, t * block : (t + 1) * block].astype(BF16))

    def own_slot(t, carry):
        def store(n, term, value):
            own_ref[t, n * block : (n + 1) * block, term * states : (term + 1) * states] = value.T

        gate_left(
            [
                [(lown[t, first : first + block, :], row * rows + first)]
                for first in range(0, rows, block)
            ],
            live_ref[sec * slots + t] * site, store,
        )
        return carry

    lax.fori_loop(0, slots, own_slot, 0)

    limit = live_ref[mirror] * site
    forwarded = []
    ready = block // piece
    span = row_count * piece
    def arrive(k):
        owners = []
        for t in range(slots):
            owner = slot_row(t)
            place = lrecv.at[rows_at(owner, k), :]
            remote(place, place, lsend.at[t, k], lget.at[t, k], (partner, owner)).wait_recv()
            for d in range(1, mates):
                copy = remote(
                    place, place, fsend.at[d - 1, t, k], fget.at[d - 1, t, k],
                    (sec, slot * mates + other_mate(d)),
                )
                copy.start()
                forwarded.append(copy)
            owners.append(owner)
        return owners

    def arrive_from_mates(k):
        owners = []
        for d in range(1, mates):
            for t in range(slots):
                owner = t * mates + other_mate(mates - d)
                place = lrecv.at[rows_at(owner, k), :]
                remote(
                    place, place, fsend.at[d - 1, t, k], fget.at[d - 1, t, k],
                    (sec, slot * mates + other_mate(mates - d)),
                ).wait_recv()
                owners.append(owner)
        return owners

    def blocks_of(owners, k):
        firsts = [owner * rows + k * piece for owner in owners]
        parts = [(lrecv[pl.ds(pl.multiple_of(first, piece), piece), :], first) for first in firsts]
        return [parts[index : index + ready] for index in range(0, len(parts), ready)]

    gram = None
    for k in range(PIECES + 1):
        blocks, places = [], []
        if k < PIECES:
            blocks = blocks_of(arrive(k), k)
            places = [k * span + n * block for n in range(len(blocks))]
        if k:
            late = blocks_of(arrive_from_mates(k - 1), k - 1)
            blocks = blocks + late
            places += [(k - 1) * span + slots * piece + n * block for n in range(len(late))]

        def store(n, t, value):
            at_ref[t * states : (t + 1) * states, places[n] : places[n] + block] = value

        gate_left(blocks, limit, store)
        if k:
            done = at_ref[:, (k - 1) * span : k * span]
            gram = nt(done, done) if gram is None else ga_ref[...] + nt(done, done)
            if k < PIECES:
                ga_ref[...] = gram
    gah_ref[...], gal_ref[...] = split2(gram)
    for copy in sent + forwarded:
        copy.wait_send()

    weight = jnp.exp(jnp.full((1, states), charges_ref[home], jnp.int32).astype(F32) * (-chemical))
    coef = (iota((bond, keep), 0) == start_ref[pl.ds(mirror, 1), :]).astype(F32)
    share = bond * PANEL // keep
    for round_index in range(ITERS + 1):
        image = presplit_nn((gah_ref[...], gal_ref[...]), coef)
        norm = lax.rsqrt(jnp.sum(coef * image, axis=0, keepdims=True))
        coef, image = coef * norm, image * norm

        def following(n):
            span = pl.ds(n * share, share)
            coef_ref[span, :] = presplit_nn((gbh_ref[span, :], gbl_ref[span, :]), image)

        last = round_index == ITERS
        inverse_factor(tn3(coef, image), s_ref, t_ref, ring_ref, None if last else following)
        if not last:
            coef = nt3(coef_ref[...], t_ref[...]) * (weight * weight)
    kept_here = iota((bond, keep), 1) < kept_ref[home]
    part = bond // mates
    bit = part // BITS

    def coef_rows(m, k):
        return pl.ds(pl.multiple_of(m * part + k * bit, bit), bit)

    def coef_at(t, m, k):
        return crecv.at[t, coef_rows(m, k), :]

    def m_rows(m):
        return pl.ds(pl.multiple_of(m * part, part), part)

    coef_ref[...] = coef
    kept_part = iota((part, keep), 1) < kept_ref[home]
    csend[...] = jnp.where(kept_part, nt3(coef_ref[m_rows(mate), :], t_ref[...]), 0.0).astype(BF16)

    flying = []

    def go(*args):
        copy = remote(*args)
        copy.start()
        flying.append(copy)

    for k in range(BITS):
        go(
            csend.at[pl.ds(k * bit, bit), :], coef_at(slot, mate, k), csems.at[0, k], cgets.at[0, k],
            (partner, row),
        )
    out = jnp.where(kept_here, nt3(image, t_ref[...]) * weight, 0.0)
    msend[...] = out.astype(BF16)
    per = out * presplit_nn((gbh_ref[...], gbl_ref[...]), out)
    total_ref[0] = jnp.sum(per, axis=0, keepdims=True)

    def add_totals(start, peers):
        for n, device in enumerate(peers):
            index = start + 1 + n
            go(total_ref.at[start], total_ref.at[index], tsems.at[index], tgets.at[index], device)

    def sum_totals(start, peers):
        summed = total_ref[start]
        for n, device in enumerate(peers):
            index = start + 1 + n
            remote(
                total_ref.at[start], total_ref.at[index], tsems.at[index], tgets.at[index], device
            ).wait_recv()
            summed = summed + total_ref[index]
        return summed

    near_peers = [
        (jnp.bitwise_xor(sec, d), slot_row(other_slot(e)))
        for d in range(near_count) for e in range(slots) if d or e
    ]
    far_peers = [(jnp.bitwise_xor(sec, h * near_count), row) for h in range(1, far_count)]
    add_totals(0, near_peers)
    for e in range(1, slots):
        go(
            msend.at[m_rows(mate), :], mrecv.at[slot, m_rows(mate), :], msems.at[e - 1], mgets.at[e - 1],
            (sec, slot_row(other_slot(e))),
        )

    part_rows = here * group
    part_cols = cols // row_count
    bw_ref[0] = b_ref[:, pl.ds(pl.multiple_of(row * part_cols, part_cols), part_cols)]

    def part_chunk(c, carry):
        e = 1 + c // (states // group)
        base = pl.multiple_of(lax.rem(c, states // group) * group, group)
        piece_rows = rown[e, pl.ds(base, group), :]
        stack = jnp.concatenate([piece_rows[:, j * width : (j + 1) * width] for j in range(site)], axis=0)
        pick = [
            jnp.concatenate([
                kr_ref[h, pl.ds(pl.multiple_of(term * block + row * part_rows, part_rows), part_rows), :]
                for term in range(terms)
            ], axis=0)
            for h in range(2)
        ]
        out = (nn(pick[0], stack) + nn(pick[1], stack)).astype(BF16)
        for term in range(terms):
            for i in range(here):
                bw_ref[e, pl.ds(term * states + base, group), i * width : (i + 1) * width] = out[
                    term * part_rows + i * group : term * part_rows + (i + 1) * group, :
                ]
        return carry

    lax.fori_loop(0, (slots - 1) * (states // group), part_chunk, 0)

    def pass_on(t, m, k, index):
        for d in range(1, mates):
            go(
                coef_at(t, m, k), coef_at(t, m, k), csems.at[index + d - 1, k], cgets.at[index + d - 1, k],
                (sec, slot * mates + other_mate(d)),
            )

    far_start = len(near_peers) + 1
    for k in range(BITS):
        flying[k].wait_recv()
        for e in range(1, slots):
            go(
                coef_at(slot, mate, k), coef_at(slot, mate, k), csems.at[e, k], cgets.at[e, k],
                (sec, slot_row(other_slot(e))),
            )
        pass_on(slot, mate, k, slots)
        if k == 0:
            total_ref[far_start] = sum_totals(0, near_peers)
            add_totals(far_start, far_peers)
    number = slots - 1
    for e in range(1, slots):
        t = other_slot(slots - e)
        place = mrecv.at[t, m_rows(mate), :]
        remote(place, place, msems.at[e - 1], mgets.at[e - 1], (sec, slot_row(t))).wait_recv()
        for d in range(1, mates):
            go(place, place, msems.at[number], mgets.at[number], (sec, slot * mates + other_mate(d)))
            number += 1
    def from_mates(e):
        t = other_slot(slots - e)
        for k in range(BITS):
            for d in range(1, mates):
                index = slots + e * (mates - 1) + d - 1
                m = other_mate(mates - d)
                remote(
                    coef_at(t, m, k), coef_at(t, m, k), csems.at[index, k], cgets.at[index, k],
                    (sec, slot * mates + m),
                ).wait_recv()

    wide = [tn(msend[...], bw_ref[0])]
    from_mates(0)
    u_out[slot] = nn(own_ref[slot], crecv[slot])
    number = slots - 1
    for e in range(1, slots):
        t = other_slot(slots - e)
        for d in range(1, mates):
            m = other_mate(mates - d)
            place = mrecv.at[t, m_rows(m), :]
            remote(place, place, msems.at[number], mgets.at[number], (sec, slot * mates + m)).wait_recv()
            number += 1
        wide.append(tn(mrecv[t], bw_ref[slots - e]))
    for k in range(BITS):
        for e in range(1, slots):
            t = other_slot(slots - e)
            remote(
                coef_at(t, mate, k), coef_at(t, mate, k), csems.at[e, k], cgets.at[e, k], (sec, slot_row(t))
            ).wait_recv()
            pass_on(t, mate, k, slots + e * (mates - 1))
    for e in range(1, slots):
        t = other_slot(slots - e)
        from_mates(e)
        u_out[t] = nn(own_ref[t], crecv[t])
    scale = 1.0 / jnp.sqrt(jnp.sum(sum_totals(far_start, far_peers), keepdims=True))
    for d in range(slots):
        w_out[other_slot(slots - d)] = wide[d] * scale

    for copy in flying:
        copy.wait_send()


def solution(mesh):
    row_count, sec_count = mesh.shape["row"], mesh.shape["sec"]

    def on_device(left_block, right_block, left_ops, right_ops, charges, live_states, kept, start):
        slots, rows, states = left_block.shape
        terms, site = left_ops.shape[0], left_ops.shape[1]
        cols, bond, keep = right_block.shape[2], terms * states, start.shape[1]
        block, mates = 256, row_count // slots
        part_cols = cols // row_count
        coef_copies = slots + slots * (mates - 1)
        m_copies = (slots - 1) * mates
        near_count = low_part(sec_count)
        peers = slots * near_count + sec_count // near_count
        dma = pltpu.SemaphoreType.DMA
        u_shape, w_shape = (slots, rows, keep), (slots, keep, part_cols)
        return pl.pallas_call(
            functools.partial(gate_kernel, row_count, sec_count),
            out_shape=(pltpu.VMEM(u_shape, F32), pltpu.VMEM(w_shape, F32)),
            in_specs=[HBM] * 8,
            out_specs=[VM] * 2,
            scratch_shapes=[
                pltpu.VMEM(left_ops.shape, F32),
                pltpu.VMEM(right_ops.shape, F32),
                pltpu.SMEM(charges.shape, jnp.int32),
                pltpu.SMEM(live_states.shape, jnp.int32),
                pltpu.SMEM(kept.shape, jnp.int32),
                pltpu.VMEM(start.shape, jnp.int32),
                pltpu.VMEM((slots, rows, states), BF16),
                pltpu.VMEM((rows * row_count, states), BF16),
                pltpu.VMEM((slots, states, cols), BF16),
                pltpu.VMEM((2, block, terms * block), BF16),
                pltpu.VMEM((2, terms * block, block), BF16),
                pltpu.VMEM((bond, rows * row_count), BF16),
                pltpu.VMEM((slots, rows, bond), BF16),
                pltpu.VMEM((bond, cols), BF16),
                pltpu.VMEM((slots, bond, part_cols), BF16),
                pltpu.VMEM((bond, bond), F32),
                pltpu.VMEM((bond, bond), BF16),
                pltpu.VMEM((bond, bond), BF16),
                pltpu.VMEM((bond, bond), BF16),
                pltpu.VMEM((bond, bond), BF16),
                pltpu.VMEM((keep, keep), F32),
                pltpu.VMEM((keep, keep), F32),
                pltpu.VMEM((RING, 2, PANEL + TILE, keep), F32),
                pltpu.VMEM((bond, keep), F32),
                pltpu.VMEM((bond // mates, keep), BF16),
                pltpu.VMEM((slots, bond, keep), BF16),
                pltpu.VMEM((bond, keep), BF16),
                pltpu.VMEM((slots, bond, keep), BF16),
                pltpu.VMEM((peers, 1, keep), F32),
                dma((7 + slots,)),
                dma((slots, PIECES)), dma((slots, PIECES)),
                dma((mates - 1, slots, PIECES)), dma((mates - 1, slots, PIECES)),
                dma((coef_copies, BITS)), dma((coef_copies, BITS)),
                dma((m_copies,)), dma((m_copies,)),
                dma((peers,)), dma((peers,)),
            ],
            compiler_params=pltpu.CompilerParams(
                collective_id=0, has_side_effects=True, vmem_limit_bytes=62 * 2**20
            ),
        )(left_block, right_block, left_ops, right_ops, charges, live_states, kept, start)
    return jax.shard_map(
        on_device,
        mesh=mesh,
        in_specs=(P("sec", "row", None), P("sec", None, None), P(), P(), P(), P(), P(), P()),
        out_specs=(P("sec", "row", None), P("sec", None, "row")),
        check_vma=False,
    )
```
